32 devices in a mesh: groups: 2 (over y), seq: 4 (over z), adapter: 2 (over x), head: 2 (over core).
Axes of the slice: x: 2, y: 2, z: 4, core: 2. Of those that a mesh axis runs over, the one named last changes fastest.
Arguments:
- hidden: bfloat16 [64, 3, 8192], P(('groups', 'seq', 'adapter'), None, 'head'), parts along dimension 0, may hold values from -6 to 6
- base_query_rows: bfloat16 [64, 3, 8192], P(('groups', 'seq', 'adapter'), None, 'head'), parts along dimension 0, may hold values from -16 to 16
- fresh_key_value: bfloat16 [2, 64, 3, 1024], P(None, ('groups', 'seq', 'adapter'), None, 'head'), parts along dimension 1, may hold values from -12 to 12
- suffix_key_value: bfloat16 [2, 64, 32, 1024], P(None, ('groups', 'seq', 'adapter'), None, 'head'), parts along dimension 1, may hold values from -12 to 12
- suffix_length: int32 [64], P(('groups', 'seq', 'adapter')), parts along dimension 0, may hold values from 0 to 32, as said below
- row_adapter_index: int32 [64, 1], P(('groups', 'seq', 'adapter')), parts along dimension 0, may hold values from 0 to 1
- prompt_key_value: bfloat16 [2, 8192, 1024], P(None, ('groups', 'seq'), 'head'), parts along dimension 1, may hold values from -16 to 16
- query_down_factors: bfloat16 [4, 64, 8192], P(('groups', 'adapter'), None, 'head'), parts along dimension 0, may hold values from -0.0625 to 0.0625
- query_up_factors: bfloat16 [4, 64, 8192], P(('groups', 'adapter'), None, 'head'), parts along dimension 0, may hold values from -0.75 to 0.75
- output_down_factors: bfloat16 [4, 64, 8192], P(('groups', 'adapter'), None, 'head'), parts along dimension 0, may hold values from -0.0625 to 0.0625
- output_up_factors: bfloat16 [4, 64, 8192], P(('groups', 'adapter'), None, 'head'), parts along dimension 0, may hold values from -0.75 to 0.75
Outputs:
- attended: bfloat16 [64, 3, 8192], P(('groups', 'seq', 'adapter'), None, 'head'), parts along dimension 0
- adapted: bfloat16 [64, 3, 8192], P(('groups', 'seq', 'adapter'), None, 'head'), parts along dimension 0
The draws below stay inside these ranges and needn't reach their ends.
There are 2 independent parts, one for each index of `groups`. The reference program is written for one: setup_inputs(seed, part) draws one part's arguments, and reference() takes and returns one part's arrays. A program takes and returns all parts, laid end to end along the dimension named above; each array names one. Nothing has to cross between parts.
Inputs may be any that keep to these rules, and one draw needn't show every extreme that they name: `suffix_length`: each row's suffix holds at most 32 tokens, and some row holds exactly 32.
All inputs are finite; a program needn't handle non-finite values.
Results may differ from the reference program's by a relative error of at most 0.011.
Values may be sent and summed in bfloat16 or wider, within the bound.
A program may use at most 64 MiB of HBM per device.

```python
import math
import jax
import jax.numpy as jnp
from jax import lax

MODEL_WIDTH = 8192
QUERY_HEADS = 64
KVH = 8
HEAD_SIZE = 128
FACTOR_RANK = 64
STEPS = 3
P_DEV = 1024
SUF = 32
ADAPTER_TOTAL = 2
ROWS = 32
PROMPT = 4096
N_SEQ = 4


def draw_base_query_rows(key, part):
    values = jax.random.truncated_normal(key, -6.0, 6.0, (ROWS, STEPS, QUERY_HEADS, HEAD_SIZE), jnp.float32)
    return values.reshape(ROWS, STEPS, QUERY_HEADS * HEAD_SIZE).astype(jnp.bfloat16)


def draw_prompt_key_value(key, part):
    first_key, second_key = jax.random.split(jax.random.fold_in(key, 17))
    keys_part = 2.0 * jax.random.truncated_normal(first_key, -8.0, 8.0, (PROMPT, KVH, HEAD_SIZE), jnp.float32)
    values_part = jax.random.truncated_normal(second_key, -6.0, 6.0, (PROMPT, KVH * HEAD_SIZE), jnp.float32)
    return jnp.stack([keys_part.reshape(PROMPT, KVH * HEAD_SIZE), values_part]).astype(jnp.bfloat16)


def draw_suffix_length(key, part):
    lengths = jax.random.randint(jax.random.fold_in(key, 29), (ROWS,), 0, SUF + 1)
    return lengths.at[0].set(SUF)


def block_scale(rng, extent, cuts, smallest, high):
    factor_of = 1.0
    for axis_at, blocks in cuts:
        heights = jax.random.uniform(jax.random.fold_in(jax.random.fold_in(rng, 6), axis_at), (blocks,), jnp.float32, smallest / len(cuts), high / len(cuts))
        factor_of = factor_of * jnp.repeat(jnp.exp(heights), extent[axis_at] // blocks).reshape((-1,) + (1,) * (len(extent) - 1 - axis_at))
    return factor_of


def choose_distinct(stream_key, rows, amount, top, lift):
    sequence = jax.random.permutation(jax.random.fold_in(stream_key, 1), amount)
    favour = sequence
    for power in range(3):
        favour = favour * favour // amount
    favour = favour * lift // amount
    tickets = jax.random.randint(jax.random.fold_in(stream_key, 2), (rows, amount), 0, 4096) + favour
    fixed_rows = jax.random.permutation(jax.random.fold_in(stream_key, 3), rows)[jnp.arange(amount) % rows]
    tickets = jnp.where(jnp.arange(rows)[:, None] == fixed_rows[None, :], 1 << 14, tickets)
    priority = tickets * amount + jnp.arange(amount)
    return lax.top_k(priority.astype(jnp.int32), top)[1].astype(jnp.int32)


def gaussian(key, shape, width, most, cuts=(), kind=jnp.bfloat16):
    values = jax.random.normal(key, shape, jnp.float32) * width
    if len(cuts) > 0:
        values = block_scale(key, shape, cuts, -0.22, 0.18) * values
    return jnp.clip(values, min=-most, max=most).astype(kind)


def setup_inputs(seed: int = 0, part: int = 0) -> dict:
    streams_of = jax.random.split(jax.random.key(seed), 12)
    part_splits = jax.random.split(jax.random.fold_in(streams_of[11], part), 12)
    hidden = gaussian(part_splits[0], (ROWS, STEPS, MODEL_WIDTH), 1.0, 6.0, ((0, 8), (2, 2)))
    base_query_rows = draw_base_query_rows(jax.random.fold_in(jax.random.fold_in(streams_of[11], part), 71), part)
    fresh_key_value = gaussian(part_splits[2], (2, ROWS, STEPS, KVH * HEAD_SIZE), 2.0, 12.0, ((1, 8), (3, 2)))
    suffix_key_value = gaussian(part_splits[3], (2, ROWS, SUF, KVH * HEAD_SIZE), 2.0, 12.0, ((1, 8), (3, 2)))
    suffix_length = draw_suffix_length(jax.random.fold_in(jax.random.fold_in(streams_of[11], part), 71), part)
    row_adapter_index = choose_distinct(part_splits[5], ROWS, ADAPTER_TOTAL, 1, 4096)
    prompt_key_value = draw_prompt_key_value(jax.random.fold_in(jax.random.fold_in(streams_of[11], part), 71), part)
    query_down_factors = gaussian(part_splits[7], (ADAPTER_TOTAL, FACTOR_RANK, MODEL_WIDTH), MODEL_WIDTH ** -0.5, 0.0625, ((0, 2), (2, 2)))
    query_up_factors = gaussian(part_splits[8], (ADAPTER_TOTAL, FACTOR_RANK, QUERY_HEADS * HEAD_SIZE), FACTOR_RANK ** -0.5, 0.75, ((0, 2), (2, 2)))
    output_down_factors = gaussian(part_splits[9], (ADAPTER_TOTAL, FACTOR_RANK, QUERY_HEADS * HEAD_SIZE), (QUERY_HEADS * HEAD_SIZE) ** -0.5, 0.0625, ((0, 2), (2, 2)))
    output_up_factors = gaussian(part_splits[10], (ADAPTER_TOTAL, FACTOR_RANK, MODEL_WIDTH), FACTOR_RANK ** -0.5, 0.75, ((0, 2), (2, 2)))
    return dict(hidden=hidden, base_query_rows=base_query_rows, fresh_key_value=fresh_key_value, suffix_key_value=suffix_key_value, suffix_length=suffix_length, row_adapter_index=row_adapter_index, prompt_key_value=prompt_key_value, query_down_factors=query_down_factors, query_up_factors=query_up_factors, output_down_factors=output_down_factors, output_up_factors=output_up_factors)


rope_base = 1000000.0

def rotate(values_in, position):
    half_dim = values_in.shape[-1] // 2
    frequency = rope_base ** (-2.0 * jnp.arange(half_dim, dtype=jnp.float32) / values_in.shape[-1])
    angles = position[..., None] * frequency
    cos_part = jnp.cos(angles)
    sin_part = jnp.sin(angles)
    first_half = values_in[..., :half_dim]
    second_half = values_in[..., half_dim:]
    return jnp.concatenate([first_half * cos_part - second_half * sin_part, second_half * cos_part + first_half * sin_part], -1)

def rounded_values(values_in):
    narrow = lax.optimization_barrier(values_in.astype(jnp.bfloat16))
    return narrow.astype(jnp.float32)

def down_projected(inputs, factors, adapter_of_row):

    def add_adapter(carried, pair):
        factor, index = pair
        term = jnp.einsum('rsc,kc->rsk', inputs, factor.astype(jnp.float32))
        picked = (adapter_of_row == index)[:, None, None]
        return (carried + jnp.where(picked, term, 0.0), None)
    start = jnp.zeros(inputs.shape[:2] + (factors.shape[1],), jnp.float32)
    result, unused = lax.scan(add_adapter, start, (factors, jnp.arange(factors.shape[0], dtype=jnp.int32)))
    return result

def up_projected(inputs, factors, adapter_of_row):

    def add_adapter(carried, pair):
        factor, index = pair
        term = jnp.einsum('rsk,kc->rsc', inputs, factor.astype(jnp.float32))
        picked = (adapter_of_row == index)[:, None, None]
        return (carried + jnp.where(picked, term, 0.0), None)
    start = jnp.zeros(inputs.shape[:2] + (factors.shape[2],), jnp.float32)
    result, unused = lax.scan(add_adapter, start, (factors, jnp.arange(factors.shape[0], dtype=jnp.int32)))
    return result

def combine_parts(former, latter):
    weighted_a, peaks_a, totals_a = former
    weighted_b, peaks_b, totals_b = latter
    peaks = jnp.maximum(peaks_a, peaks_b)
    factor_a = jnp.exp(peaks_a - peaks)
    factor_b = jnp.exp(peaks_b - peaks)
    return (weighted_a * factor_a[..., None] + weighted_b * factor_b[..., None], peaks, totals_a * factor_a + totals_b * factor_b)

def reference(hidden, base_query_rows, fresh_key_value, suffix_key_value, suffix_length, row_adapter_index, prompt_key_value, query_down_factors, query_up_factors, output_down_factors, output_up_factors):
    adapter_of_row = row_adapter_index[:, 0]
    group_size = QUERY_HEADS // KVH
    score_scale = 1.0 / math.sqrt(HEAD_SIZE)
    query_low_rank = rounded_values(down_projected(hidden.astype(jnp.float32), query_down_factors, adapter_of_row))
    query_adjustment = up_projected(query_low_rank, query_up_factors, adapter_of_row)
    position = (PROMPT + suffix_length[:, None] + jnp.arange(STEPS, dtype=jnp.int32)[None, :]).astype(jnp.float32)
    merged = (base_query_rows.astype(jnp.float32) + query_adjustment).reshape(ROWS, STEPS, QUERY_HEADS, HEAD_SIZE)
    grouped = rounded_values(rotate(merged, position[:, :, None])).reshape(ROWS, STEPS, KVH, group_size, HEAD_SIZE)
    local_keys = jnp.concatenate([suffix_key_value[0], fresh_key_value[0]], 1).astype(jnp.float32).reshape(ROWS, SUF + STEPS, KVH, HEAD_SIZE)
    local_values = jnp.concatenate([suffix_key_value[1], fresh_key_value[1]], 1).astype(jnp.float32).reshape(ROWS, SUF + STEPS, KVH, HEAD_SIZE)
    scores = jnp.einsum('rtkgd,rpkd->rtkgp', grouped, local_keys) * score_scale
    key_slot = jnp.arange(SUF + STEPS, dtype=jnp.int32)[None, None, :]
    admitted = jnp.where(key_slot < SUF, key_slot < suffix_length[:, None, None], key_slot - SUF <= jnp.arange(STEPS, dtype=jnp.int32)[None, :, None])
    admitted = admitted[:, :, None, None, :]
    masked = jnp.where(admitted, scores, -1e+30)
    local_peaks = lax.optimization_barrier(jnp.max(masked, -1))
    local_weight = rounded_values(jnp.where(admitted, jnp.exp(masked - local_peaks[..., None]), 0.0))
    local_weighted = jnp.einsum('rtkgp,rpkd->rtkgd', local_weight, local_values)
    local_totals = lax.optimization_barrier(jnp.sum(local_weight, -1))
    token_count = ROWS * STEPS
    local_part = (local_weighted.reshape(token_count, KVH, group_size, HEAD_SIZE), local_peaks.reshape(token_count, KVH, group_size), local_totals.reshape(token_count, KVH, group_size))
    flat_query = grouped.reshape(token_count, KVH, group_size, HEAD_SIZE)
    prompt_keys = prompt_key_value[0].reshape(N_SEQ, P_DEV, KVH, HEAD_SIZE)
    prompt_values = prompt_key_value[1].reshape(N_SEQ, P_DEV, KVH, HEAD_SIZE)

    def add_block(carried, pair):
        block_keys, block_values = pair
        block_scores = jnp.einsum('nkgd,pkd->nkgp', flat_query, block_keys.astype(jnp.float32)) * score_scale
        peaks = lax.optimization_barrier(jnp.max(block_scores, -1))
        weight = rounded_values(jnp.exp(block_scores - peaks[..., None]))
        weighted = jnp.einsum('nkgp,pkd->nkgd', weight, block_values.astype(jnp.float32))
        totals = lax.optimization_barrier(jnp.sum(weight, -1))
        return (combine_parts(carried, (weighted, peaks, totals)), None)
    combined, unused = lax.scan(add_block, local_part, (prompt_keys, prompt_values))
    attended = (combined[0] / combined[2][..., None]).reshape(ROWS, STEPS, QUERY_HEADS * HEAD_SIZE).astype(jnp.bfloat16)
    attended_full_width = lax.optimization_barrier(attended).astype(jnp.float32)
    output_rank_rows = rounded_values(down_projected(attended_full_width, output_down_factors, adapter_of_row))
    adapted = up_projected(output_rank_rows, output_up_factors, adapter_of_row).astype(jnp.bfloat16)
    return (attended, adapted)
```

```python
import functools
import math

import jax
import jax.numpy as jnp
import numpy as np
from jax import lax
from jax.experimental import pallas as pl
from jax.experimental.pallas import tpu as pltpu
from jax.sharding import PartitionSpec as P

HEAD_SIZE = 128
ROPE_BASE = 1000000.0
LANES = 128
MESH = pl.DeviceIdType.MESH
NT = (((1,), (1,)), ((), ()))


def dot_nt(a, b):
    return lax.dot_general(a, b, NT, preferred_element_type=jnp.float32)


def dot_nn(a, b):
    return jnp.dot(a, b, preferred_element_type=jnp.float32)


def xor(a, b, size):
    out, bit = 0, 1
    while bit < size:
        out = out + lax.rem(lax.div(a, bit) + b // bit, 2) * bit
        bit *= 2
    return out


def body(
    cfg,
    len_ref,
    id_ref,
    cos_ref,
    sin_ref,
    hidden_hbm,
    base_hbm,
    fresh_hbm,
    suffix_hbm,
    prompt_hbm,
    qd_hbm,
    qu_hbm,
    od_hbm,
    ou_hbm,
    att_ref,
    ada_ref,
    hidden_v,
    fresh_v,
    suffix_v,
    prompt_v,
    qd_v,
    qu_v,
    od_v,
    ou_v,
    local_sem,
    hid_in,
    base_in,
    info,
    rank_in,
    rank_out,
    tok_f32,
    fresh_f32,
    fresh_pad,
    base_f,
    cos_v,
    sin_v,
    ids_v,
    wide_f,
    wide_b,
    vt,
    vlt,
    bias_v,
    part_out,
    part_in,
    stat_out,
    stat_in,
    ork_out,
    ork_in,
    att_out,
    att_in,
    hid_s,
    hid_r,
    info_s,
    info_r,
    base_s,
    base_r,
    qu_s,
    qu_r,
    od_s,
    od_r,
    ou_s,
    ou_r,
    rank_s,
    rank_r,
    part_s,
    part_r,
    stat_s,
    stat_r,
    ork_s,
    ork_r,
    att_s,
    att_r,
):
    NS, NA, NH, R, T, KV, G, S, K = cfg
    D = HEAD_SIZE
    N = R * T
    C = G * D
    GT = KV * N
    QC = G * GT
    NK = NA * K
    bf16, f32 = jnp.bfloat16, jnp.float32
    seq, ada, head = lax.axis_index("seq"), lax.axis_index("adapter"), lax.axis_index("head")
    own_k, own_j = lax.rem(seq, KV), lax.div(seq, KV)
    scale = math.log2(math.e) / math.sqrt(D)
    shift = (S + T - 1).bit_length()

    def turn(me, d, size):
        return lax.rem(me + d, size)

    def place(ds, da, dh):
        return {
            "seq": turn(seq, ds, NS),
            "adapter": turn(ada, da, NA),
            "head": turn(head, dh, NH),
        }

    others = [
        (ds, da, dh)
        for ds in range(NS)
        for da in range(NA)
        for dh in range(NH)
        if (ds, da, dh) != (0, 0, 0)
    ]
    barrier = pltpu.get_barrier_semaphore()
    for other in others:
        pl.semaphore_signal(barrier, inc=1, device_id=place(*other), device_id_type=MESH)

    def head_at(where, i):
        return xor(lax.rem(where, KV), KV - 1 - i, KV)

    def columns(k, width):
        return pl.ds(pl.multiple_of(k * width, width), width)

    own_cols = columns(own_k, C)
    loads = []
    for i, (src, dst) in enumerate(
        (
            (hidden_hbm, hidden_v),
            (qd_hbm, qd_v),
            (prompt_hbm, prompt_v),
            (suffix_hbm, suffix_v),
            (fresh_hbm, fresh_v),
            (base_hbm, base_in.at[seq]),
            (qu_hbm.at[0], qu_v.at[ada]),
            (od_hbm.at[0, :, own_cols], od_v.at[ada]),
            (ou_hbm.at[0], ou_v.at[ada]),
        )
    ):
        load = pltpu.make_async_copy(src, dst, local_sem.at[i])
        load.start()
        loads.append(load)
    l_hid, l_qd, l_prompt, l_suffix, l_fresh, l_base, l_qu, l_od, l_ou = loads

    row = lax.broadcasted_iota(jnp.int32, (N, LANES), 0)
    code = jnp.zeros((N, LANES), jnp.int32)
    for r in range(R):
        code = jnp.where(lax.rem(row, R) == r, id_ref[0, r] * 2**shift + len_ref[r], code)
    info[seq] = code + lax.div(row, R)

    pl.semaphore_wait(barrier, len(others))

    sends = []

    def send(src, dst, s_sem, r_sem, device):
        copy = pltpu.make_async_remote_copy(
            src_ref=src,
            dst_ref=dst,
            send_sem=s_sem,
            recv_sem=r_sem,
            device_id=device,
            device_id_type=MESH,
        )
        copy.start()
        sends.append(copy)
        return copy

    hid = {}
    for d in range(1, NA):
        hid[d] = send(
            hidden_hbm, hid_in.at[d - 1], hid_s.at[d - 1], hid_r.at[d - 1], place(0, d, 0)
        )
    far = sorted(range(1, NS), key=lambda d: (-min(d, NS - d), d))
    infos, bases, qus, ods, ous = {}, {}, {}, {}, {}
    for ds in far:
        infos[ds] = send(
            info.at[seq], info.at[seq], info_s.at[ds - 1], info_r.at[ds - 1], place(ds, 0, 0)
        )

    def send_base(i):
        for ds in far:
            cols = columns(head_at(turn(seq, ds, NS), i), C)
            bases[(ds, i)] = send(
                base_hbm.at[:, :, cols], base_in.at[seq, :, :, cols],
                base_s.at[ds - 1, i], base_r.at[ds - 1, i], place(ds, 0, 0),
            )

    def send_qu(i):
        cols = columns(head_at(seq, i), C)
        for d in range(1, NA):
            qus[(d, i)] = send(
                qu_hbm.at[0, :, cols], qu_v.at[ada, :, cols],
                qu_s.at[d - 1, i], qu_r.at[d - 1, i], place(0, d, 0),
            )

    half = max(KV // 2, 1)
    for i in range(half):
        send_base(i)
    send_qu(0)

    def rank_of(ref):
        for t in range(T):
            tok_f32[t * R : (t + 1) * R, :] = ref[t].astype(f32)
        part = dot_nt(tok_f32[...].astype(bf16), qd_v[0])
        return jnp.concatenate([part] * (LANES // K), 1)

    ranks = {}

    def send_rank(src, ds, da, dh):
        ranks[(ds, da, dh)] = send(
            src, rank_in.at[seq, ada, head],
            rank_s.at[ds, da, dh], rank_r.at[ds, da, dh], place(ds, da, dh),
        )

    l_hid.wait()
    l_qd.wait()
    rank_in[seq, ada, head] = rank_of(hidden_v)
    for ds in far + [0]:
        for dh in range(NH):
            if (ds, dh) != (0, 0):
                send_rank(rank_in.at[seq, ada, head], ds, 0, dh)

    l_prompt.wait()
    l_suffix.wait()
    l_fresh.wait()
    n_suf = R * S
    n_new = fresh_f32.shape[0]
    n_loc = n_suf + n_new
    for i in range(2):
        fresh_f32[...] = jnp.zeros_like(fresh_f32)
        for t in range(T):
            fresh_f32[t * R : (t + 1) * R, :] = fresh_v[i, t].astype(f32)
        fresh_pad[i] = fresh_f32[...].astype(bf16)

    def prepare(i):
        cols = columns(head_at(seq, i), D)
        vt[i, 0:D, :] = prompt_v[1, :, cols].astype(f32).T.astype(bf16)
        pad = lax.broadcasted_iota(jnp.int32, (vt.shape[1] - D, vt.shape[2]), 0)
        vt[i, D:, :] = jnp.where(pad == 0, 1.0, 0.0).astype(bf16)
        local = jnp.concatenate(
            [
                suffix_v[1, :, :, cols].reshape(n_suf, D),
                fresh_pad[1, :, cols],
                jnp.zeros((vlt.shape[2] - n_loc, D), bf16),
            ],
            0,
        )
        vlt[i, 0:D, :] = local.astype(f32).T.astype(bf16)
        pad = lax.broadcasted_iota(jnp.int32, (vlt.shape[1] - D, vlt.shape[2]), 0)
        vlt[i, D:, :] = jnp.where(pad == 0, 1.0, 0.0).astype(bf16)

    for i in range(half):
        prepare(i)

    for d in range(1, NA):
        hid[d].wait_recv()
        rank_out[d - 1] = rank_of(hid_in.at[d - 1])
        for ds in far + [0]:
            for dh in range(NH):
                send_rank(rank_out.at[d - 1], ds, d, dh)
    for i in range(half, KV):
        send_base(i)
    for i in range(1, KV):
        send_qu(i)
    for d in range(1, NA):
        ods[d] = send(
            od_hbm.at[0, :, own_cols], od_v.at[ada], od_s.at[d - 1], od_r.at[d - 1],
            place(0, d, 0),
        )
    for i in range(KV):
        for d in range(1, NA):
            cols = slice(i * C, (i + 1) * C)
            ous[(d, i)] = send(
                ou_hbm.at[0, :, cols], ou_v.at[ada, :, cols],
                ou_s.at[d - 1, i], ou_r.at[d - 1, i], place(0, d, 0),
            )

    key = lax.broadcasted_iota(jnp.int32, (n_loc, QC), 0)
    query = lax.rem(lax.broadcasted_iota(jnp.int32, (n_loc, QC), 1), GT)
    q_home, q_token = lax.div(query, N), lax.rem(query, N)
    q_step, q_row = lax.div(q_token, R), lax.rem(q_token, R)
    limit = jnp.zeros((n_loc, QC), jnp.int32)
    for r in range(R):
        limit = jnp.where(q_row == r, len_ref[r], limit)
    new = key - n_suf
    in_suffix = (lax.div(key, S) == q_row) & (lax.rem(key, S) < limit) & (new < 0)
    in_fresh = (lax.rem(new, R) == q_row) & (lax.div(new, R) <= q_step) & (new >= 0)
    bias_v[...] = jnp.where((q_home == own_k) & (in_suffix | in_fresh), 0.0, -1e30)

    for i in range(half, KV):
        prepare(i)

    def convert(i):
        cols = columns(head_at(seq, i), C)
        for ds in far:
            bases[(ds, i)].wait_recv()
        for s in range(NS):
            for t in range(T):
                at = s * N + t * R
                base_f[i, at : at + R, :] = base_in[s, t, :, cols].astype(f32)

    l_base.wait()
    l_qu.wait()
    for ds in far:
        infos[ds].wait_recv()
    for s in range(NS):
        ids_v[s * N : (s + 1) * N, :] = info[s]
    codes = ids_v[...]
    position = jnp.bitwise_and(codes, 2**shift - 1)
    cos, sin = jnp.zeros(codes.shape, f32), jnp.zeros(codes.shape, f32)
    for p in range(S + T):
        cos = jnp.where(position == p, cos_ref[p : p + 1, :], cos)
        sin = jnp.where(position == p, sin_ref[p : p + 1, :], sin)
    cos_v[...] = cos
    sin_v[...] = sin
    ids_v[...] = jnp.right_shift(codes, shift)
    convert(0)

    def spread(x):
        return jnp.concatenate([x] * (NK // LANES), 1)

    def adapter_lanes(shape):
        return lax.div(lax.broadcasted_iota(jnp.int32, shape, 1), K)

    for copy in ranks.values():
        copy.wait_recv()
    for s in range(NS):
        ids = ids_v[s * N : (s + 1) * N, :]
        chosen = jnp.zeros((N, LANES), f32)
        for e in range(NA):
            whole = functools.reduce(jnp.add, [rank_in[s, e, h] for h in range(NH)])
            chosen = jnp.where(ids == e, whole, chosen)
        wide_f[s * N : (s + 1) * N, :] = spread(chosen)
    wide = wide_f[...]
    wide_b[...] = jnp.where(adapter_lanes(wide.shape) == spread(ids_v[...]), wide, 0.0).astype(bf16)

    def attend(u):
        i = KV - 1 - u % KV
        target = xor(seq, u, NS)
        k, j = lax.rem(target, KV), lax.div(target, KV)
        rows = pl.ds(pl.multiple_of(j * GT, GT), GT)
        cols = columns(k, D)
        delta = dot_nn(wide_b[rows, :], qu_v[:, :, columns(k, C)].reshape(NK, C))
        merged = base_f[i, rows, :] + delta
        cos, sin = cos_v[rows, :], sin_v[rows, :]
        turned = []
        for g in range(G):
            x = merged[:, g * D : (g + 1) * D]
            turned.append((x * cos + pltpu.roll(x, D // 2, 1) * sin).astype(bf16))
        query = jnp.concatenate(turned, 0)
        local_keys = jnp.concatenate(
            [suffix_v[0, :, :, cols].reshape(n_suf, D), fresh_pad[0, :, cols]], 0
        )
        far_scores = dot_nt(prompt_v[0, :, cols], query)
        shut = jnp.where(j == own_j, 0.0, -1e30)
        near_scores = dot_nt(local_keys, query) + (bias_v[...] + shut)
        peak = jnp.maximum(
            jnp.max(far_scores, 0, keepdims=True), jnp.max(near_scores, 0, keepdims=True)
        )
        far_weight = jnp.exp2((far_scores - peak) * scale).astype(bf16)
        near_weight = jnp.exp2((near_scores - peak) * scale).astype(bf16)
        near_weight = jnp.concatenate(
            [near_weight, jnp.zeros((vlt.shape[2] - n_loc, QC), bf16)], 0
        )
        both = dot_nn(vt[i], far_weight) + dot_nn(vlt[i], near_weight)
        return both[0:D], peak, both[D : D + 1]

    parts, stats = {}, {}
    for u in range(NS - 1, -1, -1):
        i = NS - 1 - u
        if i < KV:
            if i > 0:
                convert(i)
            for d in range(1, NA):
                qus[(d, i)].wait_recv()
        o, m, t = attend(u)
        if u > 0:
            part_out[u - 1] = o.astype(bf16)
            stat_out[u - 1, 0:1, :] = m
            stat_out[u - 1, 1:2, :] = t
            home = {"seq": xor(seq, u, NS)}
            parts[u] = send(
                part_out.at[u - 1], part_in.at[u - 1], part_s.at[u - 1], part_r.at[u - 1], home
            )
            stats[u] = send(
                stat_out.at[u - 1], stat_in.at[u - 1], stat_s.at[u - 1], stat_r.at[u - 1], home
            )
    pieces = [(o, m, t)]
    for u in range(1, NS):
        parts[u].wait_recv()
        stats[u].wait_recv()
        pieces.append(
            (part_in[u - 1].astype(f32), stat_in[u - 1, 0:1, :], stat_in[u - 1, 1:2, :])
        )
    top = functools.reduce(jnp.maximum, [p[1] for p in pieces])
    factors = [jnp.exp2((p[1] - top) * scale) for p in pieces]
    num = functools.reduce(jnp.add, [p[0] * f for p, f in zip(pieces, factors)])
    den = functools.reduce(jnp.add, [p[2] * f for p, f in zip(pieces, factors)])
    turned = (num / den).T
    result = jnp.concatenate([turned[g * GT : (g + 1) * GT] for g in range(G)], 1)

    l_od.wait()
    for d in range(1, NA):
        ods[d].wait_recv()
    down = dot_nt(result.astype(bf16), od_v[...].reshape(NK, C))
    group_rows = pl.ds(pl.multiple_of(own_j * GT, GT), GT)
    down = jnp.where(adapter_lanes(down.shape) == spread(ids_v[group_rows, :]), down, 0.0)
    for jj in range(KV):
        ork_out[jj] = down[jj * N : (jj + 1) * N]
    orks, atts = {}, {}

    def home_of(e):
        jj = xor(own_k, e, KV)
        return jj, own_j * KV + jj

    for e in range(KV - 1, -1, -1):
        jj, where = home_of(e)
        for dh in range(NH):
            if (e, dh) != (0, 0):
                orks[(e, dh)] = send(
                    ork_out.at[jj], ork_in.at[own_k, head],
                    ork_s.at[e, dh], ork_r.at[e, dh],
                    {"seq": where, "head": turn(head, dh, NH)},
                )
    for jj in range(KV):
        for t in range(T):
            at = jj * N + t * R
            att_out[jj, t] = result[at : at + R].astype(bf16)
    for e in range(KV - 1, 0, -1):
        jj, where = home_of(e)
        atts[e] = send(
            att_out.at[jj], att_in.at[own_k], att_s.at[e - 1], att_r.at[e - 1], {"seq": where}
        )
    att_in[own_k] = att_out[own_k]

    ork_in[own_k, head] = ork_out[own_k]
    for copy in orks.values():
        copy.wait_recv()
    total = functools.reduce(
        jnp.add, [ork_in[k, h] for k in range(KV) for h in range(NH)]
    ).astype(bf16)
    l_ou.wait()
    for i in range(KV):
        cols = slice(i * C, (i + 1) * C)
        for d in range(1, NA):
            ous[(d, i)].wait_recv()
        up = dot_nn(total, ou_v[:, :, cols].reshape(NK, C))
        for t in range(T):
            ada_ref[t, :, cols] = up[t * R : (t + 1) * R].astype(bf16)
    for copy in atts.values():
        copy.wait_recv()
    for k in range(KV):
        att_ref[:, :, k * C : (k + 1) * C] = att_in[k]

    for copy in sends:
        copy.wait_send()


def finish(first, second, att_ref, ada_ref):
    att_ref[...] = first[...]
    ada_ref[...] = second[...]


def on_device(
    hidden,
    base_query_rows,
    fresh_key_value,
    suffix_key_value,
    suffix_length,
    row_adapter_index,
    prompt_key_value,
    query_down_factors,
    query_up_factors,
    output_down_factors,
    output_up_factors,
):
    NS, NA, NH = lax.axis_size("seq"), lax.axis_size("adapter"), lax.axis_size("head")
    hidden, base_query_rows = (x.transpose(1, 0, 2) for x in (hidden, base_query_rows))
    fresh_key_value = fresh_key_value.transpose(0, 2, 1, 3)
    T, R, width = hidden.shape
    D = HEAD_SIZE
    KV = prompt_key_value.shape[2] // D
    G = width // D // KV
    S = suffix_key_value.shape[2]
    keys = prompt_key_value.shape[1]
    N, C = R * T, G * D
    K = query_down_factors.shape[1]
    GT = KV * N
    QC, NK = G * GT, NA * K
    assert query_down_factors.shape[0] == 1
    assert NS % KV == 0 and NS & (NS - 1) == 0 and KV & (KV - 1) == 0
    assert GT % 16 == 0 and LANES % K == 0 and NK % LANES == 0
    prompt_total = keys * NS
    positions = prompt_total + np.arange(S + T, dtype=np.float64)
    frequency = ROPE_BASE ** (-2.0 * np.arange(D // 2, dtype=np.float64) / D)
    angle = positions[:, None] * frequency[None, :]
    cos = np.concatenate([np.cos(angle), np.cos(angle)], 1).astype(np.float32)
    sin = np.concatenate([-np.sin(angle), np.sin(angle)], 1).astype(np.float32)
    bf16, f32 = jnp.bfloat16, jnp.float32
    dma = pltpu.SemaphoreType.DMA
    one = max(NA - 1, 1)
    far = max(NS - 1, 1)
    n_new = -(-N // 16) * 16
    n_loc = R * S + n_new
    n_loc_pad = -(-n_loc // LANES) * LANES

    def like(x):
        return pltpu.VMEM(x.shape, x.dtype)

    scratch = [
        like(hidden),
        like(fresh_key_value),
        like(suffix_key_value),
        like(prompt_key_value),
        like(query_down_factors),
        pltpu.VMEM((NA, K, width), bf16),
        pltpu.VMEM((NA, K, C), bf16),
        pltpu.VMEM((NA, K, width), bf16),
        dma((9,)),
        pltpu.VMEM((one,) + hidden.shape, bf16),
        pltpu.VMEM((NS,) + hidden.shape, bf16),
        pltpu.VMEM((NS, N, LANES), jnp.int32),
        pltpu.VMEM((NS, NA, NH, N, LANES), f32),
        pltpu.VMEM((one, N, LANES), f32),
        pltpu.VMEM((N, width), f32),
        pltpu.VMEM((n_new, KV * D), f32),
        pltpu.VMEM((2, n_new, KV * D), bf16),
        pltpu.VMEM((KV, NS * N, C), f32),
        pltpu.VMEM((NS * N, D), f32),
        pltpu.VMEM((NS * N, D), f32),
        pltpu.VMEM((NS * N, LANES), jnp.int32),
        pltpu.VMEM((NS * N, NK), f32),
        pltpu.VMEM((NS * N, NK), bf16),
        pltpu.VMEM((KV, D + 16, keys), bf16),
        pltpu.VMEM((KV, D + 16, n_loc_pad), bf16),
        pltpu.VMEM((n_loc, QC), f32),
        pltpu.VMEM((far, D, QC), bf16),
        pltpu.VMEM((far, D, QC), bf16),
        pltpu.VMEM((far, 2, QC), f32),
        pltpu.VMEM((far, 2, QC), f32),
        pltpu.VMEM((KV, N, NK), f32),
        pltpu.VMEM((KV, NH, N, NK), f32),
        pltpu.VMEM((KV, T, R, C), bf16),
        pltpu.VMEM((KV, T, R, C), bf16),
        dma((one,)), dma((one,)),
        dma((far,)), dma((far,)),
        dma((far, KV)), dma((far, KV)),
        dma((one, KV)), dma((one, KV)),
        dma((one,)), dma((one,)),
        dma((one, KV)), dma((one, KV)),
        dma((NS, NA, NH)), dma((NS, NA, NH)),
        dma((far,)), dma((far,)),
        dma((far,)), dma((far,)),
        dma((KV, NH)), dma((KV, NH)),
        dma((max(KV - 1, 1),)), dma((max(KV - 1, 1),)),
    ]
    smem = pl.BlockSpec(memory_space=pltpu.SMEM)
    vmem = pl.BlockSpec(memory_space=pltpu.VMEM)
    anywhere = pl.BlockSpec(memory_space=pl.ANY)
    results = pl.pallas_call(
        functools.partial(body, (NS, NA, NH, R, T, KV, G, S, K)),
        out_shape=(
            jax.ShapeDtypeStruct(hidden.shape, bf16),
            jax.ShapeDtypeStruct(hidden.shape, bf16),
        ),
        in_specs=[smem, smem, vmem, vmem] + [anywhere] * 9,
        out_specs=(vmem, vmem),
        scratch_shapes=scratch,
        compiler_params=pltpu.CompilerParams(
            collective_id=0, has_side_effects=True, vmem_limit_bytes=56 * 2**20
        ),
        name="decode",
    )(
        suffix_length,
        row_adapter_index.transpose(1, 0),
        jnp.asarray(cos),
        jnp.asarray(sin),
        hidden,
        base_query_rows,
        fresh_key_value,
        suffix_key_value,
        prompt_key_value,
        query_down_factors,
        query_up_factors,
        output_down_factors,
        output_up_factors,
    )
    results = pl.pallas_call(
        finish,
        out_shape=tuple(jax.ShapeDtypeStruct(x.shape, bf16) for x in results),
        in_specs=[vmem, vmem],
        out_specs=(vmem, vmem),
        name="finish",
    )(*results)
    return tuple(x.transpose(1, 0, 2) for x in results)


def solution(mesh):
    rows = P(("groups", "seq", "adapter"), None, "head")
    caches = P(None, ("groups", "seq", "adapter"), None, "head")
    factors = P(("groups", "adapter"), None, "head")
    placed = (
        rows,
        rows,
        caches,
        caches,
        P(("groups", "seq", "adapter")),
        P(("groups", "seq", "adapter"), None),
        P(None, ("groups", "seq"), "head"),
        factors,
        factors,
        factors,
        factors,
    )
    return jax.shard_map(
        on_device, mesh=mesh, in_specs=placed, out_specs=(rows, rows), check_vma=False
    )
```

```python
import functools
import math

import jax
import jax.numpy as jnp
import numpy as np
from jax import lax
from jax.experimental import pallas as pl
from jax.experimental.pallas import tpu as pltpu
from jax.sharding import PartitionSpec as P

HEAD_SIZE = 128
ROPE_BASE = 1000000.0
LANES = 128
MESH = pl.DeviceIdType.MESH
NT = (((1,), (1,)), ((), ()))


def dot_nt(a, b):
    return lax.dot_general(a, b, NT, preferred_element_type=jnp.float32)


def dot_nn(a, b):
    return jnp.dot(a, b, preferred_element_type=jnp.float32)


def xor(a, b, size):
    out, bit = 0, 1
    while bit < size:
        out = out + lax.rem(lax.div(a, bit) + b // bit, 2) * bit
        bit *= 2
    return out


def body(
    cfg,
    len_hbm,
    id_hbm,
    cos_hbm,
    sin_hbm,
    hidden_hbm,
    base_hbm,
    fresh_hbm,
    suffix_hbm,
    prompt_hbm,
    qd_hbm,
    qu_hbm,
    od_hbm,
    ou_hbm,
    att_ref,
    ada_ref,
    len_ref,
    id_ref,
    cos_ref,
    sin_ref,
    hidden_v,
    fresh_v,
    suffix_v,
    prompt_v,
    qd_v,
    qu_v,
    od_v,
    ou_v,
    local_sem,
    hid_in,
    base_in,
    info,
    rank_in,
    rank_out,
    tok_f32,
    fresh_f32,
    fresh_pad,
    base_f,
    cos_v,
    sin_v,
    ids_v,
    wide_f,
    wide_b,
    vt,
    vlt,
    bias_v,
    part_out,
    part_in,
    stat_out,
    stat_in,
    ork_out,
    ork_in,
    att_out,
    hid_s,
    hid_r,
    info_s,
    info_r,
    base_s,
    base_r,
    qu_s,
    qu_r,
    od_s,
    od_r,
    ou_s,
    ou_r,
    rank_s,
    rank_r,
    part_s,
    part_r,
    stat_s,
    stat_r,
    ork_s,
    ork_r,
    att_s,
    att_r,
):
    NS, NA, NH, R, T, KV, G, S, K = cfg
    D = HEAD_SIZE
    N = R * T
    C = G * D
    GT = KV * N
    QC = G * GT
    NK = NA * K
    bf16, f32 = jnp.bfloat16, jnp.float32
    seq, ada, head = lax.axis_index("seq"), lax.axis_index("adapter"), lax.axis_index("head")
    own_k, own_j = lax.rem(seq, KV), lax.div(seq, KV)
    scale = math.log2(math.e) / math.sqrt(D)
    shift = (S + T - 1).bit_length()

    def turn(me, d, size):
        return lax.rem(me + d, size)

    def place(ds, da, dh):
        return {
            "seq": turn(seq, ds, NS),
            "adapter": turn(ada, da, NA),
            "head": turn(head, dh, NH),
        }

    others = [
        (ds, da, dh)
        for ds in range(NS)
        for da in range(NA)
        for dh in range(NH)
        if (ds, da, dh) != (0, 0, 0)
    ]
    barrier = pltpu.get_barrier_semaphore()
    for other in others:
        pl.semaphore_signal(barrier, inc=1, device_id=place(*other), device_id_type=MESH)

    def head_at(where, i):
        return xor(lax.rem(where, KV), KV - 1 - i, KV)

    def columns(k, width):
        return pl.ds(pl.multiple_of(k * width, width), width)

    own_cols = columns(own_k, C)
    loads = []
    for i, (src, dst) in enumerate(
        (
            (len_hbm, len_ref),
            (id_hbm, id_ref),
            (hidden_hbm, hidden_v),
            (qd_hbm, qd_v),
            (cos_hbm, cos_ref),
            (sin_hbm, sin_ref),
            (prompt_hbm, prompt_v),
            (suffix_hbm, suffix_v),
            (fresh_hbm, fresh_v),
            (base_hbm, base_in.at[seq]),
            (qu_hbm.at[0], qu_v.at[ada]),
            (od_hbm.at[0, :, own_cols], od_v.at[ada]),
            (ou_hbm.at[0], ou_v.at[ada]),
        )
    ):
        load = pltpu.make_async_copy(src, dst, local_sem.at[i])
        load.start()
        loads.append(load)
    l_len, l_id, l_hid, l_qd, l_cos, l_sin = loads[:6]
    l_prompt, l_suffix, l_fresh, l_base, l_qu, l_od, l_ou = loads[6:]
    l_len.wait()
    l_id.wait()

    row = lax.broadcasted_iota(jnp.int32, (N, LANES), 0)
    code = jnp.zeros((N, LANES), jnp.int32)
    for r in range(R):
        code = jnp.where(lax.rem(row, R) == r, id_ref[0, r] * 2**shift + len_ref[r], code)
    info[seq] = code + lax.div(row, R)

    pl.semaphore_wait(barrier, len(others))

    sends = []

    def send(src, dst, s_sem, r_sem, device):
        copy = pltpu.make_async_remote_copy(
            src_ref=src,
            dst_ref=dst,
            send_sem=s_sem,
            recv_sem=r_sem,
            device_id=device,
            device_id_type=MESH,
        )
        copy.start()
        sends.append(copy)
        return copy

    hid = {}
    for d in range(1, NA):
        hid[d] = send(
            hidden_hbm, hid_in.at[d - 1], hid_s.at[d - 1], hid_r.at[d - 1], place(0, d, 0)
        )
    far = sorted(range(1, NS), key=lambda d: (-min(d, NS - d), d))
    infos, bases, qus, ods, ous = {}, {}, {}, {}, {}
    for ds in far:
        infos[ds] = send(
            info.at[seq], info.at[seq], info_s.at[ds - 1], info_r.at[ds - 1], place(ds, 0, 0)
        )

    def send_base(i):
        for ds in far:
            cols = columns(head_at(turn(seq, ds, NS), i), C)
            bases[(ds, i)] = send(
                base_hbm.at[:, :, cols], base_in.at[seq, :, :, cols],
                base_s.at[ds - 1, i], base_r.at[ds - 1, i], place(ds, 0, 0),
            )

    def send_qu(i):
        cols = columns(head_at(seq, i), C)
        for d in range(1, NA):
            qus[(d, i)] = send(
                qu_hbm.at[0, :, cols], qu_v.at[ada, :, cols],
                qu_s.at[d - 1, i], qu_r.at[d - 1, i], place(0, d, 0),
            )

    half = max(KV // 2, 1)
    for i in range(half):
        send_base(i)
    send_qu(0)

    def rank_of(ref):
        for t in range(T):
            tok_f32[t * R : (t + 1) * R, :] = ref[t].astype(f32)
        part = dot_nt(tok_f32[...].astype(bf16), qd_v[0])
        return jnp.concatenate([part] * (LANES // K), 1)

    ranks = {}

    def send_rank(src, ds, da, dh):
        ranks[(ds, da, dh)] = send(
            src, rank_in.at[seq, ada, head],
            rank_s.at[ds, da, dh], rank_r.at[ds, da, dh], place(ds, da, dh),
        )

    l_hid.wait()
    l_qd.wait()
    rank_in[seq, ada, head] = rank_of(hidden_v)
    for ds in far + [0]:
        for dh in range(NH):
            if (ds, dh) != (0, 0):
                send_rank(rank_in.at[seq, ada, head], ds, 0, dh)

    l_prompt.wait()
    l_suffix.wait()
    l_fresh.wait()
    n_suf = R * S
    n_new = fresh_f32.shape[0]
    n_loc = n_suf + n_new
    for i in range(2):
        fresh_f32[...] = jnp.zeros_like(fresh_f32)
        for t in range(T):
            fresh_f32[t * R : (t + 1) * R, :] = fresh_v[i, t].astype(f32)
        fresh_pad[i] = fresh_f32[...].astype(bf16)

    def prepare(i):
        cols = columns(head_at(seq, i), D)
        vt[i, 0:D, :] = prompt_v[1, :, cols].astype(f32).T.astype(bf16)
        pad = lax.broadcasted_iota(jnp.int32, (vt.shape[1] - D, vt.shape[2]), 0)
        vt[i, D:, :] = jnp.where(pad == 0, 1.0, 0.0).astype(bf16)
        local = jnp.concatenate(
            [
                suffix_v[1, :, :, cols].reshape(n_suf, D),
                fresh_pad[1, :, cols],
                jnp.zeros((vlt.shape[2] - n_loc, D), bf16),
            ],
            0,
        )
        vlt[i, 0:D, :] = local.astype(f32).T.astype(bf16)
        pad = lax.broadcasted_iota(jnp.int32, (vlt.shape[1] - D, vlt.shape[2]), 0)
        vlt[i, D:, :] = jnp.where(pad == 0, 1.0, 0.0).astype(bf16)

    for i in range(half):
        prepare(i)

    for d in range(1, NA):
        hid[d].wait_recv()
        rank_out[d - 1] = rank_of(hid_in.at[d - 1])
        for ds in far + [0]:
            for dh in range(NH):
                send_rank(rank_out.at[d - 1], ds, d, dh)
    for i in range(half, KV):
        send_base(i)
    for i in range(1, KV):
        send_qu(i)
    for d in range(1, NA):
        ods[d] = send(
            od_hbm.at[0, :, own_cols], od_v.at[ada], od_s.at[d - 1], od_r.at[d - 1],
            place(0, d, 0),
        )
    for i in range(KV):
        for d in range(1, NA):
            cols = slice(i * C, (i + 1) * C)
            ous[(d, i)] = send(
                ou_hbm.at[0, :, cols], ou_v.at[ada, :, cols],
                ou_s.at[d - 1, i], ou_r.at[d - 1, i], place(0, d, 0),
            )

    key = lax.broadcasted_iota(jnp.int32, (n_loc, QC), 0)
    query = lax.rem(lax.broadcasted_iota(jnp.int32, (n_loc, QC), 1), GT)
    q_home, q_token = lax.div(query, N), lax.rem(query, N)
    q_step, q_row = lax.div(q_token, R), lax.rem(q_token, R)
    limit = jnp.zeros((n_loc, QC), jnp.int32)
    for r in range(R):
        limit = jnp.where(q_row == r, len_ref[r], limit)
    new = key - n_suf
    in_suffix = (lax.div(key, S) == q_row) & (lax.rem(key, S) < limit) & (new < 0)
    in_fresh = (lax.rem(new, R) == q_row) & (lax.div(new, R) <= q_step) & (new >= 0)
    bias_v[...] = jnp.where((q_home == own_k) & (in_suffix | in_fresh), 0.0, -1e30)

    for i in range(half, KV):
        prepare(i)

    def convert(i):
        cols = columns(head_at(seq, i), C)
        for ds in far:
            bases[(ds, i)].wait_recv()
        for s in range(NS):
            for t in range(T):
                at = s * N + t * R
                base_f[i, at : at + R, :] = base_in[s, t, :, cols].astype(f32)

    l_base.wait()
    l_qu.wait()
    l_cos.wait()
    l_sin.wait()
    for ds in far:
        infos[ds].wait_recv()
    for s in range(NS):
        ids_v[s * N : (s + 1) * N, :] = info[s]
    codes = ids_v[...]
    position = jnp.bitwise_and(codes, 2**shift - 1)
    cos, sin = jnp.zeros(codes.shape, f32), jnp.zeros(codes.shape, f32)
    for p in range(S + T):
        cos = jnp.where(position == p, cos_ref[p : p + 1, :], cos)
        sin = jnp.where(position == p, sin_ref[p : p + 1, :], sin)
    cos_v[...] = cos
    sin_v[...] = sin
    ids_v[...] = jnp.right_shift(codes, shift)
    convert(0)

    def spread(x):
        return jnp.concatenate([x] * (NK // LANES), 1)

    def adapter_lanes(shape):
        return lax.div(lax.broadcasted_iota(jnp.int32, shape, 1), K)

    for copy in ranks.values():
        copy.wait_recv()
    for s in range(NS):
        ids = ids_v[s * N : (s + 1) * N, :]
        chosen = jnp.zeros((N, LANES), f32)
        for e in range(NA):
            whole = functools.reduce(jnp.add, [rank_in[s, e, h] for h in range(NH)])
            chosen = jnp.where(ids == e, whole, chosen)
        wide_f[s * N : (s + 1) * N, :] = spread(chosen)
    wide = wide_f[...]
    wide_b[...] = jnp.where(adapter_lanes(wide.shape) == spread(ids_v[...]), wide, 0.0).astype(bf16)

    def attend(u):
        i = KV - 1 - u % KV
        target = xor(seq, u, NS)
        k, j = lax.rem(target, KV), lax.div(target, KV)
        rows = pl.ds(pl.multiple_of(j * GT, GT), GT)
        cols = columns(k, D)
        delta = dot_nn(wide_b[rows, :], qu_v[:, :, columns(k, C)].reshape(NK, C))
        merged = base_f[i, rows, :] + delta
        cos, sin = cos_v[rows, :], sin_v[rows, :]
        turned = []
        for g in range(G):
            x = merged[:, g * D : (g + 1) * D]
            turned.append((x * cos + pltpu.roll(x, D // 2, 1) * sin).astype(bf16))
        query = jnp.concatenate(turned, 0)
        local_keys = jnp.concatenate(
            [suffix_v[0, :, :, cols].reshape(n_suf, D), fresh_pad[0, :, cols]], 0
        )
        far_scores = dot_nt(prompt_v[0, :, cols], query)
        shut = jnp.where(j == own_j, 0.0, -1e30)
        near_scores = dot_nt(local_keys, query) + (bias_v[...] + shut)
        peak = jnp.maximum(
            jnp.max(far_scores, 0, keepdims=True), jnp.max(near_scores, 0, keepdims=True)
        )
        far_weight = jnp.exp2((far_scores - peak) * scale).astype(bf16)
        near_weight = jnp.exp2((near_scores - peak) * scale).astype(bf16)
        near_weight = jnp.concatenate(
            [near_weight, jnp.zeros((vlt.shape[2] - n_loc, QC), bf16)], 0
        )
        both = dot_nn(vt[i], far_weight) + dot_nn(vlt[i], near_weight)
        return both[0:D], peak, both[D : D + 1]

    parts, stats = {}, {}
    for u in range(NS - 1, -1, -1):
        i = NS - 1 - u
        if i < KV:
            if i > 0:
                convert(i)
            for d in range(1, NA):
                qus[(d, i)].wait_recv()
        o, m, t = attend(u)
        if u > 0:
            part_out[u - 1] = o.astype(bf16)
            stat_out[u - 1, 0:1, :] = m
            stat_out[u - 1, 1:2, :] = t
            home = {"seq": xor(seq, u, NS)}
            parts[u] = send(
                part_out.at[u - 1], part_in.at[u - 1], part_s.at[u - 1], part_r.at[u - 1], home
            )
            stats[u] = send(
                stat_out.at[u - 1], stat_in.at[u - 1], stat_s.at[u - 1], stat_r.at[u - 1], home
            )
    pieces = [(o, m, t)]
    for u in range(1, NS):
        parts[u].wait_recv()
        stats[u].wait_recv()
        pieces.append(
            (part_in[u - 1].astype(f32), stat_in[u - 1, 0:1, :], stat_in[u - 1, 1:2, :])
        )
    top = functools.reduce(jnp.maximum, [p[1] for p in pieces])
    factors = [jnp.exp2((p[1] - top) * scale) for p in pieces]
    num = functools.reduce(jnp.add, [p[0] * f for p, f in zip(pieces, factors)])
    den = functools.reduce(jnp.add, [p[2] * f for p, f in zip(pieces, factors)])
    turned = (num / den).T
    result = jnp.concatenate([turned[g * GT : (g + 1) * GT] for g in range(G)], 1)

    l_od.wait()
    for d in range(1, NA):
        ods[d].wait_recv()
    down = dot_nt(result.astype(bf16), od_v[...].reshape(NK, C))
    group_rows = pl.ds(pl.multiple_of(own_j * GT, GT), GT)
    down = jnp.where(adapter_lanes(down.shape) == spread(ids_v[group_rows, :]), down, 0.0)
    for jj in range(KV):
        ork_out[jj] = down[jj * N : (jj + 1) * N]
    orks, atts = {}, {}

    def home_of(e):
        jj = xor(own_k, e, KV)
        return jj, own_j * KV + jj

    for e in range(KV - 1, -1, -1):
        jj, where = home_of(e)
        for dh in range(NH):
            if (e, dh) != (0, 0):
                orks[(e, dh)] = send(
                    ork_out.at[jj], ork_in.at[own_k, head],
                    ork_s.at[e, dh], ork_r.at[e, dh],
                    {"seq": where, "head": turn(head, dh, NH)},
                )
    for jj in range(KV):
        for t in range(T):
            at = jj * N + t * R
            att_out[jj, t] = result[at : at + R].astype(bf16)
    for e in range(KV - 1, 0, -1):
        jj, where = home_of(e)
        atts[e] = send(
            att_out.at[jj], att_ref.at[:, :, own_cols], att_s.at[e - 1], att_r.at[e - 1],
            {"seq": where},
        )
    att_ref[:, :, own_cols] = att_out[own_k]

    ork_in[own_k, head] = ork_out[own_k]
    for copy in orks.values():
        copy.wait_recv()
    total = functools.reduce(
        jnp.add, [ork_in[k, h] for k in range(KV) for h in range(NH)]
    ).astype(bf16)
    l_ou.wait()
    for i in range(KV):
        cols = slice(i * C, (i + 1) * C)
        for d in range(1, NA):
            ous[(d, i)].wait_recv()
        up = dot_nn(total, ou_v[:, :, cols].reshape(NK, C))
        for t in range(T):
            ada_ref[t, :, cols] = up[t * R : (t + 1) * R].astype(bf16)
    for copy in atts.values():
        copy.wait_recv()

    for copy in sends:
        copy.wait_send()


def finish(first, second, att_hbm, ada_hbm, sem):
    copies = [
        pltpu.make_async_copy(first, att_hbm, sem.at[0]),
        pltpu.make_async_copy(second, ada_hbm, sem.at[1]),
    ]
    for copy in copies:
        copy.start()
    for copy in copies:
        copy.wait()


def on_device(
    hidden,
    base_query_rows,
    fresh_key_value,
    suffix_key_value,
    suffix_length,
    row_adapter_index,
    prompt_key_value,
    query_down_factors,
    query_up_factors,
    output_down_factors,
    output_up_factors,
):
    NS, NA, NH = lax.axis_size("seq"), lax.axis_size("adapter"), lax.axis_size("head")
    hidden, base_query_rows = (x.transpose(1, 0, 2) for x in (hidden, base_query_rows))
    fresh_key_value = fresh_key_value.transpose(0, 2, 1, 3)
    T, R, width = hidden.shape
    D = HEAD_SIZE
    KV = prompt_key_value.shape[2] // D
    G = width // D // KV
    S = suffix_key_value.shape[2]
    keys = prompt_key_value.shape[1]
    N, C = R * T, G * D
    K = query_down_factors.shape[1]
    GT = KV * N
    QC, NK = G * GT, NA * K
    assert query_down_factors.shape[0] == 1
    assert NS % KV == 0 and NS & (NS - 1) == 0 and KV & (KV - 1) == 0
    assert GT % 16 == 0 and LANES % K == 0 and NK % LANES == 0
    prompt_total = keys * NS
    positions = prompt_total + np.arange(S + T, dtype=np.float64)
    frequency = ROPE_BASE ** (-2.0 * np.arange(D // 2, dtype=np.float64) / D)
    angle = positions[:, None] * frequency[None, :]
    cos = np.concatenate([np.cos(angle), np.cos(angle)], 1).astype(np.float32)
    sin = np.concatenate([-np.sin(angle), np.sin(angle)], 1).astype(np.float32)
    bf16, f32 = jnp.bfloat16, jnp.float32
    dma = pltpu.SemaphoreType.DMA
    one = max(NA - 1, 1)
    far = max(NS - 1, 1)
    n_new = -(-N // 16) * 16
    n_loc = R * S + n_new
    n_loc_pad = -(-n_loc // LANES) * LANES

    def like(x):
        return pltpu.VMEM(x.shape, x.dtype)

    scratch = [
        pltpu.SMEM((R,), jnp.int32),
        pltpu.SMEM((1, R), jnp.int32),
        pltpu.VMEM(cos.shape, f32),
        pltpu.VMEM(sin.shape, f32),
        like(hidden),
        like(fresh_key_value),
        like(suffix_key_value),
        like(prompt_key_value),
        like(query_down_factors),
        pltpu.VMEM((NA, K, width), bf16),
        pltpu.VMEM((NA, K, C), bf16),
        pltpu.VMEM((NA, K, width), bf16),
        dma((13,)),
        pltpu.VMEM((one,) + hidden.shape, bf16),
        pltpu.VMEM((NS,) + hidden.shape, bf16),
        pltpu.VMEM((NS, N, LANES), jnp.int32),
        pltpu.VMEM((NS, NA, NH, N, LANES), f32),
        pltpu.VMEM((one, N, LANES), f32),
        pltpu.VMEM((N, width), f32),
        pltpu.VMEM((n_new, KV * D), f32),
        pltpu.VMEM((2, n_new, KV * D), bf16),
        pltpu.VMEM((KV, NS * N, C), f32),
        pltpu.VMEM((NS * N, D), f32),
        pltpu.VMEM((NS * N, D), f32),
        pltpu.VMEM((NS * N, LANES), jnp.int32),
        pltpu.VMEM((NS * N, NK), f32),
        pltpu.VMEM((NS * N, NK), bf16),
        pltpu.VMEM((KV, D + 16, keys), bf16),
        pltpu.VMEM((KV, D + 16, n_loc_pad), bf16),
        pltpu.VMEM((n_loc, QC), f32),
        pltpu.VMEM((far, D, QC), bf16),
        pltpu.VMEM((far, D, QC), bf16),
        pltpu.VMEM((far, 2, QC), f32),
        pltpu.VMEM((far, 2, QC), f32),
        pltpu.VMEM((KV, N, NK), f32),
        pltpu.VMEM((KV, NH, N, NK), f32),
        pltpu.VMEM((KV, T, R, C), bf16),
        dma((one,)), dma((one,)),
        dma((far,)), dma((far,)),
        dma((far, KV)), dma((far, KV)),
        dma((one, KV)), dma((one, KV)),
        dma((one,)), dma((one,)),
        dma((one, KV)), dma((one, KV)),
        dma((NS, NA, NH)), dma((NS, NA, NH)),
        dma((far,)), dma((far,)),
        dma((far,)), dma((far,)),
        dma((KV, NH)), dma((KV, NH)),
        dma((max(KV - 1, 1),)), dma((max(KV - 1, 1),)),
    ]
    vmem = pl.BlockSpec(memory_space=pltpu.VMEM)
    anywhere = pl.BlockSpec(memory_space=pl.ANY)
    results = pl.pallas_call(
        functools.partial(body, (NS, NA, NH, R, T, KV, G, S, K)),
        out_shape=(like(hidden), like(hidden)),
        in_specs=[anywhere] * 13,
        out_specs=(vmem, vmem),
        scratch_shapes=scratch,
        compiler_params=pltpu.CompilerParams(
            collective_id=0, has_side_effects=True, vmem_limit_bytes=56 * 2**20
        ),
        name="decode",
    )(
        suffix_length,
        row_adapter_index.transpose(1, 0),
        jnp.asarray(cos),
        jnp.asarray(sin),
        hidden,
        base_query_rows,
        fresh_key_value,
        suffix_key_value,
        prompt_key_value,
        query_down_factors,
        query_up_factors,
        output_down_factors,
        output_up_factors,
    )
    results = pl.pallas_call(
        finish,
        out_shape=tuple(jax.ShapeDtypeStruct(x.shape, bf16) for x in results),
        in_specs=[vmem, vmem],
        out_specs=(anywhere, anywhere),
        scratch_shapes=[dma((2,))],
        name="finish",
    )(*(pltpu.with_memory_space_constraint(x, pltpu.VMEM) for x in results))
    return tuple(x.transpose(1, 0, 2) for x in results)


def solution(mesh):
    rows = P(("groups", "seq", "adapter"), None, "head")
    caches = P(None, ("groups", "seq", "adapter"), None, "head")
    factors = P(("groups", "adapter"), None, "head")
    placed = (
        rows,
        rows,
        caches,
        caches,
        P(("groups", "seq", "adapter")),
        P(("groups", "seq", "adapter"), None),
        P(None, ("groups", "seq"), "head"),
        factors,
        factors,
        factors,
        factors,
    )
    return jax.shard_map(
        on_device, mesh=mesh, in_specs=placed, out_specs=(rows, rows), check_vma=False
    )
```

```python
import functools
import math

import jax
import jax.numpy as jnp
import numpy as np
from jax import lax
from jax.experimental import pallas as pl
from jax.experimental.pallas import tpu as pltpu
from jax.sharding import PartitionSpec as P

HEAD_SIZE = 128
ROPE_BASE = 1000000.0
LANES = 128
OU_RELAYED, OU_DIRECT = 0, 8
MESH = pl.DeviceIdType.MESH
NT = (((1,), (1,)), ((), ()))


def dot_nt(a, b):
    return lax.dot_general(a, b, NT, preferred_element_type=jnp.float32)


def dot_nn(a, b):
    return jnp.dot(a, b, preferred_element_type=jnp.float32)


def xor(a, b, size):
    out, bit = 0, 1
    while bit < size:
        out = out + lax.rem(lax.div(a, bit) + b // bit, 2) * bit
        bit *= 2
    return out


def body(
    cfg,
    len_hbm,
    id_hbm,
    cos_hbm,
    sin_hbm,
    hidden_hbm,
    base_hbm,
    fresh_hbm,
    suffix_hbm,
    prompt_hbm,
    qd_hbm,
    qu_hbm,
    od_hbm,
    ou_hbm,
    att_ref,
    ada_ref,
    len_ref,
    id_ref,
    cos_ref,
    sin_ref,
    hidden_v,
    fresh_v,
    suffix_v,
    prompt_v,
    qd_v,
    qu_v,
    od_v,
    ou_v,
    local_sem,
    hid_in,
    base_in,
    info,
    rank_in,
    rank_out,
    tok_f32,
    fresh_f32,
    fresh_pad,
    base_f,
    cos_v,
    sin_v,
    ids_v,
    wide_f,
    wide_b,
    vt,
    vlt,
    bias_v,
    part_out,
    part_in,
    stat_out,
    stat_in,
    ork_out,
    ork_in,
    att_out,
    hid_s,
    hid_r,
    info_s,
    info_r,
    base_s,
    base_r,
    qu_s,
    qu_r,
    od_s,
    od_r,
    ou_s,
    ou_r,
    rank_s,
    rank_r,
    part_s,
    part_r,
    stat_s,
    stat_r,
    ork_s,
    ork_r,
    att_s,
    att_r,
):
    NS, NA, NH, R, T, KV, G, S, K = cfg
    D = HEAD_SIZE
    N = R * T
    C = G * D
    GT = KV * N
    QC = G * GT
    NK = NA * K
    bf16, f32 = jnp.bfloat16, jnp.float32
    seq, ada, head = lax.axis_index("seq"), lax.axis_index("adapter"), lax.axis_index("head")
    own_k, own_j = lax.rem(seq, KV), lax.div(seq, KV)
    scale = math.log2(math.e) / math.sqrt(D)
    shift = (S + T - 1).bit_length()

    def turn(me, d, size):
        return lax.rem(me + d, size)

    def place(ds, da, dh):
        return {
            "seq": turn(seq, ds, NS),
            "adapter": turn(ada, da, NA),
            "head": turn(head, dh, NH),
        }

    far = sorted(range(1, NS), key=lambda d: (-min(d, NS - d), d))
    others = [
        (ds, da, dh)
        for ds in far + [0]
        for da in range(NA - 1, -1, -1)
        for dh in range(NH)
        if (ds, da, dh) != (0, 0, 0)
    ]
    barrier = pltpu.get_barrier_semaphore()
    for other in others:
        pl.semaphore_signal(barrier, inc=1, device_id=place(*other), device_id_type=MESH)

    def head_at(where, i):
        return xor(lax.rem(where, KV), KV - 1 - i, KV)

    def columns(k, width):
        return pl.ds(pl.multiple_of(k * width, width), width)

    own_cols = columns(own_k, C)
    loads = []
    for i, (src, dst) in enumerate(
        (
            (len_hbm, len_ref),
            (id_hbm, id_ref),
            (hidden_hbm, hidden_v),
            (qd_hbm, qd_v),
            (cos_hbm, cos_ref),
            (sin_hbm, sin_ref),
            (prompt_hbm, prompt_v),
            (suffix_hbm, suffix_v),
            (fresh_hbm, fresh_v),
            (base_hbm, base_in.at[seq]),
            (qu_hbm.at[0], qu_v.at[ada]),
            (od_hbm.at[0, :, own_cols], od_v.at[ada]),
            (ou_hbm.at[0], ou_v.at[ada]),
        )
    ):
        load = pltpu.make_async_copy(src, dst, local_sem.at[i])
        load.start()
        loads.append(load)
    l_len, l_id, l_hid, l_qd, l_cos, l_sin = loads[:6]
    l_prompt, l_suffix, l_fresh, l_base, l_qu, l_od, l_ou = loads[6:]
    l_len.wait()
    l_id.wait()

    token = lax.broadcasted_iota(jnp.int32, (1, LANES), 1)
    code = jnp.zeros((1, LANES), jnp.int32)
    for r in range(R):
        code = jnp.where(lax.rem(token, R) == r, id_ref[0, r] * 2**shift + len_ref[r], code)
    info[seq] = (code + lax.div(token, R)).astype(f32)

    pl.semaphore_wait(barrier, len(others))

    sends = []

    def send(src, dst, s_sem, r_sem, device):
        copy = pltpu.make_async_remote_copy(
            src_ref=src,
            dst_ref=dst,
            send_sem=s_sem,
            recv_sem=r_sem,
            device_id=device,
            device_id_type=MESH,
        )
        copy.start()
        sends.append(copy)
        return copy

    hid = {}
    for d in range(1, NA):
        hid[d] = send(
            hidden_hbm, hid_in.at[d - 1], hid_s.at[d - 1], hid_r.at[d - 1], place(0, d, 0)
        )
    infos, bases, qus, ods, ous = {}, {}, {}, {}, {}
    for ds in far:
        infos[ds] = send(
            info.at[seq], info.at[seq], info_s.at[ds - 1], info_r.at[ds - 1], place(ds, 0, 0)
        )

    def base_cols(where, b):
        pair = xor(lax.div(lax.rem(where, KV), 2), KV // 2 - 1 - b, KV // 2)
        return columns(pair, 2 * C)

    def send_base(b):
        for u in range(NS - 1, 0, -1):
            to = xor(seq, u, NS)
            cols = base_cols(to, b)
            bases[(u, b)] = send(
                base_hbm.at[:, :, cols], base_in.at[seq, :, :, cols],
                base_s.at[u - 1, b], base_r.at[u - 1, b], {"seq": to},
            )

    def send_qu(i):
        cols = columns(head_at(seq, i), C)
        for d in range(1, NA):
            qus[(d, i)] = send(
                qu_hbm.at[0, :, cols], qu_v.at[ada, :, cols],
                qu_s.at[d - 1, i], qu_r.at[d - 1, i], place(0, d, 0),
            )

    parity = lax.rem(seq, 2)
    neighbour = {"seq": xor(seq, 1, NS)}
    ou_width = ou_hbm.shape[2] // (2 * OU_RELAYED + OU_DIRECT)

    def ou_cols(n, side):
        if n < OU_RELAYED:
            return columns(side * OU_RELAYED + n, ou_width)
        return columns(OU_RELAYED + n, ou_width)

    def source_slot(d):
        return lax.rem(ada + NA - d, NA)

    relays = {}

    def relay_qu(i):
        cols = columns(head_at(seq, i), C)
        for d in range(1, NA):
            qus[(d, i)].wait_recv()
            part = qu_v.at[source_slot(d), :, cols]
            qus[(d, i + 1)] = send(
                part, part, qu_s.at[d - 1, i + 1], qu_r.at[d - 1, i + 1], neighbour
            )

    def relay_ou(n):
        cols = ou_cols(n, parity)
        for d in range(1, NA):
            ous[(d, n)].wait_recv()
            part = ou_v.at[source_slot(d), :, cols]
            at = OU_RELAYED + OU_DIRECT + n
            relays[("ou", d, n)] = send(
                part, part, ou_s.at[d - 1, at], ou_r.at[d - 1, at], neighbour
            )

    turns = list(range(KV))
    half = KV // 2
    send_base(0)
    send_qu(0)

    packed = rank_in.shape[3]

    def rank_of(ref):
        for t in range(T):
            tok_f32[t * R : (t + 1) * R, :] = ref[t].astype(f32)
        part = dot_nt(tok_f32[...].astype(bf16), qd_v[0])
        return jnp.concatenate([part[p * packed : (p + 1) * packed] for p in range(LANES // K)], 1)

    ranks = {}

    def send_rank(src, ds, da, dh):
        ranks[(ds, da, dh)] = send(
            src, rank_in.at[seq, ada, head],
            rank_s.at[ds, da, dh], rank_r.at[ds, da, dh], place(ds, da, dh),
        )

    tok_f32[N:, :] = jnp.zeros((tok_f32.shape[0] - N, tok_f32.shape[1]), f32)
    l_hid.wait()
    l_qd.wait()
    rank_in[seq, ada, head] = rank_of(hidden_v)
    for ds in far + [0]:
        for dh in range(NH):
            if (ds, dh) != (0, 0):
                send_rank(rank_in.at[seq, ada, head], ds, 0, dh)

    l_prompt.wait()
    l_suffix.wait()
    l_fresh.wait()
    n_suf = R * S
    n_new = fresh_f32.shape[0]
    n_loc = n_suf + n_new
    for i in range(2):
        fresh_f32[...] = jnp.zeros_like(fresh_f32)
        for t in range(T):
            fresh_f32[t * R : (t + 1) * R, :] = fresh_v[i, t].astype(f32)
        fresh_pad[i] = fresh_f32[...].astype(bf16)

    def prepare(i):
        cols = columns(head_at(seq, i), D)
        vt[i, 0:D, :] = prompt_v[1, :, cols].astype(f32).T.astype(bf16)
        pad = lax.broadcasted_iota(jnp.int32, (vt.shape[1] - D, vt.shape[2]), 0)
        vt[i, D:, :] = jnp.where(pad == 0, 1.0, 0.0).astype(bf16)
        local = jnp.concatenate(
            [
                suffix_v[1, :, :, cols].reshape(n_suf, D),
                fresh_pad[1, :, cols],
                jnp.zeros((vlt.shape[2] - n_loc, D), bf16),
            ],
            0,
        )
        vlt[i, 0:D, :] = local.astype(f32).T.astype(bf16)
        pad = lax.broadcasted_iota(jnp.int32, (vlt.shape[1] - D, vlt.shape[2]), 0)
        vlt[i, D:, :] = jnp.where(pad == 0, 1.0, 0.0).astype(bf16)

    for i in turns[:half]:
        prepare(i)

    for d in range(1, NA):
        hid[d].wait_recv()
        rank_out[d - 1] = rank_of(hid_in.at[d - 1])
        for ds in far + [0]:
            for dh in range(NH):
                send_rank(rank_out.at[d - 1], ds, d, dh)
    for i in range(2, KV, 2):
        send_qu(i)
    for b in range(1, half):
        send_base(b)
    for d in range(1, NA):
        ods[d] = send(
            od_hbm.at[0, :, own_cols], od_v.at[ada], od_s.at[d - 1], od_r.at[d - 1],
            place(0, d, 0),
        )
    for n in range(OU_RELAYED + OU_DIRECT):
        cols = ou_cols(n, parity)
        for d in range(1, NA):
            ous[(d, n)] = send(
                ou_hbm.at[0, :, cols], ou_v.at[ada, :, cols],
                ou_s.at[d - 1, n], ou_r.at[d - 1, n], place(0, d, 0),
            )

    key = lax.broadcasted_iota(jnp.int32, (n_loc, QC), 0)
    query = lax.rem(lax.broadcasted_iota(jnp.int32, (n_loc, QC), 1), GT)
    q_home, q_token = lax.div(query, N), lax.rem(query, N)
    q_step, q_row = lax.div(q_token, R), lax.rem(q_token, R)
    limit = jnp.zeros((n_loc, QC), jnp.int32)
    for r in range(R):
        limit = jnp.where(q_row == r, len_ref[r], limit)
    new = key - n_suf
    in_suffix = (lax.div(key, S) == q_row) & (lax.rem(key, S) < limit) & (new < 0)
    in_fresh = (lax.rem(new, R) == q_row) & (lax.div(new, R) <= q_step) & (new >= 0)
    bias_v[...] = jnp.where((q_home == own_k) & (in_suffix | in_fresh), 0.0, -1e30)

    for i in turns[half:]:
        prepare(i)

    landed = set()

    def convert(i):
        cols = columns(head_at(seq, i), C)
        for u in range(1, NS):
            if (u, i // 2) not in landed:
                bases[(u, i // 2)].wait_recv()
                landed.add((u, i // 2))
        for s in range(NS):
            for t in range(T):
                at = s * N + t * R
                base_f[i, at : at + R, :] = base_in[s, t, :, cols].astype(f32)

    l_base.wait()
    l_qu.wait()
    l_cos.wait()
    l_sin.wait()
    for ds in far:
        infos[ds].wait_recv()
    row = lax.broadcasted_iota(jnp.int32, (N, LANES), 0)
    diagonal = row == lax.broadcasted_iota(jnp.int32, (N, LANES), 1)
    for s in range(NS):
        code = jnp.sum(jnp.where(diagonal, info[s], 0.0), 1, keepdims=True)
        ids_v[s * N : (s + 1) * N, :] = jnp.broadcast_to(code.astype(jnp.int32), (N, LANES))
    codes = ids_v[...]
    position = jnp.bitwise_and(codes, 2**shift - 1)
    cos, sin = jnp.zeros(codes.shape, f32), jnp.zeros(codes.shape, f32)
    for p in range(S + T):
        cos = jnp.where(position == p, cos_ref[p : p + 1, :], cos)
        sin = jnp.where(position == p, sin_ref[p : p + 1, :], sin)
    cos_v[...] = cos
    sin_v[...] = sin
    ids_v[...] = jnp.right_shift(codes, shift)
    convert(0)
    relay_qu(0)

    def spread(x):
        return jnp.concatenate([x] * (NK // LANES), 1)

    def adapter_lanes(shape):
        return lax.div(lax.broadcasted_iota(jnp.int32, shape, 1), K)

    for copy in ranks.values():
        copy.wait_recv()
    for s in range(NS):
        ids = ids_v[s * N : (s + 1) * N, :]
        chosen = jnp.zeros((N, LANES), f32)
        for e in range(NA):
            whole = functools.reduce(jnp.add, [rank_in[s, e, h] for h in range(NH)])
            rows = [whole[:, p * K : (p + 1) * K] for p in range(LANES // K)]
            whole = jnp.concatenate([jnp.concatenate(rows, 0)] * (LANES // K), 1)[0:N]
            chosen = jnp.where(ids == e, whole, chosen)
        wide_f[s * N : (s + 1) * N, :] = spread(chosen)
    wide = wide_f[...]
    wide_b[...] = jnp.where(adapter_lanes(wide.shape) == spread(ids_v[...]), wide, 0.0).astype(bf16)

    def attend(u):
        i = KV - 1 - u % KV
        target = xor(seq, u, NS)
        k, j = lax.rem(target, KV), lax.div(target, KV)
        rows = pl.ds(pl.multiple_of(j * GT, GT), GT)
        cols = columns(k, D)
        delta = dot_nn(wide_b[rows, :], qu_v[:, :, columns(k, C)].reshape(NK, C))
        merged = base_f[i, rows, :] + delta
        cos, sin = cos_v[rows, :], sin_v[rows, :]
        turned = []
        for g in range(G):
            x = merged[:, g * D : (g + 1) * D]
            turned.append((x * cos + pltpu.roll(x, D // 2, 1) * sin).astype(bf16))
        query = jnp.concatenate(turned, 0)
        local_keys = jnp.concatenate(
            [suffix_v[0, :, :, cols].reshape(n_suf, D), fresh_pad[0, :, cols]], 0
        )
        far_scores = dot_nt(prompt_v[0, :, cols], query)
        shut = jnp.where(j == own_j, 0.0, -1e30)
        near_scores = dot_nt(local_keys, query) + (bias_v[...] + shut)
        peak = jnp.maximum(
            jnp.max(far_scores, 0, keepdims=True), jnp.max(near_scores, 0, keepdims=True)
        )
        far_weight = jnp.exp2((far_scores - peak) * scale).astype(bf16)
        near_weight = jnp.exp2((near_scores - peak) * scale).astype(bf16)
        near_weight = jnp.concatenate(
            [near_weight, jnp.zeros((vlt.shape[2] - n_loc, QC), bf16)], 0
        )
        both = dot_nn(vt[i], far_weight) + dot_nn(vlt[i], near_weight)
        return both[0:D], peak, both[D : D + 1]

    parts, stats = {}, {}
    units = [(j - 1) * KV + KV - 1 - i for j in range(NS // KV, 0, -1) for i in turns]
    for at, u in enumerate(units):
        i = KV - 1 - u % KV
        if at < KV:
            if i % 2:
                for d in range(1, NA):
                    qus[(d, i)].wait_recv()
            elif i > 0:
                relay_qu(i)
            if i > 0:
                convert(i)
        o, m, t = attend(u)
        if u > 0:
            part_out[u - 1] = o.astype(bf16)
            stat_out[u - 1, 0:1, :] = m
            stat_out[u - 1, 1:2, :] = t
            home = {"seq": xor(seq, u, NS)}
            parts[u] = send(
                part_out.at[u - 1], part_in.at[u - 1], part_s.at[u - 1], part_r.at[u - 1], home
            )
            stats[u] = send(
                stat_out.at[u - 1], stat_in.at[u - 1], stat_s.at[u - 1], stat_r.at[u - 1], home
            )
    for n in range(OU_RELAYED):
        relay_ou(n)
    whole = (o, m, t)
    for u in [u for u in units if u > 0]:
        parts[u].wait_recv()
        stats[u].wait_recv()
        o, m, t = part_in[u - 1].astype(f32), stat_in[u - 1, 0:1, :], stat_in[u - 1, 1:2, :]
        top = jnp.maximum(whole[1], m)
        one, two = jnp.exp2((whole[1] - top) * scale), jnp.exp2((m - top) * scale)
        whole = (whole[0] * one + o * two, top, whole[2] * one + t * two)
    turned = (whole[0] * (1.0 / whole[2])).T
    result = jnp.concatenate([turned[g * GT : (g + 1) * GT] for g in range(G)], 1)

    l_od.wait()
    for d in range(1, NA):
        ods[d].wait_recv()
    down = dot_nt(result.astype(bf16), od_v[...].reshape(NK, C))
    group_rows = pl.ds(pl.multiple_of(own_j * GT, GT), GT)
    down = jnp.where(adapter_lanes(down.shape) == spread(ids_v[group_rows, :]), down, 0.0)
    for jj in range(KV):
        ork_out[jj] = down[jj * N : (jj + 1) * N]
    orks, atts = {}, {}

    def home_of(e):
        jj = xor(own_k, e, KV)
        return jj, own_j * KV + jj

    for e in range(KV - 1, -1, -1):
        jj, where = home_of(e)
        for dh in range(NH):
            if (e, dh) != (0, 0):
                orks[(e, dh)] = send(
                    ork_out.at[jj], ork_in.at[own_k, head],
                    ork_s.at[e, dh], ork_r.at[e, dh],
                    {"seq": where, "head": turn(head, dh, NH)},
                )
    for jj in range(KV):
        for t in range(T):
            at = jj * N + t * R
            att_out[jj, t] = result[at : at + R].astype(bf16)
    for e in range(KV - 1, 0, -1):
        jj, where = home_of(e)
        atts[e] = send(
            att_out.at[jj], att_ref.at[:, :, own_cols], att_s.at[e - 1], att_r.at[e - 1],
            {"seq": where},
        )
    att_ref[:, :, own_cols] = att_out[own_k]

    ork_in[own_k, head] = ork_out[own_k]
    for copy in orks.values():
        copy.wait_recv()
    total = functools.reduce(
        jnp.add, [ork_in[k, h] for k in range(KV) for h in range(NH)]
    ).astype(bf16)
    l_ou.wait()

    def raise_up(cols):
        up = dot_nn(total, ou_v[:, :, cols].reshape(NK, ou_width))
        for t in range(T):
            ada_ref[t, :, cols] = up[t * R : (t + 1) * R].astype(bf16)

    for n in range(OU_RELAYED + OU_DIRECT):
        if n >= OU_RELAYED:
            for d in range(1, NA):
                ous[(d, n)].wait_recv()
        raise_up(ou_cols(n, parity))
    for n in range(OU_RELAYED):
        for d in range(1, NA):
            relays[("ou", d, n)].wait_recv()
        raise_up(ou_cols(n, 1 - parity))
    for copy in atts.values():
        copy.wait_recv()

    for copy in sends:
        copy.wait_send()


def finish(first, second, att_hbm, ada_hbm, sem):
    copies = [
        pltpu.make_async_copy(first, att_hbm, sem.at[0]),
        pltpu.make_async_copy(second, ada_hbm, sem.at[1]),
    ]
    for copy in copies:
        copy.start()
    for copy in copies:
        copy.wait()


def on_device(
    hidden,
    base_query_rows,
    fresh_key_value,
    suffix_key_value,
    suffix_length,
    row_adapter_index,
    prompt_key_value,
    query_down_factors,
    query_up_factors,
    output_down_factors,
    output_up_factors,
):
    NS, NA, NH = lax.axis_size("seq"), lax.axis_size("adapter"), lax.axis_size("head")
    hidden, base_query_rows = (x.transpose(1, 0, 2) for x in (hidden, base_query_rows))
    fresh_key_value = fresh_key_value.transpose(0, 2, 1, 3)
    T, R, width = hidden.shape
    D = HEAD_SIZE
    KV = prompt_key_value.shape[2] // D
    G = width // D // KV
    S = suffix_key_value.shape[2]
    keys = prompt_key_value.shape[1]
    N, C = R * T, G * D
    K = query_down_factors.shape[1]
    GT = KV * N
    QC, NK = G * GT, NA * K
    assert query_down_factors.shape[0] == 1
    assert width % (LANES * (2 * OU_RELAYED + OU_DIRECT)) == 0 and KV >= 2
    assert NS % KV == 0 and NS & (NS - 1) == 0 and KV & (KV - 1) == 0
    assert GT % 16 == 0 and LANES % K == 0 and NK % LANES == 0
    prompt_total = keys * NS
    positions = prompt_total + np.arange(S + T, dtype=np.float64)
    frequency = ROPE_BASE ** (-2.0 * np.arange(D // 2, dtype=np.float64) / D)
    angle = positions[:, None] * frequency[None, :]
    cos = np.concatenate([np.cos(angle), np.cos(angle)], 1).astype(np.float32)
    sin = np.concatenate([-np.sin(angle), np.sin(angle)], 1).astype(np.float32)
    bf16, f32 = jnp.bfloat16, jnp.float32
    dma = pltpu.SemaphoreType.DMA
    one = max(NA - 1, 1)
    far = max(NS - 1, 1)
    packed = -(-N // (8 * (LANES // K))) * 8
    n_new = -(-N // 16) * 16
    n_loc = R * S + n_new
    n_loc_pad = -(-n_loc // LANES) * LANES

    def like(x):
        return pltpu.VMEM(x.shape, x.dtype)

    scratch = [
        pltpu.SMEM((R,), jnp.int32),
        pltpu.SMEM((1, R), jnp.int32),
        pltpu.VMEM(cos.shape, f32),
        pltpu.VMEM(sin.shape, f32),
        like(hidden),
        like(fresh_key_value),
        like(suffix_key_value),
        like(prompt_key_value),
        like(query_down_factors),
        pltpu.VMEM((NA, K, width), bf16),
        pltpu.VMEM((NA, K, C), bf16),
        pltpu.VMEM((NA, K, width), bf16),
        dma((13,)),
        pltpu.VMEM((one,) + hidden.shape, bf16),
        pltpu.VMEM((NS,) + hidden.shape, bf16),
        pltpu.VMEM((NS, 1, LANES), f32),
        pltpu.VMEM((NS, NA, NH, packed, LANES), f32),
        pltpu.VMEM((one, packed, LANES), f32),
        pltpu.VMEM((packed * (LANES // K), width), f32),
        pltpu.VMEM((n_new, KV * D), f32),
        pltpu.VMEM((2, n_new, KV * D), bf16),
        pltpu.VMEM((KV, NS * N, C), f32),
        pltpu.VMEM((NS * N, D), f32),
        pltpu.VMEM((NS * N, D), f32),
        pltpu.VMEM((NS * N, LANES), jnp.int32),
        pltpu.VMEM((NS * N, NK), f32),
        pltpu.VMEM((NS * N, NK), bf16),
        pltpu.VMEM((KV, D + 16, keys), bf16),
        pltpu.VMEM((KV, D + 16, n_loc_pad), bf16),
        pltpu.VMEM((n_loc, QC), f32),
        pltpu.VMEM((far, D, QC), bf16),
        pltpu.VMEM((far, D, QC), bf16),
        pltpu.VMEM((far, 2, QC), f32),
        pltpu.VMEM((far, 2, QC), f32),
        pltpu.VMEM((KV, N, NK), f32),
        pltpu.VMEM((KV, NH, N, NK), f32),
        pltpu.VMEM((KV, T, R, C), bf16),
        dma((one,)), dma((one,)),
        dma((far,)), dma((far,)),
        dma((far, KV // 2)), dma((far, KV // 2)),
        dma((one, KV)), dma((one, KV)),
        dma((one,)), dma((one,)),
        dma((one, 2 * OU_RELAYED + OU_DIRECT)), dma((one, 2 * OU_RELAYED + OU_DIRECT)),
        dma((NS, NA, NH)), dma((NS, NA, NH)),
        dma((far,)), dma((far,)),
        dma((far,)), dma((far,)),
        dma((KV, NH)), dma((KV, NH)),
        dma((max(KV - 1, 1),)), dma((max(KV - 1, 1),)),
    ]
    vmem = pl.BlockSpec(memory_space=pltpu.VMEM)
    anywhere = pl.BlockSpec(memory_space=pl.ANY)
    results = pl.pallas_call(
        functools.partial(body, (NS, NA, NH, R, T, KV, G, S, K)),
        out_shape=(like(hidden), like(hidden)),
        in_specs=[anywhere] * 13,
        out_specs=(vmem, vmem),
        scratch_shapes=scratch,
        compiler_params=pltpu.CompilerParams(
            collective_id=0, has_side_effects=True, vmem_limit_bytes=56 * 2**20
        ),
        name="decode",
    )(
        suffix_length,
        row_adapter_index.transpose(1, 0),
        jnp.asarray(cos),
        jnp.asarray(sin),
        hidden,
        base_query_rows,
        fresh_key_value,
        suffix_key_value,
        prompt_key_value,
        query_down_factors,
        query_up_factors,
        output_down_factors,
        output_up_factors,
    )
    results = pl.pallas_call(
        finish,
        out_shape=tuple(jax.ShapeDtypeStruct(x.shape, bf16) for x in results),
        in_specs=[vmem, vmem],
        out_specs=(anywhere, anywhere),
        scratch_shapes=[dma((2,))],
        name="finish",
    )(*(pltpu.with_memory_space_constraint(x, pltpu.VMEM) for x in results))
    return tuple(x.transpose(1, 0, 2) for x in results)


def solution(mesh):
    rows = P(("groups", "seq", "adapter"), None, "head")
    caches = P(None, ("groups", "seq", "adapter"), None, "head")
    factors = P(("groups", "adapter"), None, "head")
    placed = (
        rows,
        rows,
        caches,
        caches,
        P(("groups", "seq", "adapter")),
        P(("groups", "seq", "adapter"), None),
        P(None, ("groups", "seq"), "head"),
        factors,
        factors,
        factors,
        factors,
    )
    return jax.shard_map(
        on_device, mesh=mesh, in_specs=placed, out_specs=(rows, rows), check_vma=False
    )
```

```python
import functools
import math

import jax
import jax.numpy as jnp
import numpy as np
from jax import lax
from jax.experimental import pallas as pl
from jax.experimental.pallas import tpu as pltpu
from jax.sharding import PartitionSpec as P

HEAD_SIZE = 128
ROPE_BASE = 1000000.0
LANES = 128
OU_RELAYED, OU_DIRECT = 2, 4
MESH = pl.DeviceIdType.MESH
NT = (((1,), (1,)), ((), ()))


def dot_nt(a, b):
    return lax.dot_general(a, b, NT, preferred_element_type=jnp.float32)


def dot_nn(a, b):
    return jnp.dot(a, b, preferred_element_type=jnp.float32)


def xor(a, b, size):
    out, bit = 0, 1
    while bit < size:
        out = out + lax.rem(lax.div(a, bit) + b // bit, 2) * bit
        bit *= 2
    return out


def body(
    cfg,
    len_hbm,
    id_hbm,
    cos_hbm,
    sin_hbm,
    hidden_hbm,
    base_hbm,
    fresh_hbm,
    suffix_hbm,
    prompt_hbm,
    qd_hbm,
    qu_hbm,
    od_hbm,
    ou_hbm,
    att_ref,
    ada_ref,
    len_ref,
    id_ref,
    cos_ref,
    sin_ref,
    hidden_v,
    fresh_v,
    suffix_v,
    prompt_v,
    qd_v,
    qu_v,
    od_v,
    ou_v,
    local_sem,
    hid_in,
    base_in,
    info,
    rank_in,
    rank_out,
    tok_f32,
    fresh_f32,
    fresh_pad,
    base_f,
    cos_v,
    sin_v,
    ids_v,
    wide_f,
    wide_b,
    vt,
    vlt,
    bias_v,
    part_out,
    part_in,
    stat_out,
    stat_in,
    ork_out,
    ork_in,
    att_out,
    hid_s,
    hid_r,
    info_s,
    info_r,
    base_s,
    base_r,
    qu_s,
    qu_r,
    od_s,
    od_r,
    ou_s,
    ou_r,
    rank_s,
    rank_r,
    part_s,
    part_r,
    stat_s,
    stat_r,
    ork_s,
    ork_r,
    att_s,
    att_r,
):
    NS, NA, NH, R, T, KV, G, S, K = cfg
    D = HEAD_SIZE
    N = R * T
    C = G * D
    GT = KV * N
    QC = G * GT
    NK = NA * K
    bf16, f32 = jnp.bfloat16, jnp.float32
    seq, ada, head = lax.axis_index("seq"), lax.axis_index("adapter"), lax.axis_index("head")
    own_k, own_j = lax.rem(seq, KV), lax.div(seq, KV)
    scale = math.log2(math.e) / math.sqrt(D)
    shift = (S + T - 1).bit_length()

    def turn(me, d, size):
        return lax.rem(me + d, size)

    def place(ds, da, dh):
        return {
            "seq": turn(seq, ds, NS),
            "adapter": turn(ada, da, NA),
            "head": turn(head, dh, NH),
        }

    far = sorted(range(1, NS), key=lambda d: (-min(d, NS - d), d))
    others = [
        (ds, da, dh)
        for ds in far + [0]
        for da in range(NA - 1, -1, -1)
        for dh in range(NH)
        if (ds, da, dh) != (0, 0, 0)
    ]
    barrier = pltpu.get_barrier_semaphore()
    for other in others:
        pl.semaphore_signal(barrier, inc=1, device_id=place(*other), device_id_type=MESH)

    def head_at(where, i):
        return xor(lax.rem(where, KV), KV - 1 - i, KV)

    def columns(k, width):
        return pl.ds(pl.multiple_of(k * width, width), width)

    own_cols = columns(own_k, C)
    loads = []
    for i, (src, dst) in enumerate(
        (
            (len_hbm, len_ref),
            (id_hbm, id_ref),
            (hidden_hbm, hidden_v),
            (qd_hbm, qd_v),
            (cos_hbm, cos_ref),
            (sin_hbm, sin_ref),
            (prompt_hbm, prompt_v),
            (suffix_hbm, suffix_v),
            (fresh_hbm, fresh_v),
            (base_hbm, base_in.at[seq]),
            (qu_hbm.at[0], qu_v.at[ada]),
            (od_hbm.at[0, :, own_cols], od_v.at[ada]),
            (ou_hbm.at[0], ou_v.at[ada]),
        )
    ):
        load = pltpu.make_async_copy(src, dst, local_sem.at[i])
        load.start()
        loads.append(load)
    l_len, l_id, l_hid, l_qd, l_cos, l_sin = loads[:6]
    l_prompt, l_suffix, l_fresh, l_base, l_qu, l_od, l_ou = loads[6:]
    l_len.wait()
    l_id.wait()

    token = lax.broadcasted_iota(jnp.int32, (1, LANES), 1)
    code = jnp.zeros((1, LANES), jnp.int32)
    for r in range(R):
        code = jnp.where(lax.rem(token, R) == r, id_ref[0, r] * 2**shift + len_ref[r], code)
    info[seq] = (code + lax.div(token, R)).astype(f32)

    pl.semaphore_wait(barrier, len(others))

    sends = []

    def send(src, dst, s_sem, r_sem, device):
        copy = pltpu.make_async_remote_copy(
            src_ref=src,
            dst_ref=dst,
            send_sem=s_sem,
            recv_sem=r_sem,
            device_id=device,
            device_id_type=MESH,
        )
        copy.start()
        sends.append(copy)
        return copy

    hid = {}
    for d in range(1, NA):
        hid[d] = send(
            hidden_hbm, hid_in.at[d - 1], hid_s.at[d - 1], hid_r.at[d - 1], place(0, d, 0)
        )
    infos, bases, qus, ods, ous = {}, {}, {}, {}, {}
    for ds in far:
        infos[ds] = send(
            info.at[seq], info.at[seq], info_s.at[ds - 1], info_r.at[ds - 1], place(ds, 0, 0)
        )

    def base_cols(where, b):
        pair = xor(lax.div(lax.rem(where, KV), 2), KV // 2 - 1 - b, KV // 2)
        return columns(pair, 2 * C)

    def send_base(b):
        for u in range(NS - 1, 0, -1):
            to = xor(seq, u, NS)
            cols = base_cols(to, b)
            bases[(u, b)] = send(
                base_hbm.at[:, :, cols], base_in.at[seq, :, :, cols],
                base_s.at[u - 1, b], base_r.at[u - 1, b], {"seq": to},
            )

    def send_qu(i):
        cols = columns(head_at(seq, i), C)
        for d in range(1, NA):
            qus[(d, i)] = send(
                qu_hbm.at[0, :, cols], qu_v.at[ada, :, cols],
                qu_s.at[d - 1, i], qu_r.at[d - 1, i], place(0, d, 0),
            )

    parity = lax.rem(seq, 2)
    neighbour = {"seq": xor(seq, 1, NS)}
    ou_width = ou_hbm.shape[2] // (2 * OU_RELAYED + OU_DIRECT)

    def ou_cols(n, side):
        if n < OU_RELAYED:
            return columns(side * OU_RELAYED + n, ou_width)
        return columns(OU_RELAYED + n, ou_width)

    def source_slot(d):
        return lax.rem(ada + NA - d, NA)

    relays = {}

    def relay_qu(i):
        cols = columns(head_at(seq, i), C)
        for d in range(1, NA):
            qus[(d, i)].wait_recv()
            part = qu_v.at[source_slot(d), :, cols]
            qus[(d, i + 1)] = send(
                part, part, qu_s.at[d - 1, i + 1], qu_r.at[d - 1, i + 1], neighbour
            )

    def relay_ou(n):
        cols = ou_cols(n, parity)
        for d in range(1, NA):
            ous[(d, n)].wait_recv()
            part = ou_v.at[source_slot(d), :, cols]
            at = OU_RELAYED + OU_DIRECT + n
            relays[("ou", d, n)] = send(
                part, part, ou_s.at[d - 1, at], ou_r.at[d - 1, at], neighbour
            )

    turns = list(range(KV))
    half = KV // 2
    send_base(0)
    send_qu(0)

    packed = rank_in.shape[3]

    def rank_of(ref):
        for t in range(T):
            tok_f32[t * R : (t + 1) * R, :] = ref[t].astype(f32)
        part = dot_nt(tok_f32[...].astype(bf16), qd_v[0])
        return jnp.concatenate([part[p * packed : (p + 1) * packed] for p in range(LANES // K)], 1)

    ranks = {}

    def send_rank(src, ds, da, dh):
        ranks[(ds, da, dh)] = send(
            src, rank_in.at[seq, ada, head],
            rank_s.at[ds, da, dh], rank_r.at[ds, da, dh], place(ds, da, dh),
        )

    tok_f32[N:, :] = jnp.zeros((tok_f32.shape[0] - N, tok_f32.shape[1]), f32)
    l_hid.wait()
    l_qd.wait()
    rank_in[seq, ada, head] = rank_of(hidden_v)
    for ds in far + [0]:
        for dh in range(NH):
            if (ds, dh) != (0, 0):
                send_rank(rank_in.at[seq, ada, head], ds, 0, dh)

    l_prompt.wait()
    l_suffix.wait()
    l_fresh.wait()
    n_suf = R * S
    n_new = fresh_f32.shape[0]
    n_loc = n_suf + n_new
    for i in range(2):
        fresh_f32[...] = jnp.zeros_like(fresh_f32)
        for t in range(T):
            fresh_f32[t * R : (t + 1) * R, :] = fresh_v[i, t].astype(f32)
        fresh_pad[i] = fresh_f32[...].astype(bf16)

    def prepare(i):
        cols = columns(head_at(seq, i), D)
        vt[i, 0:D, :] = prompt_v[1, :, cols].astype(f32).T.astype(bf16)
        pad = lax.broadcasted_iota(jnp.int32, (vt.shape[1] - D, vt.shape[2]), 0)
        vt[i, D:, :] = jnp.where(pad == 0, 1.0, 0.0).astype(bf16)
        local = jnp.concatenate(
            [
                suffix_v[1, :, :, cols].reshape(n_suf, D),
                fresh_pad[1, :, cols],
                jnp.zeros((vlt.shape[2] - n_loc, D), bf16),
            ],
            0,
        )
        vlt[i, 0:D, :] = local.astype(f32).T.astype(bf16)
        pad = lax.broadcasted_iota(jnp.int32, (vlt.shape[1] - D, vlt.shape[2]), 0)
        vlt[i, D:, :] = jnp.where(pad == 0, 1.0, 0.0).astype(bf16)

    for i in turns[:half]:
        prepare(i)

    for d in range(1, NA):
        hid[d].wait_recv()
        rank_out[d - 1] = rank_of(hid_in.at[d - 1])
        for ds in far + [0]:
            for dh in range(NH):
                send_rank(rank_out.at[d - 1], ds, d, dh)
    def send_ou(n):
        cols = ou_cols(n, parity)
        for d in range(1, NA):
            ous[(d, n)] = send(
                ou_hbm.at[0, :, cols], ou_v.at[ada, :, cols],
                ou_s.at[d - 1, n], ou_r.at[d - 1, n], place(0, d, 0),
            )

    for i in range(2, KV, 2):
        send_qu(i)
    for b in range(1, half):
        send_base(b)
    for n in range(OU_RELAYED):
        send_ou(n)
    for i in range(3, KV, 2):
        send_qu(i)
    for d in range(1, NA):
        ods[d] = send(
            od_hbm.at[0, :, own_cols], od_v.at[ada], od_s.at[d - 1], od_r.at[d - 1],
            place(0, d, 0),
        )
    for n in range(OU_RELAYED, OU_RELAYED + OU_DIRECT):
        send_ou(n)

    key = lax.broadcasted_iota(jnp.int32, (n_loc, QC), 0)
    query = lax.rem(lax.broadcasted_iota(jnp.int32, (n_loc, QC), 1), GT)
    q_home, q_token = lax.div(query, N), lax.rem(query, N)
    q_step, q_row = lax.div(q_token, R), lax.rem(q_token, R)
    limit = jnp.zeros((n_loc, QC), jnp.int32)
    for r in range(R):
        limit = jnp.where(q_row == r, len_ref[r], limit)
    new = key - n_suf
    in_suffix = (lax.div(key, S) == q_row) & (lax.rem(key, S) < limit) & (new < 0)
    in_fresh = (lax.rem(new, R) == q_row) & (lax.div(new, R) <= q_step) & (new >= 0)
    bias_v[...] = jnp.where((q_home == own_k) & (in_suffix | in_fresh), 0.0, -1e30)

    for i in turns[half:]:
        prepare(i)

    landed = set()

    def convert(i):
        cols = columns(head_at(seq, i), C)
        for u in range(1, NS):
            if (u, i // 2) not in landed:
                bases[(u, i // 2)].wait_recv()
                landed.add((u, i // 2))
        for s in range(NS):
            for t in range(T):
                at = s * N + t * R
                base_f[i, at : at + R, :] = base_in[s, t, :, cols].astype(f32)

    l_base.wait()
    l_qu.wait()
    l_cos.wait()
    l_sin.wait()
    for ds in far:
        infos[ds].wait_recv()
    row = lax.broadcasted_iota(jnp.int32, (N, LANES), 0)
    diagonal = row == lax.broadcasted_iota(jnp.int32, (N, LANES), 1)
    for s in range(NS):
        code = jnp.sum(jnp.where(diagonal, info[s], 0.0), 1, keepdims=True)
        ids_v[s * N : (s + 1) * N, :] = jnp.broadcast_to(code.astype(jnp.int32), (N, LANES))
    codes = ids_v[...]
    position = jnp.bitwise_and(codes, 2**shift - 1)
    cos, sin = jnp.zeros(codes.shape, f32), jnp.zeros(codes.shape, f32)
    for p in range(S + T):
        cos = jnp.where(position == p, cos_ref[p : p + 1, :], cos)
        sin = jnp.where(position == p, sin_ref[p : p + 1, :], sin)
    cos_v[...] = cos
    sin_v[...] = sin
    ids_v[...] = jnp.right_shift(codes, shift)
    relay_qu(0)
    convert(0)

    def spread(x):
        return jnp.concatenate([x] * (NK // LANES), 1)

    def adapter_lanes(shape):
        return lax.div(lax.broadcasted_iota(jnp.int32, shape, 1), K)

    for copy in ranks.values():
        copy.wait_recv()
    for s in range(NS):
        ids = ids_v[s * N : (s + 1) * N, :]
        chosen = jnp.zeros((N, LANES), f32)
        for e in range(NA):
            whole = functools.reduce(jnp.add, [rank_in[s, e, h] for h in range(NH)])
            rows = [whole[:, p * K : (p + 1) * K] for p in range(LANES // K)]
            whole = jnp.concatenate([jnp.concatenate(rows, 0)] * (LANES // K), 1)[0:N]
            chosen = jnp.where(ids == e, whole, chosen)
        wide_f[s * N : (s + 1) * N, :] = spread(chosen)
    wide = wide_f[...]
    wide_b[...] = jnp.where(adapter_lanes(wide.shape) == spread(ids_v[...]), wide, 0.0).astype(bf16)

    def attend(u):
        i = KV - 1 - u % KV
        target = xor(seq, u, NS)
        k, j = lax.rem(target, KV), lax.div(target, KV)
        rows = pl.ds(pl.multiple_of(j * GT, GT), GT)
        cols = columns(k, D)
        delta = dot_nn(wide_b[rows, :], qu_v[:, :, columns(k, C)].reshape(NK, C))
        merged = base_f[i, rows, :] + delta
        cos, sin = cos_v[rows, :], sin_v[rows, :]
        turned = []
        for g in range(G):
            x = merged[:, g * D : (g + 1) * D]
            turned.append((x * cos + pltpu.roll(x, D // 2, 1) * sin).astype(bf16))
        query = jnp.concatenate(turned, 0)
        local_keys = jnp.concatenate(
            [suffix_v[0, :, :, cols].reshape(n_suf, D), fresh_pad[0, :, cols]], 0
        )
        far_scores = dot_nt(prompt_v[0, :, cols], query)
        shut = jnp.where(j == own_j, 0.0, -1e30)
        near_scores = dot_nt(local_keys, query) + (bias_v[...] + shut)
        peak = jnp.maximum(
            jnp.max(far_scores, 0, keepdims=True), jnp.max(near_scores, 0, keepdims=True)
        )
        far_weight = jnp.exp2((far_scores - peak) * scale).astype(bf16)
        near_weight = jnp.exp2((near_scores - peak) * scale).astype(bf16)
        near_weight = jnp.concatenate(
            [near_weight, jnp.zeros((vlt.shape[2] - n_loc, QC), bf16)], 0
        )
        both = dot_nn(vt[i], far_weight) + dot_nn(vlt[i], near_weight)
        return both[0:D], peak, both[D : D + 1]

    parts, stats = {}, {}
    units = [(j - 1) * KV + KV - 1 - i for j in range(NS // KV, 0, -1) for i in turns]
    for at, u in enumerate(units):
        i = KV - 1 - u % KV
        if at < KV:
            if i % 2:
                for d in range(1, NA):
                    qus[(d, i)].wait_recv()
            elif i > 0:
                for d in range(1, NA):
                    qus[(d, i)].wait_recv()
            if i > 0:
                convert(i)
        o, m, t = attend(u)
        if u > 0:
            part_out[u - 1] = o.astype(bf16)
            stat_out[u - 1, 0:1, :] = m
            stat_out[u - 1, 1:2, :] = t
            home = {"seq": xor(seq, u, NS)}
            parts[u] = send(
                part_out.at[u - 1], part_in.at[u - 1], part_s.at[u - 1], part_r.at[u - 1], home
            )
            stats[u] = send(
                stat_out.at[u - 1], stat_in.at[u - 1], stat_s.at[u - 1], stat_r.at[u - 1], home
            )
    for n in range(OU_RELAYED):
        relay_ou(n)
    whole = (o, m, t)
    for u in [u for u in units if u > 0]:
        parts[u].wait_recv()
        stats[u].wait_recv()
        o, m, t = part_in[u - 1].astype(f32), stat_in[u - 1, 0:1, :], stat_in[u - 1, 1:2, :]
        top = jnp.maximum(whole[1], m)
        one, two = jnp.exp2((whole[1] - top) * scale), jnp.exp2((m - top) * scale)
        whole = (whole[0] * one + o * two, top, whole[2] * one + t * two)
    turned = (whole[0] * (1.0 / whole[2])).T
    result = jnp.concatenate([turned[g * GT : (g + 1) * GT] for g in range(G)], 1)

    l_od.wait()
    for d in range(1, NA):
        ods[d].wait_recv()
    down = dot_nt(result.astype(bf16), od_v[...].reshape(NK, C))
    group_rows = pl.ds(pl.multiple_of(own_j * GT, GT), GT)
    down = jnp.where(adapter_lanes(down.shape) == spread(ids_v[group_rows, :]), down, 0.0)
    for jj in range(KV):
        ork_out[jj] = down[jj * N : (jj + 1) * N]
    orks, atts = {}, {}

    def home_of(e):
        jj = xor(own_k, e, KV)
        return jj, own_j * KV + jj

    for e in range(KV - 1, -1, -1):
        jj, where = home_of(e)
        for dh in range(NH):
            if (e, dh) != (0, 0):
                orks[(e, dh)] = send(
                    ork_out.at[jj], ork_in.at[own_k, head],
                    ork_s.at[e, dh], ork_r.at[e, dh],
                    {"seq": where, "head": turn(head, dh, NH)},
                )
    for jj in range(KV):
        for t in range(T):
            at = jj * N + t * R
            att_out[jj, t] = result[at : at + R].astype(bf16)
    for e in range(KV - 1, 0, -1):
        jj, where = home_of(e)
        atts[e] = send(
            att_out.at[jj], att_ref.at[:, :, own_cols], att_s.at[e - 1], att_r.at[e - 1],
            {"seq": where},
        )
    att_ref[:, :, own_cols] = att_out[own_k]

    ork_in[own_k, head] = ork_out[own_k]
    for copy in orks.values():
        copy.wait_recv()
    total = functools.reduce(
        jnp.add, [ork_in[k, h] for k in range(KV) for h in range(NH)]
    ).astype(bf16)
    l_ou.wait()

    def raise_up(cols):
        up = dot_nn(total, ou_v[:, :, cols].reshape(NK, ou_width))
        for t in range(T):
            ada_ref[t, :, cols] = up[t * R : (t + 1) * R].astype(bf16)

    for n in range(OU_RELAYED + OU_DIRECT):
        if n >= OU_RELAYED:
            for d in range(1, NA):
                ous[(d, n)].wait_recv()
        raise_up(ou_cols(n, parity))
    for n in range(OU_RELAYED):
        for d in range(1, NA):
            relays[("ou", d, n)].wait_recv()
        raise_up(ou_cols(n, 1 - parity))
    for copy in atts.values():
        copy.wait_recv()

    for copy in sends:
        copy.wait_send()


def finish(first, second, att_hbm, ada_hbm, sem):
    copies = [
        pltpu.make_async_copy(first, att_hbm, sem.at[0]),
        pltpu.make_async_copy(second, ada_hbm, sem.at[1]),
    ]
    for copy in copies:
        copy.start()
    for copy in copies:
        copy.wait()


def on_device(
    hidden,
    base_query_rows,
    fresh_key_value,
    suffix_key_value,
    suffix_length,
    row_adapter_index,
    prompt_key_value,
    query_down_factors,
    query_up_factors,
    output_down_factors,
    output_up_factors,
):
    NS, NA, NH = lax.axis_size("seq"), lax.axis_size("adapter"), lax.axis_size("head")
    hidden, base_query_rows = (x.transpose(1, 0, 2) for x in (hidden, base_query_rows))
    fresh_key_value = fresh_key_value.transpose(0, 2, 1, 3)
    T, R, width = hidden.shape
    D = HEAD_SIZE
    KV = prompt_key_value.shape[2] // D
    G = width // D // KV
    S = suffix_key_value.shape[2]
    keys = prompt_key_value.shape[1]
    N, C = R * T, G * D
    K = query_down_factors.shape[1]
    GT = KV * N
    QC, NK = G * GT, NA * K
    assert query_down_factors.shape[0] == 1
    assert width % (LANES * (2 * OU_RELAYED + OU_DIRECT)) == 0 and KV >= 2
    assert NS % KV == 0 and NS & (NS - 1) == 0 and KV & (KV - 1) == 0
    assert GT % 16 == 0 and LANES % K == 0 and NK % LANES == 0
    prompt_total = keys * NS
    positions = prompt_total + np.arange(S + T, dtype=np.float64)
    frequency = ROPE_BASE ** (-2.0 * np.arange(D // 2, dtype=np.float64) / D)
    angle = positions[:, None] * frequency[None, :]
    cos = np.concatenate([np.cos(angle), np.cos(angle)], 1).astype(np.float32)
    sin = np.concatenate([-np.sin(angle), np.sin(angle)], 1).astype(np.float32)
    bf16, f32 = jnp.bfloat16, jnp.float32
    dma = pltpu.SemaphoreType.DMA
    one = max(NA - 1, 1)
    far = max(NS - 1, 1)
    packed = -(-N // (8 * (LANES // K))) * 8
    n_new = -(-N // 16) * 16
    n_loc = R * S + n_new
    n_loc_pad = -(-n_loc // LANES) * LANES

    def like(x):
        return pltpu.VMEM(x.shape, x.dtype)

    scratch = [
        pltpu.SMEM((R,), jnp.int32),
        pltpu.SMEM((1, R), jnp.int32),
        pltpu.VMEM(cos.shape, f32),
        pltpu.VMEM(sin.shape, f32),
        like(hidden),
        like(fresh_key_value),
        like(suffix_key_value),
        like(prompt_key_value),
        like(query_down_factors),
        pltpu.VMEM((NA, K, width), bf16),
        pltpu.VMEM((NA, K, C), bf16),
        pltpu.VMEM((NA, K, width), bf16),
        dma((13,)),
        pltpu.VMEM((one,) + hidden.shape, bf16),
        pltpu.VMEM((NS,) + hidden.shape, bf16),
        pltpu.VMEM((NS, 1, LANES), f32),
        pltpu.VMEM((NS, NA, NH, packed, LANES), f32),
        pltpu.VMEM((one, packed, LANES), f32),
        pltpu.VMEM((packed * (LANES // K), width), f32),
        pltpu.VMEM((n_new, KV * D), f32),
        pltpu.VMEM((2, n_new, KV * D), bf16),
        pltpu.VMEM((KV, NS * N, C), f32),
        pltpu.VMEM((NS * N, D), f32),
        pltpu.VMEM((NS * N, D), f32),
        pltpu.VMEM((NS * N, LANES), jnp.int32),
        pltpu.VMEM((NS * N, NK), f32),
        pltpu.VMEM((NS * N, NK), bf16),
        pltpu.VMEM((KV, D + 16, keys), bf16),
        pltpu.VMEM((KV, D + 16, n_loc_pad), bf16),
        pltpu.VMEM((n_loc, QC), f32),
        pltpu.VMEM((far, D, QC), bf16),
        pltpu.VMEM((far, D, QC), bf16),
        pltpu.VMEM((far, 2, QC), f32),
        pltpu.VMEM((far, 2, QC), f32),
        pltpu.VMEM((KV, N, NK), f32),
        pltpu.VMEM((KV, NH, N, NK), f32),
        pltpu.VMEM((KV, T, R, C), bf16),
        dma((one,)), dma((one,)),
        dma((far,)), dma((far,)),
        dma((far, KV // 2)), dma((far, KV // 2)),
        dma((one, KV)), dma((one, KV)),
        dma((one,)), dma((one,)),
        dma((one, 2 * OU_RELAYED + OU_DIRECT)), dma((one, 2 * OU_RELAYED + OU_DIRECT)),
        dma((NS, NA, NH)), dma((NS, NA, NH)),
        dma((far,)), dma((far,)),
        dma((far,)), dma((far,)),
        dma((KV, NH)), dma((KV, NH)),
        dma((max(KV - 1, 1),)), dma((max(KV - 1, 1),)),
    ]
    vmem = pl.BlockSpec(memory_space=pltpu.VMEM)
    anywhere = pl.BlockSpec(memory_space=pl.ANY)
    results = pl.pallas_call(
        functools.partial(body, (NS, NA, NH, R, T, KV, G, S, K)),
        out_shape=(like(hidden), like(hidden)),
        in_specs=[anywhere] * 13,
        out_specs=(vmem, vmem),
        scratch_shapes=scratch,
        compiler_params=pltpu.CompilerParams(
            collective_id=0, has_side_effects=True, vmem_limit_bytes=56 * 2**20
        ),
        name="decode",
    )(
        suffix_length,
        row_adapter_index.transpose(1, 0),
        jnp.asarray(cos),
        jnp.asarray(sin),
        hidden,
        base_query_rows,
        fresh_key_value,
        suffix_key_value,
        prompt_key_value,
        query_down_factors,
        query_up_factors,
        output_down_factors,
        output_up_factors,
    )
    results = pl.pallas_call(
        finish,
        out_shape=tuple(jax.ShapeDtypeStruct(x.shape, bf16) for x in results),
        in_specs=[vmem, vmem],
        out_specs=(anywhere, anywhere),
        scratch_shapes=[dma((2,))],
        name="finish",
    )(*(pltpu.with_memory_space_constraint(x, pltpu.VMEM) for x in results))
    return tuple(x.transpose(1, 0, 2) for x in results)


def solution(mesh):
    rows = P(("groups", "seq", "adapter"), None, "head")
    caches = P(None, ("groups", "seq", "adapter"), None, "head")
    factors = P(("groups", "adapter"), None, "head")
    placed = (
        rows,
        rows,
        caches,
        caches,
        P(("groups", "seq", "adapter")),
        P(("groups", "seq", "adapter"), None),
        P(None, ("groups", "seq"), "head"),
        factors,
        factors,
        factors,
        factors,
    )
    return jax.shard_map(
        on_device, mesh=mesh, in_specs=placed, out_specs=(rows, rows), check_vma=False
    )
```

```python
import functools
import math

import jax
import jax.numpy as jnp
import numpy as np
from jax import lax
from jax.experimental import pallas as pl
from jax.experimental.pallas import tpu as pltpu
from jax.sharding import PartitionSpec as P

HEAD_SIZE = 128
ROPE_BASE = 1000000.0
LANES = 128
FOLD_TILES = 1
FOLD_BEFORE = 0
OU_RELAYED, OU_DIRECT = 2, 4
MESH = pl.DeviceIdType.MESH
NT = (((1,), (1,)), ((), ()))


def dot_nt(a, b):
    return lax.dot_general(a, b, NT, preferred_element_type=jnp.float32)


def dot_nn(a, b):
    return jnp.dot(a, b, preferred_element_type=jnp.float32)


def xor(a, b, size):
    out, bit = 0, 1
    while bit < size:
        out = out + lax.rem(lax.div(a, bit) + b // bit, 2) * bit
        bit *= 2
    return out


def body(
    cfg,
    len_hbm,
    id_hbm,
    cos_hbm,
    sin_hbm,
    hidden_hbm,
    base_hbm,
    fresh_hbm,
    suffix_hbm,
    prompt_hbm,
    qd_hbm,
    qu_hbm,
    od_hbm,
    ou_hbm,
    att_ref,
    ada_ref,
    len_ref,
    id_ref,
    cos_ref,
    sin_ref,
    hidden_v,
    fresh_v,
    suffix_v,
    prompt_v,
    qd_v,
    qu_v,
    od_v,
    ou_v,
    od_t,
    local_sem,
    hid_in,
    base_in,
    info,
    rank_in,
    rank_out,
    tok_f32,
    fresh_f32,
    fresh_pad,
    base_f,
    cos_v,
    sin_v,
    ids_v,
    wide_f,
    wide_b,
    vt,
    vlt,
    bias_v,
    part_out,
    part_in,
    stat_out,
    stat_in,
    fold_own,
    pre_in,
    pre_stat,
    fold_out,
    fold_stat,
    fold_in_o,
    fold_in_s,
    ork_out,
    ork_in,
    att_out,
    hid_s,
    hid_r,
    info_s,
    info_r,
    base_s,
    base_r,
    qu_s,
    qu_r,
    od_s,
    od_r,
    ou_s,
    ou_r,
    rank_s,
    rank_r,
    part_s,
    part_r,
    stat_s,
    stat_r,
    pre_s,
    pre_r,
    fold_s,
    fold_r,
    ork_s,
    ork_r,
    att_s,
    att_r,
):
    NS, NA, NH, R, T, KV, G, S, K = cfg
    D = HEAD_SIZE
    N = R * T
    C = G * D
    GT = KV * N
    QC = G * GT
    NK = NA * K
    bf16, f32 = jnp.bfloat16, jnp.float32
    seq, ada, head = lax.axis_index("seq"), lax.axis_index("adapter"), lax.axis_index("head")
    own_k, own_j = lax.rem(seq, KV), lax.div(seq, KV)
    scale = math.log2(math.e) / math.sqrt(D)
    shift = (S + T - 1).bit_length()

    def turn(me, d, size):
        return lax.rem(me + d, size)

    def place(ds, da, dh):
        return {
            "seq": turn(seq, ds, NS),
            "adapter": turn(ada, da, NA),
            "head": turn(head, dh, NH),
        }

    far = sorted(range(1, NS), key=lambda d: (-min(d, NS - d), d))
    others = [
        (ds, da, dh)
        for ds in far + [0]
        for da in range(NA - 1, -1, -1)
        for dh in range(NH)
        if (ds, da, dh) != (0, 0, 0)
    ]
    barrier = pltpu.get_barrier_semaphore()
    for other in others:
        pl.semaphore_signal(barrier, inc=1, device_id=place(*other), device_id_type=MESH)

    def head_at(where, i):
        return xor(lax.rem(where, KV), KV - 1 - i, KV)

    def columns(k, width):
        return pl.ds(pl.multiple_of(k * width, width), width)

    own_cols = columns(own_k, C)
    loads = []
    for i, (src, dst) in enumerate(
        (
            (len_hbm, len_ref),
            (id_hbm, id_ref),
            (hidden_hbm, hidden_v),
            (qd_hbm, qd_v),
            (cos_hbm, cos_ref),
            (sin_hbm, sin_ref),
            (prompt_hbm, prompt_v),
            (suffix_hbm, suffix_v),
            (fresh_hbm, fresh_v),
            (base_hbm, base_in.at[seq]),
            (qu_hbm.at[0], qu_v.at[ada]),
            (od_hbm.at[0, :, own_cols], od_v.at[ada]),
            (ou_hbm.at[0], ou_v.at[ada]),
        )
    ):
        load = pltpu.make_async_copy(src, dst, local_sem.at[i])
        load.start()
        loads.append(load)
    l_len, l_id, l_hid, l_qd, l_cos, l_sin = loads[:6]
    l_prompt, l_suffix, l_fresh, l_base, l_qu, l_od, l_ou = loads[6:]
    l_len.wait()
    l_id.wait()

    token = lax.broadcasted_iota(jnp.int32, (1, LANES), 1)
    code = jnp.zeros((1, LANES), jnp.int32)
    for r in range(R):
        code = jnp.where(lax.rem(token, R) == r, id_ref[0, r] * 2**shift + len_ref[r], code)
    info[seq] = (code + lax.div(token, R)).astype(f32)

    pl.semaphore_wait(barrier, len(others))

    sends = []

    def send(src, dst, s_sem, r_sem, device):
        copy = pltpu.make_async_remote_copy(
            src_ref=src,
            dst_ref=dst,
            send_sem=s_sem,
            recv_sem=r_sem,
            device_id=device,
            device_id_type=MESH,
        )
        copy.start()
        sends.append(copy)
        return copy

    hid = {}
    for d in range(1, NA):
        hid[d] = send(
            hidden_hbm, hid_in.at[d - 1], hid_s.at[d - 1], hid_r.at[d - 1], place(0, d, 0)
        )
    infos, bases, qus, ods, ous = {}, {}, {}, {}, {}
    for ds in far:
        infos[ds] = send(
            info.at[seq], info.at[seq], info_s.at[ds - 1], info_r.at[ds - 1], place(ds, 0, 0)
        )

    def base_cols(where, b):
        pair = xor(lax.div(lax.rem(where, KV), 2), KV // 2 - 1 - b, KV // 2)
        return columns(pair, 2 * C)

    def send_base(b):
        for u in range(NS - 1, 0, -1):
            to = xor(seq, u, NS)
            cols = base_cols(to, b)
            bases[(u, b)] = send(
                base_hbm.at[:, :, cols], base_in.at[seq, :, :, cols],
                base_s.at[u - 1, b], base_r.at[u - 1, b], {"seq": to},
            )

    def send_qu(i):
        cols = columns(head_at(seq, i), C)
        for d in range(1, NA):
            qus[(d, i)] = send(
                qu_hbm.at[0, :, cols], qu_v.at[ada, :, cols],
                qu_s.at[d - 1, i], qu_r.at[d - 1, i], place(0, d, 0),
            )

    parity = lax.rem(seq, 2)
    neighbour = {"seq": xor(seq, 1, NS)}
    ou_width = ou_hbm.shape[2] // (2 * OU_RELAYED + OU_DIRECT)

    def ou_cols(n, side):
        if n < OU_RELAYED:
            return columns(side * OU_RELAYED + n, ou_width)
        return columns(OU_RELAYED + n, ou_width)

    def source_slot(d):
        return lax.rem(ada + NA - d, NA)

    relays = {}

    def relay_qu(i):
        cols = columns(head_at(seq, i), C)
        for d in range(1, NA):
            qus[(d, i)].wait_recv()
            part = qu_v.at[source_slot(d), :, cols]
            qus[(d, i + 1)] = send(
                part, part, qu_s.at[d - 1, i + 1], qu_r.at[d - 1, i + 1], neighbour
            )

    def relay_ou(n):
        cols = ou_cols(n, parity)
        for d in range(1, NA):
            ous[(d, n)].wait_recv()
            part = ou_v.at[source_slot(d), :, cols]
            at = OU_RELAYED + OU_DIRECT + n
            relays[("ou", d, n)] = send(
                part, part, ou_s.at[d - 1, at], ou_r.at[d - 1, at], neighbour
            )

    turns = list(range(KV))
    half = KV // 2
    send_base(0)
    send_qu(0)

    packed = rank_in.shape[3]

    def rank_of(ref):
        for t in range(T):
            tok_f32[t * R : (t + 1) * R, :] = ref[t].astype(f32)
        part = dot_nt(tok_f32[...].astype(bf16), qd_v[0])
        return jnp.concatenate([part[p * packed : (p + 1) * packed] for p in range(LANES // K)], 1)

    ranks = {}

    def send_rank(src, ds, da, dh):
        ranks[(ds, da, dh)] = send(
            src, rank_in.at[seq, ada, head],
            rank_s.at[ds, da, dh], rank_r.at[ds, da, dh], place(ds, da, dh),
        )

    tok_f32[N:, :] = jnp.zeros((tok_f32.shape[0] - N, tok_f32.shape[1]), f32)
    l_hid.wait()
    l_qd.wait()
    rank_in[seq, ada, head] = rank_of(hidden_v)
    for ds in far + [0]:
        for dh in range(NH):
            if (ds, dh) != (0, 0):
                send_rank(rank_in.at[seq, ada, head], ds, 0, dh)

    l_prompt.wait()
    l_suffix.wait()
    l_fresh.wait()
    n_suf = R * S
    n_new = fresh_f32.shape[0]
    n_loc = n_suf + n_new
    for i in range(2):
        fresh_f32[...] = jnp.zeros_like(fresh_f32)
        for t in range(T):
            fresh_f32[t * R : (t + 1) * R, :] = fresh_v[i, t].astype(f32)
        fresh_pad[i] = fresh_f32[...].astype(bf16)

    def prepare(i):
        cols = columns(head_at(seq, i), D)
        vt[i, 0:D, :] = prompt_v[1, :, cols].astype(f32).T.astype(bf16)
        pad = lax.broadcasted_iota(jnp.int32, (vt.shape[1] - D, vt.shape[2]), 0)
        vt[i, D:, :] = jnp.where(pad == 0, 1.0, 0.0).astype(bf16)
        local = jnp.concatenate(
            [
                suffix_v[1, :, :, cols].reshape(n_suf, D),
                fresh_pad[1, :, cols],
                jnp.zeros((vlt.shape[2] - n_loc, D), bf16),
            ],
            0,
        )
        vlt[i, 0:D, :] = local.astype(f32).T.astype(bf16)
        pad = lax.broadcasted_iota(jnp.int32, (vlt.shape[1] - D, vlt.shape[2]), 0)
        vlt[i, D:, :] = jnp.where(pad == 0, 1.0, 0.0).astype(bf16)

    for i in turns[:half]:
        prepare(i)

    for d in range(1, NA):
        hid[d].wait_recv()
        rank_out[d - 1] = rank_of(hid_in.at[d - 1])
        for ds in far + [0]:
            for dh in range(NH):
                send_rank(rank_out.at[d - 1], ds, d, dh)
    def send_ou(n):
        cols = ou_cols(n, parity)
        for d in range(1, NA):
            ous[(d, n)] = send(
                ou_hbm.at[0, :, cols], ou_v.at[ada, :, cols],
                ou_s.at[d - 1, n], ou_r.at[d - 1, n], place(0, d, 0),
            )

    for i in range(2, KV, 2):
        send_qu(i)
    for b in range(1, half):
        send_base(b)
    for n in range(OU_RELAYED):
        send_ou(n)
    for i in range(3, KV, 2):
        send_qu(i)
    for d in range(1, NA):
        ods[d] = send(
            od_hbm.at[0, :, own_cols], od_v.at[ada], od_s.at[d - 1], od_r.at[d - 1],
            place(0, d, 0),
        )

    key = lax.broadcasted_iota(jnp.int32, (n_loc, QC), 0)
    query = lax.rem(lax.broadcasted_iota(jnp.int32, (n_loc, QC), 1), GT)
    q_home, q_token = lax.div(query, N), lax.rem(query, N)
    q_step, q_row = lax.div(q_token, R), lax.rem(q_token, R)
    limit = jnp.zeros((n_loc, QC), jnp.int32)
    for r in range(R):
        limit = jnp.where(q_row == r, len_ref[r], limit)
    new = key - n_suf
    in_suffix = (lax.div(key, S) == q_row) & (lax.rem(key, S) < limit) & (new < 0)
    in_fresh = (lax.rem(new, R) == q_row) & (lax.div(new, R) <= q_step) & (new >= 0)
    bias_v[...] = jnp.where((q_home == own_k) & (in_suffix | in_fresh), 0.0, -1e30)

    for i in turns[half:]:
        prepare(i)

    landed = set()

    def convert(i):
        cols = columns(head_at(seq, i), C)
        for u in range(1, NS):
            if (u, i // 2) not in landed:
                bases[(u, i // 2)].wait_recv()
                landed.add((u, i // 2))
        for s in range(NS):
            for t in range(T):
                at = s * N + t * R
                base_f[i, at : at + R, :] = base_in[s, t, :, cols].astype(f32)

    l_base.wait()
    l_qu.wait()
    l_cos.wait()
    l_sin.wait()
    for ds in far:
        infos[ds].wait_recv()
    row = lax.broadcasted_iota(jnp.int32, (N, LANES), 0)
    diagonal = row == lax.broadcasted_iota(jnp.int32, (N, LANES), 1)
    for s in range(NS):
        code = jnp.sum(jnp.where(diagonal, info[s], 0.0), 1, keepdims=True)
        ids_v[s * N : (s + 1) * N, :] = jnp.broadcast_to(code.astype(jnp.int32), (N, LANES))
    codes = ids_v[...]
    position = jnp.bitwise_and(codes, 2**shift - 1)
    cos, sin = jnp.zeros(codes.shape, f32), jnp.zeros(codes.shape, f32)
    for p in range(S + T):
        cos = jnp.where(position == p, cos_ref[p : p + 1, :], cos)
        sin = jnp.where(position == p, sin_ref[p : p + 1, :], sin)
    cos_v[...] = cos
    sin_v[...] = sin
    ids_v[...] = jnp.right_shift(codes, shift)
    relay_qu(0)
    convert(0)

    def spread(x):
        return jnp.concatenate([x] * (NK // LANES), 1)

    def adapter_lanes(shape):
        return lax.div(lax.broadcasted_iota(jnp.int32, shape, 1), K)

    for copy in ranks.values():
        copy.wait_recv()
    for s in range(NS):
        ids = ids_v[s * N : (s + 1) * N, :]
        chosen = jnp.zeros((N, LANES), f32)
        for e in range(NA):
            whole = functools.reduce(jnp.add, [rank_in[s, e, h] for h in range(NH)])
            rows = [whole[:, p * K : (p + 1) * K] for p in range(LANES // K)]
            whole = jnp.concatenate([jnp.concatenate(rows, 0)] * (LANES // K), 1)[0:N]
            chosen = jnp.where(ids == e, whole, chosen)
        wide_f[s * N : (s + 1) * N, :] = spread(chosen)
    wide = wide_f[...]
    wide_b[...] = jnp.where(adapter_lanes(wide.shape) == spread(ids_v[...]), wide, 0.0).astype(bf16)

    def attend(u):
        i = KV - 1 - u % KV
        target = xor(seq, u, NS)
        k, j = lax.rem(target, KV), lax.div(target, KV)
        rows = pl.ds(pl.multiple_of(j * GT, GT), GT)
        cols = columns(k, D)
        delta = dot_nn(wide_b[rows, :], qu_v[:, :, columns(k, C)].reshape(NK, C))
        merged = base_f[i, rows, :] + delta
        cos, sin = cos_v[rows, :], sin_v[rows, :]
        turned = []
        for g in range(G):
            x = merged[:, g * D : (g + 1) * D]
            turned.append((x * cos + pltpu.roll(x, D // 2, 1) * sin).astype(bf16))
        query = jnp.concatenate(turned, 0)
        local_keys = jnp.concatenate(
            [suffix_v[0, :, :, cols].reshape(n_suf, D), fresh_pad[0, :, cols]], 0
        )
        far_scores = dot_nt(prompt_v[0, :, cols], query)
        shut = jnp.where(j == own_j, 0.0, -1e30)
        near_scores = dot_nt(local_keys, query) + (bias_v[...] + shut)
        peak = jnp.maximum(
            jnp.max(far_scores, 0, keepdims=True), jnp.max(near_scores, 0, keepdims=True)
        )
        far_weight = jnp.exp2((far_scores - peak) * scale).astype(bf16)
        near_weight = jnp.exp2((near_scores - peak) * scale).astype(bf16)
        near_weight = jnp.concatenate(
            [near_weight, jnp.zeros((vlt.shape[2] - n_loc, QC), bf16)], 0
        )
        both = dot_nn(vt[i], far_weight) + dot_nn(vlt[i], near_weight)
        return both[0:D], peak, both[D : D + 1]

    A = LANES * FOLD_TILES
    fold, rest = slice(0, A), slice(A, QC)
    parts, stats, folds, pres = {}, {}, {}, {}

    def merge(pieces):
        whole = pieces[0]
        for o, m, t in pieces[1:]:
            top = jnp.maximum(whole[1], m)
            one, two = jnp.exp2((whole[1] - top) * scale), jnp.exp2((m - top) * scale)
            whole = (whole[0] * one + o * two, top, whole[2] * one + t * two)
        return whole

    def remote(src, dst, s_sem, r_sem, device):
        return pltpu.make_async_remote_copy(
            src_ref=src, dst_ref=dst, send_sem=s_sem, recv_sem=r_sem,
            device_id=device, device_id_type=MESH,
        )

    def nearer(u):
        return (xor(seq, u, NS) > seq).astype(jnp.int32) == parity

    def begin(copies):
        for copy in copies:
            copy.start()

    def fold_in(u):
        for copy in pres[u ^ 1]:
            copy.wait_recv()
        num, top, den = merge(
            [
                (fold_own[u - 2], stat_out[u - 1, 0:1, fold], stat_out[u - 1, 1:2, fold]),
                (pre_in[u - 2].astype(f32), pre_stat[u - 2, 0:1, :], pre_stat[u - 2, 1:2, :]),
            ]
        )
        fold_out[u - 2] = num.astype(bf16)
        fold_stat[u - 2, 0:1, :] = top
        fold_stat[u - 2, 1:2, :] = den
        begin(folds[u])

    def folding():
        for u in range(NS - 1, 1, -1):
            pl.when(nearer(u ^ 1))(functools.partial(fold_in, u ^ 1))

    units = [(j - 1) * KV + KV - 1 - i for j in range(NS // KV, 0, -1) for i in turns]
    for at, u in enumerate(units):
        i = KV - 1 - u % KV
        if at < KV:
            if i % 2:
                for d in range(1, NA):
                    qus[(d, i)].wait_recv()
            elif i > 0:
                for d in range(1, NA):
                    qus[(d, i)].wait_recv()
            if i > 0:
                convert(i)
        if at == 1:
            for n in range(OU_RELAYED, OU_RELAYED + OU_DIRECT):
                send_ou(n)
        if u == FOLD_BEFORE:
            folding()
        o, m, t = attend(u)
        if u > 0:
            part_out[u - 1] = o.astype(bf16)
            stat_out[u - 1, 0:1, :] = m
            stat_out[u - 1, 1:2, :] = t
            home = {"seq": xor(seq, u, NS)}
            if u > 1:
                fold_own[u - 2] = o[:, fold]
                slot, pair = (u ^ 1) - 2, u // 2 - 1
                pres[u] = (
                    remote(
                        part_out.at[u - 1, :, fold], pre_in.at[slot],
                        pre_s.at[slot, 0], pre_r.at[slot, 0], neighbour,
                    ),
                    remote(
                        stat_out.at[u - 1, :, fold], pre_stat.at[slot],
                        pre_s.at[slot, 1], pre_r.at[slot, 1], neighbour,
                    ),
                )
                folds[u] = (
                    remote(
                        fold_out.at[u - 2], fold_in_o.at[pair],
                        fold_s.at[pair, 0], fold_r.at[pair, 0], home,
                    ),
                    remote(
                        fold_stat.at[u - 2], fold_in_s.at[pair],
                        fold_s.at[pair, 1], fold_r.at[pair, 1], home,
                    ),
                )
                pl.when(jnp.logical_not(nearer(u)))(functools.partial(begin, pres[u]))
            cols = rest if u > 1 else slice(0, QC)
            parts[u] = send(
                part_out.at[u - 1, :, cols], part_in.at[u - 1, :, cols],
                part_s.at[u - 1], part_r.at[u - 1], home,
            )
            stats[u] = send(
                stat_out.at[u - 1, :, cols], stat_in.at[u - 1, :, cols],
                stat_s.at[u - 1], stat_r.at[u - 1], home,
            )
    for n in range(OU_RELAYED):
        relay_ou(n)
    l_od.wait()
    for d in range(1, NA):
        ods[d].wait_recv()
    for g in range(G):
        lanes = slice(g * D, (g + 1) * D)
        od_t[lanes, :] = od_v[:, :, lanes].reshape(NK, D).astype(f32).T.astype(bf16)
    near, beyond = [(o[:, fold], m[:, fold], t[:, fold])], [(o[:, rest], m[:, rest], t[:, rest])]

    def piece(values, at, where, cols):
        return values[where, :, cols].astype(f32), at[where, 0:1, cols], at[where, 1:2, cols]

    for u in [u for u in units if u > 0]:
        parts[u].wait_recv()
        stats[u].wait_recv()
        beyond.append(piece(part_in, stat_in, u - 1, rest))
        if u == 1:
            near.append(piece(part_in, stat_in, 0, fold))
    for u in range(2, NS, 2):
        for copy in folds[u]:
            copy.wait_recv()
        near.append(piece(fold_in_o, fold_in_s, u // 2 - 1, slice(0, A)))
    near, beyond = merge(near), merge(beyond)
    turned = jnp.concatenate([w[0] * (1.0 / w[2]) for w in (near, beyond)], 1).T
    result = jnp.concatenate([turned[g * GT : (g + 1) * GT] for g in range(G)], 1)

    down = dot_nn(result.astype(bf16), od_t[...])
    group_rows = pl.ds(pl.multiple_of(own_j * GT, GT), GT)
    down = jnp.where(adapter_lanes(down.shape) == spread(ids_v[group_rows, :]), down, 0.0)
    for jj in range(KV):
        ork_out[jj] = down[jj * N : (jj + 1) * N]
    orks, atts = {}, {}

    def home_of(e):
        jj = xor(own_k, e, KV)
        return jj, own_j * KV + jj

    for e in range(KV - 1, -1, -1):
        jj, where = home_of(e)
        for dh in range(NH):
            if (e, dh) != (0, 0):
                orks[(e, dh)] = send(
                    ork_out.at[jj], ork_in.at[own_k, head],
                    ork_s.at[e, dh], ork_r.at[e, dh],
                    {"seq": where, "head": turn(head, dh, NH)},
                )
    for jj in range(KV):
        for t in range(T):
            at = jj * N + t * R
            att_out[jj, t] = result[at : at + R].astype(bf16)
    for e in range(KV - 1, 0, -1):
        jj, where = home_of(e)
        atts[e] = send(
            att_out.at[jj], att_ref.at[:, :, own_cols], att_s.at[e - 1], att_r.at[e - 1],
            {"seq": where},
        )
    att_ref[:, :, own_cols] = att_out[own_k]

    ork_in[own_k, head] = ork_out[own_k]
    for copy in orks.values():
        copy.wait_recv()
    total = functools.reduce(
        jnp.add, [ork_in[k, h] for k in range(KV) for h in range(NH)]
    ).astype(bf16)
    l_ou.wait()

    def raise_up(cols):
        up = dot_nn(total, ou_v[:, :, cols].reshape(NK, ou_width))
        for t in range(T):
            ada_ref[t, :, cols] = up[t * R : (t + 1) * R].astype(bf16)

    for n in range(OU_RELAYED + OU_DIRECT):
        if n >= OU_RELAYED:
            for d in range(1, NA):
                ous[(d, n)].wait_recv()
        raise_up(ou_cols(n, parity))
    for n in range(OU_RELAYED):
        for d in range(1, NA):
            relays[("ou", d, n)].wait_recv()
        raise_up(ou_cols(n, 1 - parity))
    for copy in atts.values():
        copy.wait_recv()

    for copy in sends:
        copy.wait_send()

    def drain(copies):
        for copy in copies:
            copy.wait_send()

    for u in range(NS - 1, 1, -1):
        pl.when(jnp.logical_not(nearer(u)))(functools.partial(drain, pres[u]))
        pl.when(nearer(u))(functools.partial(drain, folds[u]))


def finish(first, second, att_hbm, ada_hbm, sem):
    copies = [
        pltpu.make_async_copy(first, att_hbm, sem.at[0]),
        pltpu.make_async_copy(second, ada_hbm, sem.at[1]),
    ]
    for copy in copies:
        copy.start()
    for copy in copies:
        copy.wait()


def on_device(
    hidden,
    base_query_rows,
    fresh_key_value,
    suffix_key_value,
    suffix_length,
    row_adapter_index,
    prompt_key_value,
    query_down_factors,
    query_up_factors,
    output_down_factors,
    output_up_factors,
):
    NS, NA, NH = lax.axis_size("seq"), lax.axis_size("adapter"), lax.axis_size("head")
    hidden, base_query_rows = (x.transpose(1, 0, 2) for x in (hidden, base_query_rows))
    fresh_key_value = fresh_key_value.transpose(0, 2, 1, 3)
    T, R, width = hidden.shape
    D = HEAD_SIZE
    KV = prompt_key_value.shape[2] // D
    G = width // D // KV
    S = suffix_key_value.shape[2]
    keys = prompt_key_value.shape[1]
    N, C = R * T, G * D
    K = query_down_factors.shape[1]
    GT = KV * N
    QC, NK = G * GT, NA * K
    assert query_down_factors.shape[0] == 1
    assert width % (LANES * (2 * OU_RELAYED + OU_DIRECT)) == 0 and KV >= 2
    assert NS % KV == 0 and NS & (NS - 1) == 0 and KV & (KV - 1) == 0
    assert GT % 16 == 0 and LANES % K == 0 and NK % LANES == 0
    prompt_total = keys * NS
    positions = prompt_total + np.arange(S + T, dtype=np.float64)
    frequency = ROPE_BASE ** (-2.0 * np.arange(D // 2, dtype=np.float64) / D)
    angle = positions[:, None] * frequency[None, :]
    cos = np.concatenate([np.cos(angle), np.cos(angle)], 1).astype(np.float32)
    sin = np.concatenate([-np.sin(angle), np.sin(angle)], 1).astype(np.float32)
    bf16, f32 = jnp.bfloat16, jnp.float32
    dma = pltpu.SemaphoreType.DMA
    one = max(NA - 1, 1)
    far, outer = NS - 1, NS - 2
    A = LANES * FOLD_TILES
    assert A < QC and NS >= 4
    packed = -(-N // (8 * (LANES // K))) * 8
    n_new = -(-N // 16) * 16
    n_loc = R * S + n_new
    n_loc_pad = -(-n_loc // LANES) * LANES

    def like(x):
        return pltpu.VMEM(x.shape, x.dtype)

    scratch = [
        pltpu.SMEM((R,), jnp.int32),
        pltpu.SMEM((1, R), jnp.int32),
        pltpu.VMEM(cos.shape, f32),
        pltpu.VMEM(sin.shape, f32),
        like(hidden),
        like(fresh_key_value),
        like(suffix_key_value),
        like(prompt_key_value),
        like(query_down_factors),
        pltpu.VMEM((NA, K, width), bf16),
        pltpu.VMEM((NA, K, C), bf16),
        pltpu.VMEM((NA, K, width), bf16),
        pltpu.VMEM((C, NK), bf16),
        dma((13,)),
        pltpu.VMEM((one,) + hidden.shape, bf16),
        pltpu.VMEM((NS,) + hidden.shape, bf16),
        pltpu.VMEM((NS, 1, LANES), f32),
        pltpu.VMEM((NS, NA, NH, packed, LANES), f32),
        pltpu.VMEM((one, packed, LANES), f32),
        pltpu.VMEM((packed * (LANES // K), width), f32),
        pltpu.VMEM((n_new, KV * D), f32),
        pltpu.VMEM((2, n_new, KV * D), bf16),
        pltpu.VMEM((KV, NS * N, C), f32),
        pltpu.VMEM((NS * N, D), f32),
        pltpu.VMEM((NS * N, D), f32),
        pltpu.VMEM((NS * N, LANES), jnp.int32),
        pltpu.VMEM((NS * N, NK), f32),
        pltpu.VMEM((NS * N, NK), bf16),
        pltpu.VMEM((KV, D + 16, keys), bf16),
        pltpu.VMEM((KV, D + 16, n_loc_pad), bf16),
        pltpu.VMEM((n_loc, QC), f32),
        pltpu.VMEM((far, D, QC), bf16),
        pltpu.VMEM((far, D, QC), bf16),
        pltpu.VMEM((far, 2, QC), f32),
        pltpu.VMEM((far, 2, QC), f32),
        pltpu.VMEM((outer, D, A), f32),
        pltpu.VMEM((outer, D, A), bf16),
        pltpu.VMEM((outer, 2, A), f32),
        pltpu.VMEM((outer, D, A), bf16),
        pltpu.VMEM((outer, 2, A), f32),
        pltpu.VMEM((outer // 2, D, A), bf16),
        pltpu.VMEM((outer // 2, 2, A), f32),
        pltpu.VMEM((KV, N, NK), f32),
        pltpu.VMEM((KV, NH, N, NK), f32),
        pltpu.VMEM((KV, T, R, C), bf16),
        dma((one,)), dma((one,)),
        dma((far,)), dma((far,)),
        dma((far, KV // 2)), dma((far, KV // 2)),
        dma((one, KV)), dma((one, KV)),
        dma((one,)), dma((one,)),
        dma((one, 2 * OU_RELAYED + OU_DIRECT)), dma((one, 2 * OU_RELAYED + OU_DIRECT)),
        dma((NS, NA, NH)), dma((NS, NA, NH)),
        dma((far,)), dma((far,)),
        dma((far,)), dma((far,)),
        dma((outer, 2)), dma((outer, 2)),
        dma((outer // 2, 2)), dma((outer // 2, 2)),
        dma((KV, NH)), dma((KV, NH)),
        dma((max(KV - 1, 1),)), dma((max(KV - 1, 1),)),
    ]
    vmem = pl.BlockSpec(memory_space=pltpu.VMEM)
    anywhere = pl.BlockSpec(memory_space=pl.ANY)
    results = pl.pallas_call(
        functools.partial(body, (NS, NA, NH, R, T, KV, G, S, K)),
        out_shape=(like(hidden), like(hidden)),
        in_specs=[anywhere] * 13,
        out_specs=(vmem, vmem),
        scratch_shapes=scratch,
        compiler_params=pltpu.CompilerParams(
            collective_id=0, has_side_effects=True, vmem_limit_bytes=56 * 2**20
        ),
        name="decode",
    )(
        suffix_length,
        row_adapter_index.transpose(1, 0),
        jnp.asarray(cos),
        jnp.asarray(sin),
        hidden,
        base_query_rows,
        fresh_key_value,
        suffix_key_value,
        prompt_key_value,
        query_down_factors,
        query_up_factors,
        output_down_factors,
        output_up_factors,
    )
    results = pl.pallas_call(
        finish,
        out_shape=tuple(jax.ShapeDtypeStruct(x.shape, bf16) for x in results),
        in_specs=[vmem, vmem],
        out_specs=(anywhere, anywhere),
        scratch_shapes=[dma((2,))],
        name="finish",
    )(*(pltpu.with_memory_space_constraint(x, pltpu.VMEM) for x in results))
    return tuple(x.transpose(1, 0, 2) for x in results)


def solution(mesh):
    rows = P(("groups", "seq", "adapter"), None, "head")
    caches = P(None, ("groups", "seq", "adapter"), None, "head")
    factors = P(("groups", "adapter"), None, "head")
    placed = (
        rows,
        rows,
        caches,
        caches,
        P(("groups", "seq", "adapter")),
        P(("groups", "seq", "adapter"), None),
        P(None, ("groups", "seq"), "head"),
        factors,
        factors,
        factors,
        factors,
    )
    return jax.shard_map(
        on_device, mesh=mesh, in_specs=placed, out_specs=(rows, rows), check_vma=False
    )
```

```python
import functools
import math

import jax
import jax.numpy as jnp
import numpy as np
from jax import lax
from jax.experimental import pallas as pl
from jax.experimental.pallas import tpu as pltpu
from jax.sharding import PartitionSpec as P

HEAD_SIZE = 128
ROPE_BASE = 1000000.0
LANES = 128
FOLD_TILES = 1
FOLD_BEFORE = 0
OU_RELAYED, OU_DIRECT = 1, 1
MESH = pl.DeviceIdType.MESH
NT = (((1,), (1,)), ((), ()))


def dot_nt(a, b):
    return lax.dot_general(a, b, NT, preferred_element_type=jnp.float32)


def dot_nn(a, b):
    return jnp.dot(a, b, preferred_element_type=jnp.float32)


def xor(a, b, size):
    out, bit = 0, 1
    while bit < size:
        out = out + lax.rem(lax.div(a, bit) + b // bit, 2) * bit
        bit *= 2
    return out


def body(
    cfg,
    len_hbm,
    id_hbm,
    cos_hbm,
    sin_hbm,
    hidden_hbm,
    base_hbm,
    fresh_hbm,
    suffix_hbm,
    prompt_hbm,
    qd_hbm,
    qu_hbm,
    od_hbm,
    ou_hbm,
    att_ref,
    ada_ref,
    len_ref,
    id_ref,
    cos_ref,
    sin_ref,
    hidden_v,
    fresh_v,
    suffix_v,
    prompt_v,
    qd_v,
    qu_v,
    od_v,
    ou_v,
    od_t,
    local_sem,
    hid_in,
    base_in,
    info,
    rank_in,
    rank_out,
    tok_f32,
    fresh_f32,
    fresh_pad,
    base_f,
    cos_v,
    sin_v,
    ids_v,
    wide_f,
    wide_b,
    vt,
    vlt,
    bias_v,
    part_out,
    part_in,
    stat_out,
    stat_in,
    fold_own,
    pre_in,
    pre_stat,
    fold_out,
    fold_stat,
    fold_in_o,
    fold_in_s,
    ork_out,
    ork_in,
    att_out,
    hid_s,
    hid_r,
    info_s,
    info_r,
    base_s,
    base_r,
    qu_s,
    qu_r,
    od_s,
    od_r,
    ou_s,
    ou_r,
    rank_s,
    rank_r,
    part_s,
    part_r,
    stat_s,
    stat_r,
    pre_s,
    pre_r,
    fold_s,
    fold_r,
    ork_s,
    ork_r,
    att_s,
    att_r,
):
    NS, NA, NH, R, T, KV, G, S, K = cfg
    D = HEAD_SIZE
    N = R * T
    C = G * D
    GT = KV * N
    QC = G * GT
    NK = NA * K
    bf16, f32 = jnp.bfloat16, jnp.float32
    seq, ada, head = lax.axis_index("seq"), lax.axis_index("adapter"), lax.axis_index("head")
    own_k, own_j = lax.rem(seq, KV), lax.div(seq, KV)
    scale = math.log2(math.e) / math.sqrt(D)
    shift = (S + T - 1).bit_length()

    def turn(me, d, size):
        return lax.rem(me + d, size)

    def place(ds, da, dh):
        return {
            "seq": turn(seq, ds, NS),
            "adapter": turn(ada, da, NA),
            "head": turn(head, dh, NH),
        }

    far = sorted(range(1, NS), key=lambda d: (-min(d, NS - d), d))
    others = [
        (ds, da, dh)
        for ds in far + [0]
        for da in range(NA - 1, -1, -1)
        for dh in range(NH)
        if (ds, da, dh) != (0, 0, 0)
    ]
    barrier = pltpu.get_barrier_semaphore()
    for other in others:
        pl.semaphore_signal(barrier, inc=1, device_id=place(*other), device_id_type=MESH)

    def head_at(where, i):
        return xor(lax.rem(where, KV), KV - 1 - i, KV)

    def columns(k, width):
        return pl.ds(pl.multiple_of(k * width, width), width)

    own_cols = columns(own_k, C)
    loads = []
    for i, (src, dst) in enumerate(
        (
            (len_hbm, len_ref),
            (id_hbm, id_ref),
            (hidden_hbm, hidden_v),
            (qd_hbm, qd_v),
            (cos_hbm, cos_ref),
            (sin_hbm, sin_ref),
            (prompt_hbm, prompt_v),
            (suffix_hbm, suffix_v),
            (fresh_hbm, fresh_v),
            (base_hbm, base_in.at[seq]),
            (qu_hbm.at[0], qu_v.at[ada]),
            (od_hbm.at[0, :, own_cols], od_v.at[ada]),
            (ou_hbm.at[0], ou_v.at[ada]),
        )
    ):
        load = pltpu.make_async_copy(src, dst, local_sem.at[i])
        load.start()
        loads.append(load)
    l_len, l_id, l_hid, l_qd, l_cos, l_sin = loads[:6]
    l_prompt, l_suffix, l_fresh, l_base, l_qu, l_od, l_ou = loads[6:]
    l_len.wait()
    l_id.wait()

    token = lax.broadcasted_iota(jnp.int32, (1, LANES), 1)
    code = jnp.zeros((1, LANES), jnp.int32)
    for r in range(R):
        code = jnp.where(lax.rem(token, R) == r, id_ref[0, r] * 2**shift + len_ref[r], code)
    info[seq] = (code + lax.div(token, R)).astype(f32)

    pl.semaphore_wait(barrier, len(others))

    sends = []

    def send(src, dst, s_sem, r_sem, device):
        copy = pltpu.make_async_remote_copy(
            src_ref=src,
            dst_ref=dst,
            send_sem=s_sem,
            recv_sem=r_sem,
            device_id=device,
            device_id_type=MESH,
        )
        copy.start()
        sends.append(copy)
        return copy

    hid = {}
    for d in range(1, NA):
        hid[d] = send(
            hidden_hbm, hid_in.at[d - 1], hid_s.at[d - 1], hid_r.at[d - 1], place(0, d, 0)
        )
    infos, bases, qus, ods, ous = {}, {}, {}, {}, {}
    for ds in far:
        infos[ds] = send(
            info.at[seq], info.at[seq], info_s.at[ds - 1], info_r.at[ds - 1], place(ds, 0, 0)
        )

    def base_cols(where, b):
        pair = xor(lax.div(lax.rem(where, KV), 2), KV // 2 - 1 - b, KV // 2)
        return columns(pair, 2 * C)

    def send_base(b):
        for u in range(NS - 1, 0, -1):
            to = xor(seq, u, NS)
            cols = base_cols(to, b)
            bases[(u, b)] = send(
                base_hbm.at[:, :, cols], base_in.at[seq, :, :, cols],
                base_s.at[u - 1, b], base_r.at[u - 1, b], {"seq": to},
            )

    def send_qu(i):
        cols = columns(head_at(seq, i), C)
        for d in range(1, NA):
            qus[(d, i)] = send(
                qu_hbm.at[0, :, cols], qu_v.at[ada, :, cols],
                qu_s.at[d - 1, i], qu_r.at[d - 1, i], place(0, d, 0),
            )

    parity = lax.rem(seq, 2)
    neighbour = {"seq": xor(seq, 1, NS)}
    quarter = ou_hbm.shape[2] // 4

    def ou_cols(n, side):
        if n < OU_RELAYED:
            return columns(side, quarter)
        return pl.ds(2 * quarter, 2 * quarter)

    def source_slot(d):
        return lax.rem(ada + NA - d, NA)

    relays = {}

    def relay_qu(i):
        cols = columns(head_at(seq, i), C)
        for d in range(1, NA):
            qus[(d, i)].wait_recv()
            part = qu_v.at[source_slot(d), :, cols]
            qus[(d, i + 1)] = send(
                part, part, qu_s.at[d - 1, i + 1], qu_r.at[d - 1, i + 1], neighbour
            )

    def relay_ou(n):
        cols = ou_cols(n, parity)
        for d in range(1, NA):
            ous[(d, n)].wait_recv()
            part = ou_v.at[source_slot(d), :, cols]
            at = OU_RELAYED + OU_DIRECT + n
            relays[("ou", d, n)] = send(
                part, part, ou_s.at[d - 1, at], ou_r.at[d - 1, at], neighbour
            )

    turns = list(range(KV))
    half = KV // 2
    send_base(0)
    send_qu(0)

    packed = rank_in.shape[3]

    def rank_of(ref):
        for t in range(T):
            tok_f32[t * R : (t + 1) * R, :] = ref[t].astype(f32)
        part = dot_nt(tok_f32[...].astype(bf16), qd_v[0])
        return jnp.concatenate([part[p * packed : (p + 1) * packed] for p in range(LANES // K)], 1)

    ranks = {}

    def send_rank(src, ds, da, dh):
        ranks[(ds, da, dh)] = send(
            src, rank_in.at[seq, ada, head],
            rank_s.at[ds, da, dh], rank_r.at[ds, da, dh], place(ds, da, dh),
        )

    l_hid.wait()
    l_qd.wait()
    rank_in[seq, ada, head] = rank_of(hidden_v)
    for ds in far + [0]:
        for dh in range(NH):
            if (ds, dh) != (0, 0):
                send_rank(rank_in.at[seq, ada, head], ds, 0, dh)

    l_prompt.wait()
    l_suffix.wait()
    l_fresh.wait()
    n_suf = R * S
    n_new = fresh_f32.shape[0]
    n_loc = n_suf + n_new
    for i in range(2):
        fresh_f32[...] = jnp.zeros_like(fresh_f32)
        for t in range(T):
            fresh_f32[t * R : (t + 1) * R, :] = fresh_v[i, t].astype(f32)
        fresh_pad[i] = fresh_f32[...].astype(bf16)

    def prepare(i):
        cols = columns(head_at(seq, i), D)
        vt[i, 0:D, :] = prompt_v[1, :, cols].astype(f32).T.astype(bf16)
        pad = lax.broadcasted_iota(jnp.int32, (vt.shape[1] - D, vt.shape[2]), 0)
        vt[i, D:, :] = jnp.where(pad == 0, 1.0, 0.0).astype(bf16)
        local = jnp.concatenate(
            [
                suffix_v[1, :, :, cols].reshape(n_suf, D),
                fresh_pad[1, :, cols],
                jnp.zeros((vlt.shape[2] - n_loc, D), bf16),
            ],
            0,
        )
        vlt[i, 0:D, :] = local.astype(f32).T.astype(bf16)
        pad = lax.broadcasted_iota(jnp.int32, (vlt.shape[1] - D, vlt.shape[2]), 0)
        vlt[i, D:, :] = jnp.where(pad == 0, 1.0, 0.0).astype(bf16)

    for i in turns[:half]:
        prepare(i)

    for d in range(1, NA):
        hid[d].wait_recv()
        rank_out[d - 1] = rank_of(hid_in.at[d - 1])
        for ds in far + [0]:
            for dh in range(NH):
                send_rank(rank_out.at[d - 1], ds, d, dh)
    def send_ou(n):
        cols = ou_cols(n, parity)
        for d in range(1, NA):
            ous[(d, n)] = send(
                ou_hbm.at[0, :, cols], ou_v.at[ada, :, cols],
                ou_s.at[d - 1, n], ou_r.at[d - 1, n], place(0, d, 0),
            )

    for i in range(2, KV, 2):
        send_qu(i)
    for b in range(1, half):
        send_base(b)
    for n in range(OU_RELAYED):
        send_ou(n)
    for i in range(3, KV, 2):
        send_qu(i)
    for d in range(1, NA):
        ods[d] = send(
            od_hbm.at[0, :, own_cols], od_v.at[ada], od_s.at[d - 1], od_r.at[d - 1],
            place(0, d, 0),
        )

    key = lax.broadcasted_iota(jnp.int32, (n_loc, QC), 0)
    query = lax.rem(lax.broadcasted_iota(jnp.int32, (n_loc, QC), 1), GT)
    q_home, q_token = lax.div(query, N), lax.rem(query, N)
    q_step, q_row = lax.div(q_token, R), lax.rem(q_token, R)
    limit = jnp.zeros((n_loc, QC), jnp.int32)
    for r in range(R):
        limit = jnp.where(q_row == r, len_ref[r], limit)
    new = key - n_suf
    in_suffix = (lax.div(key, S) == q_row) & (lax.rem(key, S) < limit) & (new < 0)
    in_fresh = (lax.rem(new, R) == q_row) & (lax.div(new, R) <= q_step) & (new >= 0)
    bias_v[...] = jnp.where((q_home == own_k) & (in_suffix | in_fresh), 0.0, -1e30)

    for i in turns[half:]:
        prepare(i)

    landed = set()

    def convert(i):
        cols = columns(head_at(seq, i), C)
        for u in range(1, NS):
            if (u, i // 2) not in landed:
                bases[(u, i // 2)].wait_recv()
                landed.add((u, i // 2))
        for s in range(NS):
            for t in range(T):
                at = s * N + t * R
                base_f[i, at : at + R, :] = base_in[s, t, :, cols].astype(f32)

    l_base.wait()
    l_qu.wait()
    l_cos.wait()
    l_sin.wait()
    for ds in far:
        infos[ds].wait_recv()
    row = lax.broadcasted_iota(jnp.int32, (N, LANES), 0)
    diagonal = row == lax.broadcasted_iota(jnp.int32, (N, LANES), 1)
    for s in range(NS):
        code = jnp.sum(jnp.where(diagonal, info[s], 0.0), 1, keepdims=True)
        ids_v[s * N : (s + 1) * N, :] = jnp.broadcast_to(code.astype(jnp.int32), (N, LANES))
    codes = ids_v[...]
    position = jnp.bitwise_and(codes, 2**shift - 1)
    cos, sin = jnp.zeros(codes.shape, f32), jnp.zeros(codes.shape, f32)
    for p in range(S + T):
        cos = jnp.where(position == p, cos_ref[p : p + 1, :], cos)
        sin = jnp.where(position == p, sin_ref[p : p + 1, :], sin)
    cos_v[...] = cos
    sin_v[...] = sin
    ids_v[...] = jnp.right_shift(codes, shift)
    relay_qu(0)
    convert(0)

    def spread(x):
        return jnp.concatenate([x] * (NK // LANES), 1)

    def adapter_lanes(shape):
        return lax.div(lax.broadcasted_iota(jnp.int32, shape, 1), K)

    for copy in ranks.values():
        copy.wait_recv()
    for s in range(NS):
        ids = ids_v[s * N : (s + 1) * N, :]
        chosen = jnp.zeros((N, LANES), f32)
        for e in range(NA):
            whole = functools.reduce(jnp.add, [rank_in[s, e, h] for h in range(NH)])
            rows = [whole[:, p * K : (p + 1) * K] for p in range(LANES // K)]
            whole = jnp.concatenate([jnp.concatenate(rows, 0)] * (LANES // K), 1)[0:N]
            chosen = jnp.where(ids == e, whole, chosen)
        wide_f[s * N : (s + 1) * N, :] = spread(chosen)
    wide = wide_f[...]
    wide_b[...] = jnp.where(adapter_lanes(wide.shape) == spread(ids_v[...]), wide, 0.0).astype(bf16)

    def attend(u):
        i = KV - 1 - u % KV
        target = xor(seq, u, NS)
        k, j = lax.rem(target, KV), lax.div(target, KV)
        rows = pl.ds(pl.multiple_of(j * GT, GT), GT)
        cols = columns(k, D)
        delta = dot_nn(wide_b[rows, :], qu_v[:, :, columns(k, C)].reshape(NK, C))
        merged = base_f[i, rows, :] + delta
        cos, sin = cos_v[rows, :], sin_v[rows, :]
        turned = []
        for g in range(G):
            x = merged[:, g * D : (g + 1) * D]
            turned.append((x * cos + pltpu.roll(x, D // 2, 1) * sin).astype(bf16))
        query = jnp.concatenate(turned, 0)
        local_keys = jnp.concatenate(
            [suffix_v[0, :, :, cols].reshape(n_suf, D), fresh_pad[0, :, cols]], 0
        )
        far_scores = dot_nt(prompt_v[0, :, cols], query)
        shut = jnp.where(j == own_j, 0.0, -1e30)
        near_scores = dot_nt(local_keys, query) + (bias_v[...] + shut)
        peak = jnp.maximum(
            jnp.max(far_scores, 0, keepdims=True), jnp.max(near_scores, 0, keepdims=True)
        )
        far_weight = jnp.exp2((far_scores - peak) * scale).astype(bf16)
        near_weight = jnp.exp2((near_scores - peak) * scale).astype(bf16)
        near_weight = jnp.concatenate(
            [near_weight, jnp.zeros((vlt.shape[2] - n_loc, QC), bf16)], 0
        )
        both = dot_nn(vt[i], far_weight) + dot_nn(vlt[i], near_weight)
        return both[0:D], peak, both[D : D + 1]

    A = LANES * FOLD_TILES
    fold, rest = slice(0, A), slice(A, QC)
    parts, stats, folds, pres = {}, {}, {}, {}

    def merge(pieces):
        whole = pieces[0]
        for o, m, t in pieces[1:]:
            top = jnp.maximum(whole[1], m)
            one, two = jnp.exp2((whole[1] - top) * scale), jnp.exp2((m - top) * scale)
            whole = (whole[0] * one + o * two, top, whole[2] * one + t * two)
        return whole

    def remote(src, dst, s_sem, r_sem, device):
        return pltpu.make_async_remote_copy(
            src_ref=src, dst_ref=dst, send_sem=s_sem, recv_sem=r_sem,
            device_id=device, device_id_type=MESH,
        )

    def nearer(u):
        return (xor(seq, u, NS) > seq).astype(jnp.int32) == parity

    def begin(copies):
        for copy in copies:
            copy.start()

    def fold_in(u):
        for copy in pres[u ^ 1]:
            copy.wait_recv()
        num, top, den = merge(
            [
                (fold_own[u - 2], stat_out[u - 1, 0:1, fold], stat_out[u - 1, 1:2, fold]),
                (pre_in[u - 2].astype(f32), pre_stat[u - 2, 0:1, :], pre_stat[u - 2, 1:2, :]),
            ]
        )
        fold_out[u - 2] = num.astype(bf16)
        fold_stat[u - 2, 0:1, :] = top
        fold_stat[u - 2, 1:2, :] = den
        begin(folds[u])

    def folding():
        for u in range(NS - 1, 1, -1):
            pl.when(nearer(u ^ 1))(functools.partial(fold_in, u ^ 1))

    units = [(j - 1) * KV + KV - 1 - i for j in range(NS // KV, 0, -1) for i in turns]
    for at, u in enumerate(units):
        i = KV - 1 - u % KV
        if at < KV:
            if i % 2:
                for d in range(1, NA):
                    qus[(d, i)].wait_recv()
            elif i > 0:
                for d in range(1, NA):
                    qus[(d, i)].wait_recv()
            if i > 0:
                convert(i)
        if at == 2:
            for n in range(OU_RELAYED, OU_RELAYED + OU_DIRECT):
                send_ou(n)
        if u == FOLD_BEFORE:
            folding()
        o, m, t = attend(u)
        if u > 0:
            part_out[u - 1] = o.astype(bf16)
            stat_out[u - 1, 0:1, :] = m
            stat_out[u - 1, 1:2, :] = t
            home = {"seq": xor(seq, u, NS)}
            if u > 1:
                fold_own[u - 2] = o[:, fold]
                slot, pair = (u ^ 1) - 2, u // 2 - 1
                pres[u] = (
                    remote(
                        part_out.at[u - 1, :, fold], pre_in.at[slot],
                        pre_s.at[slot, 0], pre_r.at[slot, 0], neighbour,
                    ),
                    remote(
                        stat_out.at[u - 1, :, fold], pre_stat.at[slot],
                        pre_s.at[slot, 1], pre_r.at[slot, 1], neighbour,
                    ),
                )
                folds[u] = (
                    remote(
                        fold_out.at[u - 2], fold_in_o.at[pair],
                        fold_s.at[pair, 0], fold_r.at[pair, 0], home,
                    ),
                    remote(
                        fold_stat.at[u - 2], fold_in_s.at[pair],
                        fold_s.at[pair, 1], fold_r.at[pair, 1], home,
                    ),
                )
                pl.when(jnp.logical_not(nearer(u)))(functools.partial(begin, pres[u]))
            cols = rest if u > 1 else slice(0, QC)
            parts[u] = send(
                part_out.at[u - 1, :, cols], part_in.at[u - 1, :, cols],
                part_s.at[u - 1], part_r.at[u - 1], home,
            )
            stats[u] = send(
                stat_out.at[u - 1, :, cols], stat_in.at[u - 1, :, cols],
                stat_s.at[u - 1], stat_r.at[u - 1], home,
            )
    for n in range(OU_RELAYED):
        relay_ou(n)
    l_od.wait()
    for d in range(1, NA):
        ods[d].wait_recv()
    for g in range(G):
        lanes = slice(g * D, (g + 1) * D)
        od_t[lanes, :] = od_v[:, :, lanes].reshape(NK, D).astype(f32).T.astype(bf16)
    near, beyond = [(o[:, fold], m[:, fold], t[:, fold])], [(o[:, rest], m[:, rest], t[:, rest])]

    def piece(values, at, where, cols):
        return values[where, :, cols].astype(f32), at[where, 0:1, cols], at[where, 1:2, cols]

    for u in [u for u in units if u > 0]:
        parts[u].wait_recv()
        stats[u].wait_recv()
        beyond.append(piece(part_in, stat_in, u - 1, rest))
        if u == 1:
            near.append(piece(part_in, stat_in, 0, fold))
    for u in range(2, NS, 2):
        for copy in folds[u]:
            copy.wait_recv()
        near.append(piece(fold_in_o, fold_in_s, u // 2 - 1, slice(0, A)))
    near, beyond = merge(near), merge(beyond)
    turned = jnp.concatenate([w[0] * (1.0 / w[2]) for w in (near, beyond)], 1).T
    result = jnp.concatenate([turned[g * GT : (g + 1) * GT] for g in range(G)], 1)

    down = dot_nn(result.astype(bf16), od_t[...])
    group_rows = pl.ds(pl.multiple_of(own_j * GT, GT), GT)
    down = jnp.where(adapter_lanes(down.shape) == spread(ids_v[group_rows, :]), down, 0.0)
    for jj in range(KV):
        ork_out[jj] = down[jj * N : (jj + 1) * N]
    orks, atts = {}, {}

    def home_of(e):
        jj = xor(own_k, e, KV)
        return jj, own_j * KV + jj

    for e in range(KV - 1, -1, -1):
        jj, where = home_of(e)
        for dh in range(NH):
            if (e, dh) != (0, 0):
                orks[(e, dh)] = send(
                    ork_out.at[jj], ork_in.at[own_k, head],
                    ork_s.at[e, dh], ork_r.at[e, dh],
                    {"seq": where, "head": turn(head, dh, NH)},
                )
    for jj in range(KV):
        for t in range(T):
            at = jj * N + t * R
            att_out[jj, t] = result[at : at + R].astype(bf16)
    for e in range(KV - 1, 0, -1):
        jj, where = home_of(e)
        atts[e] = send(
            att_out.at[jj], att_ref.at[:, :, own_cols], att_s.at[e - 1], att_r.at[e - 1],
            {"seq": where},
        )
    att_ref[:, :, own_cols] = att_out[own_k]

    ork_in[own_k, head] = ork_out[own_k]
    for copy in orks.values():
        copy.wait_recv()
    total = functools.reduce(
        jnp.add, [ork_in[k, h] for k in range(KV) for h in range(NH)]
    ).astype(bf16)
    l_ou.wait()

    def raise_up(cols):
        up = dot_nn(total, ou_v[:, :, cols].reshape(NK, cols.size))
        for t in range(T):
            ada_ref[t, :, cols] = up[t * R : (t + 1) * R].astype(bf16)

    for n in range(OU_RELAYED + OU_DIRECT):
        if n >= OU_RELAYED:
            for d in range(1, NA):
                ous[(d, n)].wait_recv()
        raise_up(ou_cols(n, parity))
    for n in range(OU_RELAYED):
        for d in range(1, NA):
            relays[("ou", d, n)].wait_recv()
        raise_up(ou_cols(n, 1 - parity))
    for copy in atts.values():
        copy.wait_recv()

    for copy in sends:
        copy.wait_send()

    def drain(copies):
        for copy in copies:
            copy.wait_send()

    for u in range(NS - 1, 1, -1):
        pl.when(jnp.logical_not(nearer(u)))(functools.partial(drain, pres[u]))
        pl.when(nearer(u))(functools.partial(drain, folds[u]))


def finish(first, second, att_hbm, ada_hbm, sem):
    copies = [
        pltpu.make_async_copy(first, att_hbm, sem.at[0]),
        pltpu.make_async_copy(second, ada_hbm, sem.at[1]),
    ]
    for copy in copies:
        copy.start()
    for copy in copies:
        copy.wait()


def on_device(
    hidden,
    base_query_rows,
    fresh_key_value,
    suffix_key_value,
    suffix_length,
    row_adapter_index,
    prompt_key_value,
    query_down_factors,
    query_up_factors,
    output_down_factors,
    output_up_factors,
):
    NS, NA, NH = lax.axis_size("seq"), lax.axis_size("adapter"), lax.axis_size("head")
    hidden, base_query_rows = (x.transpose(1, 0, 2) for x in (hidden, base_query_rows))
    fresh_key_value = fresh_key_value.transpose(0, 2, 1, 3)
    T, R, width = hidden.shape
    D = HEAD_SIZE
    KV = prompt_key_value.shape[2] // D
    G = width // D // KV
    S = suffix_key_value.shape[2]
    keys = prompt_key_value.shape[1]
    N, C = R * T, G * D
    K = query_down_factors.shape[1]
    GT = KV * N
    QC, NK = G * GT, NA * K
    assert query_down_factors.shape[0] == 1
    assert width % (LANES * 4) == 0 and KV >= 2
    assert NS % KV == 0 and NS & (NS - 1) == 0 and KV & (KV - 1) == 0
    assert GT % 16 == 0 and LANES % K == 0 and NK % LANES == 0
    prompt_total = keys * NS
    positions = prompt_total + np.arange(S + T, dtype=np.float64)
    frequency = ROPE_BASE ** (-2.0 * np.arange(D // 2, dtype=np.float64) / D)
    angle = positions[:, None] * frequency[None, :]
    cos = np.concatenate([np.cos(angle), np.cos(angle)], 1).astype(np.float32)
    sin = np.concatenate([-np.sin(angle), np.sin(angle)], 1).astype(np.float32)
    bf16, f32 = jnp.bfloat16, jnp.float32
    dma = pltpu.SemaphoreType.DMA
    one = max(NA - 1, 1)
    far, outer = NS - 1, NS - 2
    A = LANES * FOLD_TILES
    assert A < QC and NS >= 4
    packed = N // (LANES // K)
    assert N % (LANES // K) == 0
    n_new = -(-N // 16) * 16
    n_loc = R * S + n_new
    n_loc_pad = -(-n_loc // LANES) * LANES

    def like(x):
        return pltpu.VMEM(x.shape, x.dtype)

    scratch = [
        pltpu.SMEM((R,), jnp.int32),
        pltpu.SMEM((1, R), jnp.int32),
        pltpu.VMEM(cos.shape, f32),
        pltpu.VMEM(sin.shape, f32),
        like(hidden),
        like(fresh_key_value),
        like(suffix_key_value),
        like(prompt_key_value),
        like(query_down_factors),
        pltpu.VMEM((NA, K, width), bf16),
        pltpu.VMEM((NA, K, C), bf16),
        pltpu.VMEM((NA, K, width), bf16),
        pltpu.VMEM((C, NK), bf16),
        dma((13,)),
        pltpu.VMEM((one,) + hidden.shape, bf16),
        pltpu.VMEM((NS,) + hidden.shape, bf16),
        pltpu.VMEM((NS, 1, LANES), f32),
        pltpu.VMEM((NS, NA, NH, packed, LANES), f32),
        pltpu.VMEM((one, packed, LANES), f32),
        pltpu.VMEM((packed * (LANES // K), width), f32),
        pltpu.VMEM((n_new, KV * D), f32),
        pltpu.VMEM((2, n_new, KV * D), bf16),
        pltpu.VMEM((KV, NS * N, C), f32),
        pltpu.VMEM((NS * N, D), f32),
        pltpu.VMEM((NS * N, D), f32),
        pltpu.VMEM((NS * N, LANES), jnp.int32),
        pltpu.VMEM((NS * N, NK), f32),
        pltpu.VMEM((NS * N, NK), bf16),
        pltpu.VMEM((KV, D + 16, keys), bf16),
        pltpu.VMEM((KV, D + 16, n_loc_pad), bf16),
        pltpu.VMEM((n_loc, QC), f32),
        pltpu.VMEM((far, D, QC), bf16),
        pltpu.VMEM((far, D, QC), bf16),
        pltpu.VMEM((far, 2, QC), f32),
        pltpu.VMEM((far, 2, QC), f32),
        pltpu.VMEM((outer, D, A), f32),
        pltpu.VMEM((outer, D, A), bf16),
        pltpu.VMEM((outer, 2, A), f32),
        pltpu.VMEM((outer, D, A), bf16),
        pltpu.VMEM((outer, 2, A), f32),
        pltpu.VMEM((outer // 2, D, A), bf16),
        pltpu.VMEM((outer // 2, 2, A), f32),
        pltpu.VMEM((KV, N, NK), f32),
        pltpu.VMEM((KV, NH, N, NK), f32),
        pltpu.VMEM((KV, T, R, C), bf16),
        dma((one,)), dma((one,)),
        dma((far,)), dma((far,)),
        dma((far, KV // 2)), dma((far, KV // 2)),
        dma((one, KV)), dma((one, KV)),
        dma((one,)), dma((one,)),
        dma((one, 2 * OU_RELAYED + OU_DIRECT)), dma((one, 2 * OU_RELAYED + OU_DIRECT)),
        dma((NS, NA, NH)), dma((NS, NA, NH)),
        dma((far,)), dma((far,)),
        dma((far,)), dma((far,)),
        dma((outer, 2)), dma((outer, 2)),
        dma((outer // 2, 2)), dma((outer // 2, 2)),
        dma((KV, NH)), dma((KV, NH)),
        dma((max(KV - 1, 1),)), dma((max(KV - 1, 1),)),
    ]
    vmem = pl.BlockSpec(memory_space=pltpu.VMEM)
    anywhere = pl.BlockSpec(memory_space=pl.ANY)
    results = pl.pallas_call(
        functools.partial(body, (NS, NA, NH, R, T, KV, G, S, K)),
        out_shape=(like(hidden), like(hidden)),
        in_specs=[anywhere] * 13,
        out_specs=(vmem, vmem),
        scratch_shapes=scratch,
        compiler_params=pltpu.CompilerParams(
            collective_id=0, has_side_effects=True, vmem_limit_bytes=56 * 2**20
        ),
        name="decode",
    )(
        suffix_length,
        row_adapter_index.transpose(1, 0),
        jnp.asarray(cos),
        jnp.asarray(sin),
        hidden,
        base_query_rows,
        fresh_key_value,
        suffix_key_value,
        prompt_key_value,
        query_down_factors,
        query_up_factors,
        output_down_factors,
        output_up_factors,
    )
    results = pl.pallas_call(
        finish,
        out_shape=tuple(jax.ShapeDtypeStruct(x.shape, bf16) for x in results),
        in_specs=[vmem, vmem],
        out_specs=(anywhere, anywhere),
        scratch_shapes=[dma((2,))],
        name="finish",
    )(*(pltpu.with_memory_space_constraint(x, pltpu.VMEM) for x in results))
    return tuple(x.transpose(1, 0, 2) for x in results)


def solution(mesh):
    rows = P(("groups", "seq", "adapter"), None, "head")
    caches = P(None, ("groups", "seq", "adapter"), None, "head")
    factors = P(("groups", "adapter"), None, "head")
    placed = (
        rows,
        rows,
        caches,
        caches,
        P(("groups", "seq", "adapter")),
        P(("groups", "seq", "adapter"), None),
        P(None, ("groups", "seq"), "head"),
        factors,
        factors,
        factors,
        factors,
    )
    return jax.shard_map(
        on_device, mesh=mesh, in_specs=placed, out_specs=(rows, rows), check_vma=False
    )
```

```python
import functools
import math

import jax
import jax.numpy as jnp
import numpy as np
from jax import lax
from jax.experimental import pallas as pl
from jax.experimental.pallas import tpu as pltpu
from jax.sharding import PartitionSpec as P

HEAD_SIZE = 128
ROPE_BASE = 1000000.0
LANES = 128
FOLD_TILES = 1
FOLD_BEFORE = 0
OU_RELAYED, OU_DIRECT = 1, 1
MESH = pl.DeviceIdType.MESH
NT = (((1,), (1,)), ((), ()))


def dot_nt(a, b):
    return lax.dot_general(a, b, NT, preferred_element_type=jnp.float32)


def dot_nn(a, b):
    return jnp.dot(a, b, preferred_element_type=jnp.float32)


def xor(a, b, size):
    out, bit = 0, 1
    while bit < size:
        out = out + lax.rem(lax.div(a, bit) + b // bit, 2) * bit
        bit *= 2
    return out


def body(
    cfg,
    len_hbm,
    id_hbm,
    cos_hbm,
    sin_hbm,
    hidden_hbm,
    base_hbm,
    fresh_hbm,
    suffix_hbm,
    prompt_hbm,
    qd_hbm,
    qu_hbm,
    od_hbm,
    ou_hbm,
    att_ref,
    ada_ref,
    len_ref,
    id_ref,
    cos_ref,
    sin_ref,
    hidden_v,
    fresh_v,
    suffix_v,
    prompt_v,
    qd_v,
    qu_v,
    od_v,
    ou_v,
    od_t,
    local_sem,
    hid_in,
    base_in,
    info,
    rank_in,
    rank_out,
    tok_f32,
    fresh_f32,
    fresh_pad,
    base_f,
    cos_v,
    sin_v,
    ids_v,
    wide_f,
    wide_b,
    vt,
    vlt,
    bias_v,
    part_out,
    part_in,
    stat_out,
    stat_in,
    fold_own,
    pre_in,
    pre_stat,
    fold_out,
    fold_stat,
    fold_in_o,
    fold_in_s,
    ork_out,
    ork_in,
    att_out,
    hid_s,
    hid_r,
    info_s,
    info_r,
    base_s,
    base_r,
    qu_s,
    qu_r,
    od_s,
    od_r,
    ou_s,
    ou_r,
    rank_s,
    rank_r,
    part_s,
    part_r,
    stat_s,
    stat_r,
    pre_s,
    pre_r,
    fold_s,
    fold_r,
    ork_s,
    ork_r,
    att_s,
    att_r,
):
    NS, NA, NH, R, T, KV, G, S, K = cfg
    D = HEAD_SIZE
    N = R * T
    C = G * D
    GT = KV * N
    QC = G * GT
    NK = NA * K
    bf16, f32 = jnp.bfloat16, jnp.float32
    seq, ada, head = lax.axis_index("seq"), lax.axis_index("adapter"), lax.axis_index("head")
    own_k, own_j = lax.rem(seq, KV), lax.div(seq, KV)
    scale = math.log2(math.e) / math.sqrt(D)
    shift = (S + T - 1).bit_length()

    def turn(me, d, size):
        return lax.rem(me + d, size)

    def place(ds, da, dh):
        return {
            "seq": turn(seq, ds, NS),
            "adapter": turn(ada, da, NA),
            "head": turn(head, dh, NH),
        }

    far = sorted(range(1, NS), key=lambda d: (-min(d, NS - d), d))
    others = [
        (ds, da, dh)
        for ds in far + [0]
        for da in range(NA - 1, -1, -1)
        for dh in range(NH)
        if (ds, da, dh) != (0, 0, 0)
    ]
    barrier = pltpu.get_barrier_semaphore()
    for other in others:
        pl.semaphore_signal(barrier, inc=1, device_id=place(*other), device_id_type=MESH)

    def head_at(where, i):
        return xor(lax.rem(where, KV), KV - 1 - i, KV)

    def columns(k, width):
        return pl.ds(pl.multiple_of(k * width, width), width)

    own_cols = columns(own_k, C)
    loads = []
    for i, (src, dst) in enumerate(
        (
            (len_hbm, len_ref),
            (id_hbm, id_ref),
            (hidden_hbm, hidden_v),
            (qd_hbm, qd_v),
            (cos_hbm, cos_ref),
            (sin_hbm, sin_ref),
            (prompt_hbm, prompt_v),
            (suffix_hbm, suffix_v),
            (fresh_hbm, fresh_v),
            (base_hbm, base_in.at[seq]),
            (qu_hbm.at[0], qu_v.at[ada]),
            (od_hbm.at[0, :, own_cols], od_v.at[ada]),
            (ou_hbm.at[0], ou_v.at[ada]),
        )
    ):
        load = pltpu.make_async_copy(src, dst, local_sem.at[i])
        load.start()
        loads.append(load)
    l_len, l_id, l_hid, l_qd, l_cos, l_sin = loads[:6]
    l_prompt, l_suffix, l_fresh, l_base, l_qu, l_od, l_ou = loads[6:]
    l_len.wait()
    l_id.wait()

    token = lax.broadcasted_iota(jnp.int32, (1, LANES), 1)
    code = jnp.zeros((1, LANES), jnp.int32)
    for r in range(R):
        code = jnp.where(lax.rem(token, R) == r, id_ref[0, r] * 2**shift + len_ref[r], code)
    info[seq] = (code + lax.div(token, R)).astype(f32)

    pl.semaphore_wait(barrier, len(others))

    sends = []

    def send(src, dst, s_sem, r_sem, device):
        copy = pltpu.make_async_remote_copy(
            src_ref=src,
            dst_ref=dst,
            send_sem=s_sem,
            recv_sem=r_sem,
            device_id=device,
            device_id_type=MESH,
        )
        copy.start()
        sends.append(copy)
        return copy

    hid = {}
    for d in range(1, NA):
        hid[d] = send(
            hidden_hbm, hid_in.at[d - 1], hid_s.at[d - 1], hid_r.at[d - 1], place(0, d, 0)
        )
    infos, bases, qus, ods, ous = {}, {}, {}, {}, {}
    for ds in far:
        infos[ds] = send(
            info.at[seq], info.at[seq], info_s.at[ds - 1], info_r.at[ds - 1], place(ds, 0, 0)
        )

    def base_cols(where, b):
        pair = xor(lax.div(lax.rem(where, KV), 2), KV // 2 - 1 - b, KV // 2)
        return columns(pair, 2 * C)

    def send_base(b):
        for u in range(NS - 1, 0, -1):
            to = xor(seq, u, NS)
            cols = base_cols(to, b)
            bases[(u, b)] = send(
                base_hbm.at[:, :, cols], base_in.at[seq, :, :, cols],
                base_s.at[u - 1, b], base_r.at[u - 1, b], {"seq": to},
            )

    def send_qu(i):
        cols = columns(head_at(seq, i), C)
        for d in range(1, NA):
            qus[(d, i)] = send(
                qu_hbm.at[0, :, cols], qu_v.at[ada, :, cols],
                qu_s.at[d - 1, i], qu_r.at[d - 1, i], place(0, d, 0),
            )

    parity = lax.rem(seq, 2)
    neighbour = {"seq": xor(seq, 1, NS)}
    quarter = ou_hbm.shape[2] // 4

    def ou_cols(n, side):
        if n < OU_RELAYED:
            return columns(side, quarter)
        return pl.ds(2 * quarter, 2 * quarter)

    def source_slot(d):
        return lax.rem(ada + NA - d, NA)

    relays = {}

    def relay_qu(i):
        cols = columns(head_at(seq, i), C)
        for d in range(1, NA):
            qus[(d, i)].wait_recv()
            part = qu_v.at[source_slot(d), :, cols]
            qus[(d, i + 1)] = send(
                part, part, qu_s.at[d - 1, i + 1], qu_r.at[d - 1, i + 1], neighbour
            )

    def relay_ou(n):
        cols = ou_cols(n, parity)
        for d in range(1, NA):
            ous[(d, n)].wait_recv()
            part = ou_v.at[source_slot(d), :, cols]
            at = OU_RELAYED + OU_DIRECT + n
            relays[("ou", d, n)] = send(
                part, part, ou_s.at[d - 1, at], ou_r.at[d - 1, at], neighbour
            )

    turns = list(range(KV))
    half = KV // 2
    send_base(0)
    send_qu(0)

    packed = rank_in.shape[3]

    def rank_of(ref):
        for t in range(T):
            tok_f32[t * R : (t + 1) * R, :] = ref[t].astype(f32)
        part = dot_nt(tok_f32[...].astype(bf16), qd_v[0])
        return jnp.concatenate([part[p * packed : (p + 1) * packed] for p in range(LANES // K)], 1)

    ranks = {}

    def send_rank(src, ds, da, dh):
        ranks[(ds, da, dh)] = send(
            src, rank_in.at[seq, ada, head],
            rank_s.at[ds, da, dh], rank_r.at[ds, da, dh], place(ds, da, dh),
        )

    l_hid.wait()
    l_qd.wait()
    rank_in[seq, ada, head] = rank_of(hidden_v)
    for ds in far + [0]:
        for dh in range(NH):
            if (ds, dh) != (0, 0):
                send_rank(rank_in.at[seq, ada, head], ds, 0, dh)

    l_prompt.wait()
    l_suffix.wait()
    l_fresh.wait()
    n_suf = R * S
    n_new = fresh_f32.shape[0]
    n_loc = n_suf + n_new
    for i in range(2):
        fresh_f32[...] = jnp.zeros_like(fresh_f32)
        for t in range(T):
            fresh_f32[t * R : (t + 1) * R, :] = fresh_v[i, t].astype(f32)
        fresh_pad[i] = fresh_f32[...].astype(bf16)

    def prepare(i):
        cols = columns(head_at(seq, i), D)
        vt[i, 0:D, :] = prompt_v[1, :, cols].astype(f32).T.astype(bf16)
        pad = lax.broadcasted_iota(jnp.int32, (vt.shape[1] - D, vt.shape[2]), 0)
        vt[i, D:, :] = jnp.where(pad == 0, 1.0, 0.0).astype(bf16)
        local = jnp.concatenate(
            [
                suffix_v[1, :, :, cols].reshape(n_suf, D),
                fresh_pad[1, :, cols],
                jnp.zeros((vlt.shape[2] - n_loc, D), bf16),
            ],
            0,
        )
        vlt[i, 0:D, :] = local.astype(f32).T.astype(bf16)
        pad = lax.broadcasted_iota(jnp.int32, (vlt.shape[1] - D, vlt.shape[2]), 0)
        vlt[i, D:, :] = jnp.where(pad == 0, 1.0, 0.0).astype(bf16)

    for i in turns[:half]:
        prepare(i)

    for d in range(1, NA):
        hid[d].wait_recv()
        rank_out[d - 1] = rank_of(hid_in.at[d - 1])
        for ds in far + [0]:
            for dh in range(NH):
                send_rank(rank_out.at[d - 1], ds, d, dh)
    def send_ou(n):
        cols = ou_cols(n, parity)
        for d in range(1, NA):
            ous[(d, n)] = send(
                ou_hbm.at[0, :, cols], ou_v.at[ada, :, cols],
                ou_s.at[d - 1, n], ou_r.at[d - 1, n], place(0, d, 0),
            )

    for i in range(2, KV, 2):
        send_qu(i)
    for b in range(1, half):
        send_base(b)
    for n in range(OU_RELAYED):
        send_ou(n)
    for i in range(3, KV, 2):
        send_qu(i)
    for d in range(1, NA):
        ods[d] = send(
            od_hbm.at[0, :, own_cols], od_v.at[ada], od_s.at[d - 1], od_r.at[d - 1],
            place(0, d, 0),
        )

    key = lax.broadcasted_iota(jnp.int32, (n_loc, QC), 0)
    query = lax.rem(lax.broadcasted_iota(jnp.int32, (n_loc, QC), 1), GT)
    q_home, q_token = lax.div(query, N), lax.rem(query, N)
    q_step, q_row = lax.div(q_token, R), lax.rem(q_token, R)
    limit = jnp.zeros((n_loc, QC), jnp.int32)
    for r in range(R):
        limit = jnp.where(q_row == r, len_ref[r], limit)
    new = key - n_suf
    in_suffix = (lax.div(key, S) == q_row) & (lax.rem(key, S) < limit) & (new < 0)
    in_fresh = (lax.rem(new, R) == q_row) & (lax.div(new, R) <= q_step) & (new >= 0)
    bias_v[...] = jnp.where((q_home == own_k) & (in_suffix | in_fresh), 0.0, -1e30)

    for i in turns[half:]:
        prepare(i)

    landed = set()

    def convert(i):
        cols = columns(head_at(seq, i), C)
        for u in range(1, NS):
            if (u, i // 2) not in landed:
                bases[(u, i // 2)].wait_recv()
                landed.add((u, i // 2))
        for s in range(NS):
            for t in range(T):
                at = s * N + t * R
                base_f[i, at : at + R, :] = base_in[s, t, :, cols].astype(f32)

    l_base.wait()
    l_qu.wait()
    l_cos.wait()
    l_sin.wait()
    for ds in far:
        infos[ds].wait_recv()
    row = lax.broadcasted_iota(jnp.int32, (N, LANES), 0)
    diagonal = row == lax.broadcasted_iota(jnp.int32, (N, LANES), 1)
    for s in range(NS):
        code = jnp.sum(jnp.where(diagonal, info[s], 0.0), 1, keepdims=True)
        ids_v[s * N : (s + 1) * N, :] = jnp.broadcast_to(code.astype(jnp.int32), (N, LANES))
    codes = ids_v[...]
    position = jnp.bitwise_and(codes, 2**shift - 1)
    cos, sin = jnp.zeros(codes.shape, f32), jnp.zeros(codes.shape, f32)
    for p in range(S + T):
        cos = jnp.where(position == p, cos_ref[p : p + 1, :], cos)
        sin = jnp.where(position == p, sin_ref[p : p + 1, :], sin)
    cos_v[...] = cos
    sin_v[...] = sin
    ids_v[...] = jnp.right_shift(codes, shift)
    relay_qu(0)
    convert(0)

    def spread(x):
        return jnp.concatenate([x] * (NK // LANES), 1)

    def adapter_lanes(shape):
        return lax.div(lax.broadcasted_iota(jnp.int32, shape, 1), K)

    for copy in ranks.values():
        copy.wait_recv()
    for s in range(NS):
        ids = ids_v[s * N : (s + 1) * N, :]
        chosen = jnp.zeros((N, LANES), f32)
        for e in range(NA):
            whole = functools.reduce(jnp.add, [rank_in[s, e, h] for h in range(NH)])
            rows = [whole[:, p * K : (p + 1) * K] for p in range(LANES // K)]
            whole = jnp.concatenate([jnp.concatenate(rows, 0)] * (LANES // K), 1)[0:N]
            chosen = jnp.where(ids == e, whole, chosen)
        wide_f[s * N : (s + 1) * N, :] = spread(chosen)
    wide = wide_f[...]
    wide_b[...] = jnp.where(adapter_lanes(wide.shape) == spread(ids_v[...]), wide, 0.0).astype(bf16)

    def attend(u):
        i = KV - 1 - u % KV
        target = xor(seq, u, NS)
        k, j = lax.rem(target, KV), lax.div(target, KV)
        rows = pl.ds(pl.multiple_of(j * GT, GT), GT)
        cols = columns(k, D)
        delta = dot_nn(wide_b[rows, :], qu_v[:, :, columns(k, C)].reshape(NK, C))
        merged = base_f[i, rows, :] + delta
        cos, sin = cos_v[rows, :], sin_v[rows, :]
        turned = []
        for g in range(G):
            x = merged[:, g * D : (g + 1) * D]
            turned.append((x * cos + pltpu.roll(x, D // 2, 1) * sin).astype(bf16))
        query = jnp.concatenate(turned, 0)
        local_keys = jnp.concatenate(
            [suffix_v[0, :, :, cols].reshape(n_suf, D), fresh_pad[0, :, cols]], 0
        )
        far_scores = dot_nt(prompt_v[0, :, cols], query)
        shut = jnp.where(j == own_j, 0.0, -1e30)
        near_scores = dot_nt(local_keys, query) + (bias_v[...] + shut)
        peak = jnp.maximum(
            jnp.max(far_scores, 0, keepdims=True), jnp.max(near_scores, 0, keepdims=True)
        )
        far_weight = jnp.exp2((far_scores - peak) * scale).astype(bf16)
        near_weight = jnp.exp2((near_scores - peak) * scale).astype(bf16)
        near_weight = jnp.concatenate(
            [near_weight, jnp.zeros((vlt.shape[2] - n_loc, QC), bf16)], 0
        )
        both = dot_nn(vt[i], far_weight) + dot_nn(vlt[i], near_weight)
        return both[0:D], peak, both[D : D + 1]

    A = LANES * FOLD_TILES
    fold, rest = slice(0, A), slice(A, QC)
    parts, stats, folds, pres = {}, {}, {}, {}

    def merge(pieces):
        whole = pieces[0]
        for o, m, t in pieces[1:]:
            top = jnp.maximum(whole[1], m)
            one, two = jnp.exp2((whole[1] - top) * scale), jnp.exp2((m - top) * scale)
            whole = (whole[0] * one + o * two, top, whole[2] * one + t * two)
        return whole

    def remote(src, dst, s_sem, r_sem, device):
        return pltpu.make_async_remote_copy(
            src_ref=src, dst_ref=dst, send_sem=s_sem, recv_sem=r_sem,
            device_id=device, device_id_type=MESH,
        )

    def nearer(u):
        return (xor(seq, u, NS) > seq).astype(jnp.int32) == parity

    def begin(copies):
        for copy in copies:
            copy.start()

    def fold_in(u):
        for copy in pres[u ^ 1]:
            copy.wait_recv()
        num, top, den = merge(
            [
                (fold_own[u - 2], stat_out[u - 1, 0:1, fold], stat_out[u - 1, 1:2, fold]),
                (pre_in[u - 2].astype(f32), pre_stat[u - 2, 0:1, :], pre_stat[u - 2, 1:2, :]),
            ]
        )
        fold_out[u - 2] = num.astype(bf16)
        fold_stat[u - 2, 0:1, :] = top
        fold_stat[u - 2, 1:2, :] = den
        begin(folds[u])

    def folding():
        for u in range(NS - 1, 1, -1):
            pl.when(nearer(u ^ 1))(functools.partial(fold_in, u ^ 1))

    units = [(j - 1) * KV + KV - 1 - i for j in range(NS // KV, 0, -1) for i in turns]
    for at, u in enumerate(units):
        i = KV - 1 - u % KV
        if at < KV:
            if i % 2:
                for d in range(1, NA):
                    qus[(d, i)].wait_recv()
            elif i > 0:
                for d in range(1, NA):
                    qus[(d, i)].wait_recv()
            if i > 0:
                convert(i)
        if at == 2:
            for n in range(OU_RELAYED, OU_RELAYED + OU_DIRECT):
                send_ou(n)
        if u == FOLD_BEFORE:
            folding()
            for n in range(OU_RELAYED):
                relay_ou(n)
        o, m, t = attend(u)
        if u > 0:
            part_out[u - 1] = o.astype(bf16)
            stat_out[u - 1, 0:1, :] = m
            stat_out[u - 1, 1:2, :] = t
            home = {"seq": xor(seq, u, NS)}
            if u > 1:
                fold_own[u - 2] = o[:, fold]
                slot, pair = (u ^ 1) - 2, u // 2 - 1
                pres[u] = (
                    remote(
                        part_out.at[u - 1, :, fold], pre_in.at[slot],
                        pre_s.at[slot, 0], pre_r.at[slot, 0], neighbour,
                    ),
                    remote(
                        stat_out.at[u - 1, :, fold], pre_stat.at[slot],
                        pre_s.at[slot, 1], pre_r.at[slot, 1], neighbour,
                    ),
                )
                folds[u] = (
                    remote(
                        fold_out.at[u - 2], fold_in_o.at[pair],
                        fold_s.at[pair, 0], fold_r.at[pair, 0], home,
                    ),
                    remote(
                        fold_stat.at[u - 2], fold_in_s.at[pair],
                        fold_s.at[pair, 1], fold_r.at[pair, 1], home,
                    ),
                )
                pl.when(jnp.logical_not(nearer(u)))(functools.partial(begin, pres[u]))
            cols = rest if u > 1 else slice(0, QC)
            parts[u] = send(
                part_out.at[u - 1, :, cols], part_in.at[u - 1, :, cols],
                part_s.at[u - 1], part_r.at[u - 1], home,
            )
            stats[u] = send(
                stat_out.at[u - 1, :, cols], stat_in.at[u - 1, :, cols],
                stat_s.at[u - 1], stat_r.at[u - 1], home,
            )
    l_od.wait()
    for d in range(1, NA):
        ods[d].wait_recv()
    for g in range(G):
        lanes = slice(g * D, (g + 1) * D)
        od_t[lanes, :] = od_v[:, :, lanes].reshape(NK, D).astype(f32).T.astype(bf16)
    near, beyond = [(o[:, fold], m[:, fold], t[:, fold])], [(o[:, rest], m[:, rest], t[:, rest])]

    def piece(values, at, where, cols):
        return values[where, :, cols].astype(f32), at[where, 0:1, cols], at[where, 1:2, cols]

    for u in [u for u in units if u > 0]:
        parts[u].wait_recv()
        stats[u].wait_recv()
        beyond.append(piece(part_in, stat_in, u - 1, rest))
        if u == 1:
            near.append(piece(part_in, stat_in, 0, fold))
    for u in range(2, NS, 2):
        for copy in folds[u]:
            copy.wait_recv()
        near.append(piece(fold_in_o, fold_in_s, u // 2 - 1, slice(0, A)))
    near, beyond = merge(near), merge(beyond)
    turned = jnp.concatenate([w[0] * (1.0 / w[2]) for w in (near, beyond)], 1).T
    result = jnp.concatenate([turned[g * GT : (g + 1) * GT] for g in range(G)], 1)

    down = dot_nn(result.astype(bf16), od_t[...])
    group_rows = pl.ds(pl.multiple_of(own_j * GT, GT), GT)
    down = jnp.where(adapter_lanes(down.shape) == spread(ids_v[group_rows, :]), down, 0.0)
    for jj in range(KV):
        ork_out[jj] = down[jj * N : (jj + 1) * N]
    orks, atts = {}, {}

    def home_of(e):
        jj = xor(own_k, e, KV)
        return jj, own_j * KV + jj

    for e in range(KV - 1, -1, -1):
        jj, where = home_of(e)
        for dh in range(NH):
            if (e, dh) != (0, 0):
                orks[(e, dh)] = send(
                    ork_out.at[jj], ork_in.at[own_k, head],
                    ork_s.at[e, dh], ork_r.at[e, dh],
                    {"seq": where, "head": turn(head, dh, NH)},
                )
    for jj in range(KV):
        for t in range(T):
            at = jj * N + t * R
            att_out[jj, t] = result[at : at + R].astype(bf16)
    for e in range(KV - 1, 0, -1):
        jj, where = home_of(e)
        atts[e] = send(
            att_out.at[jj], att_ref.at[:, :, own_cols], att_s.at[e - 1], att_r.at[e - 1],
            {"seq": where},
        )
    att_ref[:, :, own_cols] = att_out[own_k]

    ork_in[own_k, head] = ork_out[own_k]
    for copy in orks.values():
        copy.wait_recv()
    total = functools.reduce(
        jnp.add, [ork_in[k, h] for k in range(KV) for h in range(NH)]
    ).astype(bf16)
    l_ou.wait()

    def raise_up(cols):
        up = dot_nn(total, ou_v[:, :, cols].reshape(NK, cols.size))
        for t in range(T):
            ada_ref[t, :, cols] = up[t * R : (t + 1) * R].astype(bf16)

    for n in range(OU_RELAYED + OU_DIRECT):
        if n >= OU_RELAYED:
            for d in range(1, NA):
                ous[(d, n)].wait_recv()
        raise_up(ou_cols(n, parity))
    for n in range(OU_RELAYED):
        for d in range(1, NA):
            relays[("ou", d, n)].wait_recv()
        raise_up(ou_cols(n, 1 - parity))
    for copy in atts.values():
        copy.wait_recv()

    for copy in sends:
        copy.wait_send()

    def drain(copies):
        for copy in copies:
            copy.wait_send()

    for u in range(NS - 1, 1, -1):
        pl.when(jnp.logical_not(nearer(u)))(functools.partial(drain, pres[u]))
        pl.when(nearer(u))(functools.partial(drain, folds[u]))


def finish(first, second, att_hbm, ada_hbm, sem):
    copies = [
        pltpu.make_async_copy(first, att_hbm, sem.at[0]),
        pltpu.make_async_copy(second, ada_hbm, sem.at[1]),
    ]
    for copy in copies:
        copy.start()
    for copy in copies:
        copy.wait()


def on_device(
    hidden,
    base_query_rows,
    fresh_key_value,
    suffix_key_value,
    suffix_length,
    row_adapter_index,
    prompt_key_value,
    query_down_factors,
    query_up_factors,
    output_down_factors,
    output_up_factors,
):
    NS, NA, NH = lax.axis_size("seq"), lax.axis_size("adapter"), lax.axis_size("head")
    hidden, base_query_rows = (x.transpose(1, 0, 2) for x in (hidden, base_query_rows))
    fresh_key_value = fresh_key_value.transpose(0, 2, 1, 3)
    T, R, width = hidden.shape
    D = HEAD_SIZE
    KV = prompt_key_value.shape[2] // D
    G = width // D // KV
    S = suffix_key_value.shape[2]
    keys = prompt_key_value.shape[1]
    N, C = R * T, G * D
    K = query_down_factors.shape[1]
    GT = KV * N
    QC, NK = G * GT, NA * K
    assert query_down_factors.shape[0] == 1
    assert width % (LANES * 4) == 0 and KV >= 2
    assert NS % KV == 0 and NS & (NS - 1) == 0 and KV & (KV - 1) == 0
    assert GT % 16 == 0 and LANES % K == 0 and NK % LANES == 0
    prompt_total = keys * NS
    positions = prompt_total + np.arange(S + T, dtype=np.float64)
    frequency = ROPE_BASE ** (-2.0 * np.arange(D // 2, dtype=np.float64) / D)
    angle = positions[:, None] * frequency[None, :]
    cos = np.concatenate([np.cos(angle), np.cos(angle)], 1).astype(np.float32)
    sin = np.concatenate([-np.sin(angle), np.sin(angle)], 1).astype(np.float32)
    bf16, f32 = jnp.bfloat16, jnp.float32
    dma = pltpu.SemaphoreType.DMA
    one = max(NA - 1, 1)
    far, outer = NS - 1, NS - 2
    A = LANES * FOLD_TILES
    assert A < QC and NS >= 4
    packed = N // (LANES // K)
    assert N % (LANES // K) == 0
    n_new = -(-N // 16) * 16
    n_loc = R * S + n_new
    n_loc_pad = -(-n_loc // LANES) * LANES

    def like(x):
        return pltpu.VMEM(x.shape, x.dtype)

    scratch = [
        pltpu.SMEM((R,), jnp.int32),
        pltpu.SMEM((1, R), jnp.int32),
        pltpu.VMEM(cos.shape, f32),
        pltpu.VMEM(sin.shape, f32),
        like(hidden),
        like(fresh_key_value),
        like(suffix_key_value),
        like(prompt_key_value),
        like(query_down_factors),
        pltpu.VMEM((NA, K, width), bf16),
        pltpu.VMEM((NA, K, C), bf16),
        pltpu.VMEM((NA, K, width), bf16),
        pltpu.VMEM((C, NK), bf16),
        dma((13,)),
        pltpu.VMEM((one,) + hidden.shape, bf16),
        pltpu.VMEM((NS,) + hidden.shape, bf16),
        pltpu.VMEM((NS, 1, LANES), f32),
        pltpu.VMEM((NS, NA, NH, packed, LANES), f32),
        pltpu.VMEM((one, packed, LANES), f32),
        pltpu.VMEM((packed * (LANES // K), width), f32),
        pltpu.VMEM((n_new, KV * D), f32),
        pltpu.VMEM((2, n_new, KV * D), bf16),
        pltpu.VMEM((KV, NS * N, C), f32),
        pltpu.VMEM((NS * N, D), f32),
        pltpu.VMEM((NS * N, D), f32),
        pltpu.VMEM((NS * N, LANES), jnp.int32),
        pltpu.VMEM((NS * N, NK), f32),
        pltpu.VMEM((NS * N, NK), bf16),
        pltpu.VMEM((KV, D + 16, keys), bf16),
        pltpu.VMEM((KV, D + 16, n_loc_pad), bf16),
        pltpu.VMEM((n_loc, QC), f32),
        pltpu.VMEM((far, D, QC), bf16),
        pltpu.VMEM((far, D, QC), bf16),
        pltpu.VMEM((far, 2, QC), f32),
        pltpu.VMEM((far, 2, QC), f32),
        pltpu.VMEM((outer, D, A), f32),
        pltpu.VMEM((outer, D, A), bf16),
        pltpu.VMEM((outer, 2, A), f32),
        pltpu.VMEM((outer, D, A), bf16),
        pltpu.VMEM((outer, 2, A), f32),
        pltpu.VMEM((outer // 2, D, A), bf16),
        pltpu.VMEM((outer // 2, 2, A), f32),
        pltpu.VMEM((KV, N, NK), f32),
        pltpu.VMEM((KV, NH, N, NK), f32),
        pltpu.VMEM((KV, T, R, C), bf16),
        dma((one,)), dma((one,)),
        dma((far,)), dma((far,)),
        dma((far, KV // 2)), dma((far, KV // 2)),
        dma((one, KV)), dma((one, KV)),
        dma((one,)), dma((one,)),
        dma((one, 2 * OU_RELAYED + OU_DIRECT)), dma((one, 2 * OU_RELAYED + OU_DIRECT)),
        dma((NS, NA, NH)), dma((NS, NA, NH)),
        dma((far,)), dma((far,)),
        dma((far,)), dma((far,)),
        dma((outer, 2)), dma((outer, 2)),
        dma((outer // 2, 2)), dma((outer // 2, 2)),
        dma((KV, NH)), dma((KV, NH)),
        dma((max(KV - 1, 1),)), dma((max(KV - 1, 1),)),
    ]
    vmem = pl.BlockSpec(memory_space=pltpu.VMEM)
    anywhere = pl.BlockSpec(memory_space=pl.ANY)
    results = pl.pallas_call(
        functools.partial(body, (NS, NA, NH, R, T, KV, G, S, K)),
        out_shape=(like(hidden), like(hidden)),
        in_specs=[anywhere] * 13,
        out_specs=(vmem, vmem),
        scratch_shapes=scratch,
        compiler_params=pltpu.CompilerParams(
            collective_id=0, has_side_effects=True, vmem_limit_bytes=56 * 2**20
        ),
        name="decode",
    )(
        suffix_length,
        row_adapter_index.transpose(1, 0),
        jnp.asarray(cos),
        jnp.asarray(sin),
        hidden,
        base_query_rows,
        fresh_key_value,
        suffix_key_value,
        prompt_key_value,
        query_down_factors,
        query_up_factors,
        output_down_factors,
        output_up_factors,
    )
    results = pl.pallas_call(
        finish,
        out_shape=tuple(jax.ShapeDtypeStruct(x.shape, bf16) for x in results),
        in_specs=[vmem, vmem],
        out_specs=(anywhere, anywhere),
        scratch_shapes=[dma((2,))],
        name="finish",
    )(*(pltpu.with_memory_space_constraint(x, pltpu.VMEM) for x in results))
    return tuple(x.transpose(1, 0, 2) for x in results)


def solution(mesh):
    rows = P(("groups", "seq", "adapter"), None, "head")
    caches = P(None, ("groups", "seq", "adapter"), None, "head")
    factors = P(("groups", "adapter"), None, "head")
    placed = (
        rows,
        rows,
        caches,
        caches,
        P(("groups", "seq", "adapter")),
        P(("groups", "seq", "adapter"), None),
        P(None, ("groups", "seq"), "head"),
        factors,
        factors,
        factors,
        factors,
    )
    return jax.shard_map(
        on_device, mesh=mesh, in_specs=placed, out_specs=(rows, rows), check_vma=False
    )
```
